128 devices in a mesh: dp: 16 (over z, y), expert: 8 (over x, core).
Axes of the slice: x: 4, y: 4, z: 4, core: 2. Of those that a mesh axis runs over, the one named last changes fastest.
Arguments:
- tokens: bfloat16 [65536, 768], P(('dp', 'expert')), may hold values from -6 to 6
- assigned: int32 [65536, 1], P(('dp', 'expert')), may hold values from 0 to 7; in each aligned block of 512 rows (0 to 511, 512 to 1023, ...) at most 128 rows name the same one
- gate_prob: float32 [65536, 1], P(('dp', 'expert')), may hold values from 0.2 to 1
- cotangent: bfloat16 [65536, 768], P(('dp', 'expert')), may hold values from -6 to 6
- weight_in: bfloat16 [8, 768, 3072], P('expert'), may hold values from -0.21875 to 0.21875
- weight_out: bfloat16 [8, 3072, 768], P('expert'), may hold values from -0.109375 to 0.109375
- moment_in: float32 [8, 768, 3072], P('expert', 'dp'), may hold values from -60 to 60
- moment_out: float32 [8, 3072, 768], P('expert', 'dp'), may hold values from -60 to 60
- second_in: float32 [8, 768, 3072], P('expert', 'dp'), may hold values from 1 to 1000
- second_out: float32 [8, 3072, 768], P('expert', 'dp'), may hold values from 1 to 1000
Outputs:
- combined: bfloat16 [65536, 768], P(('dp', 'expert'))
- new_weight_in: float32 [8, 768, 3072], P('expert', 'dp')
- new_weight_out: float32 [8, 3072, 768], P('expert', 'dp')
- new_moment_in: float32 [8, 768, 3072], P('expert', 'dp')
- new_moment_out: float32 [8, 3072, 768], P('expert', 'dp')
- new_second_in: float32 [8, 768, 3072], P('expert', 'dp')
- new_second_out: float32 [8, 3072, 768], P('expert', 'dp')
The draws below stay inside these ranges and needn't reach their ends.
Inputs may be any that keep to these rules, and one draw needn't show every extreme that they name: `assigned`: within each device's 512 rows (aligned blocks), no expert is named more than 128 times, a bound that some block reaches; every expert is named somewhere.
All inputs are finite; a program needn't handle non-finite values.
Results may differ from the reference program's by a relative error of at most 0.0012.
The reference program's roundings to bfloat16 on the way (of `scaled`, `hidden`, `expert_out` and `hidden_grad`) count: a program that leaves them out, or rounds other values in their place, can miss the bound.
Values may be sent and summed in bfloat16 or wider, within the bound.
A program may use at most 192 MiB of HBM per device.

```python
import math
import jax
import jax.numpy as jnp
import numpy as np
from jax import lax

D = 768
FF = 3072
TOK_DEV = 512
EXPERTS = 8
CAP = 128
TOKENS = 65536
LEVELS = 4
N_DP = 16
N_EXPERT = 8


def replica_owner():
    return jnp.arange(TOKENS, dtype=jnp.int32) // (TOKENS // N_DP)


def row_noise(key):
    return jnp.clip(jax.random.normal(key, (TOKENS, D), jnp.float32), -5.0, 5.0)


def draw_tokens(key, part):
    keys = jax.random.split(jax.random.fold_in(key, 11), 3)
    feature_pos = jnp.arange(D, dtype=jnp.float32) / D
    envelope = 0.2 + 2.8 * feature_pos * feature_pos
    common = envelope * jnp.clip(jax.random.normal(keys[0], (D,), jnp.float32), -2.0, 2.0)
    strength = jax.random.uniform(keys[1], (N_DP,), jnp.float32, 0.3, 1.2)
    owner = replica_owner()
    values = strength[owner][:, None] * common[None, :] + row_noise(keys[2])
    return jnp.clip(values, -6.0, 6.0).astype(jnp.bfloat16)


def draw_cotangent(key, part):
    keys = jax.random.split(jax.random.fold_in(key, 23), 3)
    common = jnp.clip(jax.random.normal(keys[0], (D,), jnp.float32), -3.0, 3.0)
    low_end = -3.912023
    high_end = -0.9162907
    strength = jnp.exp(jax.random.uniform(keys[1], (N_DP,), jnp.float32, low_end, high_end))
    owner = replica_owner()
    values = strength[owner][:, None] * common[None, :] + row_noise(keys[2])
    return jnp.clip(values, -6.0, 6.0).astype(jnp.bfloat16)


def shard_levels(stream_key, shape, cuts, low, top_value):
    factor_of, own = 1.0, jax.random.fold_in(stream_key, 6)
    for axis_at, parts in cuts:
        heights = jnp.exp(jax.random.uniform(jax.random.fold_in(own, axis_at), (parts,), jnp.float32, low / len(cuts), top_value / len(cuts)))
        factor_of = factor_of * jnp.repeat(heights, shape[axis_at] // parts).reshape([-1 if axis == axis_at else 1 for axis in range(len(shape))])
    return factor_of


def assign_block(own_key, own, number, rows, number_of, top, bound, slope):
    ranking = jax.random.permutation(own_key, number_of)
    crowded, usual = shares(number_of, rows * top, bound, slope, True), shares(number_of, rows * top, bound, slope, False)
    places = jnp.arange(number_of)

    def named(sizes, turn):
        used = int((sizes > 0).sum())
        fixed = max(1, used // 4)
        shifted = fixed + (places - fixed + turn * (used - fixed)) % max(1, number_of - fixed)
        return jnp.zeros((number_of,), jnp.int32).at[ranking[jnp.where(places < fixed, places, shifted)]].set(jnp.asarray(sizes, jnp.int32))

    sizes = jnp.where(number % 4 == 0, named(crowded, number // 4), named(usual, number - number // 4 - 1))
    mixed = jax.random.permutation(jax.random.fold_in(own, 3), number_of)
    source_of, sink = mixed[0:number_of // 2 * 2:2], mixed[1:number_of // 2 * 2:2]
    room = jnp.minimum(sizes[source_of] - 1, bound - sizes[sink]) // 2
    room = jnp.where((source_of == ranking[0]) | (sink == ranking[0]) | (sizes[sink] == 0), 0, jnp.maximum(room, 0))
    shifted = jax.random.randint(jax.random.fold_in(own, 4), (number_of // 2,), 0, 1 << 20) % (room + 1)
    sizes = sizes.at[source_of].add(-shifted).at[sink].add(shifted)
    items = jnp.searchsorted(jnp.cumsum(sizes), jnp.arange(rows * top), side="right").astype(jnp.int32)
    table = items.reshape(top, rows).T
    table = table[jax.random.permutation(jax.random.fold_in(own, 1), rows)]
    turn = jax.random.randint(jax.random.fold_in(own, 2), (rows, 1), 0, top)
    return jnp.take_along_axis(table, (jnp.arange(top)[None, :] + turn) % top, axis=1)


def shares(count, total, most, lean, full):
    loads = [(1 << 20) // math.isqrt(grade ** lean) + 1 for grade in range(1, count + 1)]
    largest = most if full else min(most, max(-(-total // count), total * loads[0] // sum(loads)))
    least = 1 if total - largest >= count - 1 else 0
    given, rest = [largest] + [least] * (count - 1), total - largest - least * (count - 1)
    while rest > 0:
        movable = [i for i in range(1, count) if given[i] < largest] or [i for i in range(1, count) if given[i] < most]
        mass, budget = sum([loads[i] for i in movable]), rest
        for i in movable:
            more = min(most - given[i], max(1, budget * loads[i] // mass), rest)
            given[i] = given[i] + more
            rest = rest - more
    return np.array(given)


def gaussian(own_key, shape, width, reach, cuts=(), kind=jnp.bfloat16):
    values = jax.random.normal(own_key, shape, jnp.float32) * width
    if len(cuts) > 0:
        values = shard_levels(own_key, shape, cuts, -0.22, 0.18) * values
    return jnp.clip(values, min=-reach, max=reach).astype(kind)


def setup_inputs(seed: int = 0) -> dict:
    splits = jax.random.split(jax.random.key(seed), 11)
    tokens = draw_tokens(jax.random.fold_in(splits[10], 71), 0)
    assigned_keys = jax.random.split(jax.random.fold_in(splits[1], 1), TOKENS // TOK_DEV)
    assigned_turns = jax.random.permutation(jax.random.fold_in(splits[1], 3), TOKENS // TOK_DEV)
    assigned = jax.vmap(lambda own, number: assign_block(jax.random.fold_in(splits[1], 2), own, number, TOK_DEV, EXPERTS, 1, CAP, 2))(assigned_keys, assigned_turns).reshape((TOKENS, 1))
    gate_prob = jnp.clip(0.2 + 0.8 * jax.random.uniform(splits[2], (TOKENS, 1), jnp.float32) ** shard_levels(splits[2], (TOKENS, 1), ((0, 128),), -0.2, 0.2), 0.2, 1.0)
    cotangent = draw_cotangent(jax.random.fold_in(splits[10], 71), 0)
    weight_in = gaussian(splits[4], (EXPERTS, D, FF), D ** -0.5, 0.21875, ((0, 8),))
    weight_out = gaussian(splits[5], (EXPERTS, FF, D), FF ** -0.5, 0.109375, ((0, 8),))
    moment_in = gaussian(splits[6], (EXPERTS, D, FF), 10.0, 60.0, ((0, 8), (1, 16)), jnp.float32)
    moment_out = gaussian(splits[7], (EXPERTS, FF, D), 10.0, 60.0, ((0, 8), (1, 16)), jnp.float32)
    second_in = jnp.clip(jnp.exp(math.log(1000.0) - 6.9077553 * jax.random.uniform(splits[8], (EXPERTS, D, FF), jnp.float32) ** shard_levels(splits[8], (EXPERTS, D, FF), ((0, 8), (1, 16)), -0.2, 0.2)), 1.0, 1000.0)
    second_out = jnp.clip(jnp.exp(math.log(1000.0) - 6.9077553 * jax.random.uniform(splits[9], (EXPERTS, FF, D), jnp.float32) ** shard_levels(splits[9], (EXPERTS, FF, D), ((0, 8), (1, 16)), -0.2, 0.2)), 1.0, 1000.0)
    return {"tokens": tokens, "assigned": assigned, "gate_prob": gate_prob, "cotangent": cotangent, "weight_in": weight_in, "weight_out": weight_out, "moment_in": moment_in, "moment_out": moment_out, "second_in": second_in, "second_out": second_out}


eps_adasum = 1e-06

def gelu_tanh(values):
    return jax.nn.gelu(values, approximate=True)

def adam_update(grad, weight, moment, second):
    new_moment = 0.9 * moment + 0.1 * grad
    new_second = 0.999 * second + 0.001 * grad * grad
    corr_one = 1.0 - 0.9 ** 10.0
    corr_two = 1.0 - 0.999 ** 10.0
    update = new_moment / corr_one / (jnp.sqrt(new_second / corr_two) + 1e-08)
    return (weight - 0.001 * update, new_moment, new_second)

def adasum(grad_in, grad_out):
    vectors = jnp.stack([grad_in.reshape(N_DP, -1), grad_out.reshape(N_DP, -1)], axis=1)
    count = N_DP
    for level in range(LEVELS):
        half_count = count // 2
        first = vectors[:half_count]
        second = vectors[half_count:count]
        cross = lax.optimization_barrier(jnp.sum(first * second, axis=(1, 2)))
        norm_first = lax.optimization_barrier(jnp.sum(first * first, axis=(1, 2)))
        norm_second = lax.optimization_barrier(jnp.sum(second * second, axis=(1, 2)))
        coef_first = 1.0 - cross / (2.0 * (norm_first + eps_adasum))
        coef_second = 1.0 - cross / (2.0 * (norm_second + eps_adasum))
        vectors = coef_first[:, None, None] * first + coef_second[:, None, None] * second
        count = half_count
    return vectors[0]

def reference(tokens, assigned, gate_prob, cotangent, weight_in, weight_out, moment_in, moment_out, second_in, second_out):
    f32 = jnp.float32
    bf16 = jnp.bfloat16
    blocks = N_DP * N_EXPERT
    expert_ids = assigned[:, 0].reshape(blocks, TOK_DEV)
    one_hot = (expert_ids[:, :, None] == jnp.arange(EXPERTS, dtype=jnp.int32)[None, None, :]).astype(jnp.int32)
    slot_index = lax.optimization_barrier(jnp.sum((jnp.cumsum(one_hot, axis=1) - one_hot) * one_hot, axis=2))
    slot_code = (expert_ids * CAP + slot_index).reshape(N_DP, N_EXPERT, TOK_DEV)
    scaled = (gate_prob * cotangent.astype(f32)).astype(bf16)
    token_blocks = tokens.reshape(N_DP, N_EXPERT, TOK_DEV, D)
    scaled_blocks = scaled.reshape(N_DP, N_EXPERT, TOK_DEV, D)
    buffer_rows = N_EXPERT * CAP

    def expert_step(expert):
        w_first = weight_in[expert]
        w_second = weight_out[expert]

        def replica(replica_index):
            codes = slot_code[replica_index]
            wanted = expert * CAP + jnp.arange(CAP, dtype=jnp.int32)
            table = (codes[:, None, :] == wanted[None, :, None]).astype(f32)
            dispatched = jnp.einsum('sct,std->scd', table, token_blocks[replica_index].astype(f32)).astype(bf16).reshape(buffer_rows, D)
            upstream = jnp.einsum('sct,std->scd', table, scaled_blocks[replica_index].astype(f32)).astype(bf16).reshape(buffer_rows, D)
            pre_act = jnp.dot(dispatched, w_first, preferred_element_type=f32)
            activated, gelu_back = jax.vjp(gelu_tanh, pre_act)
            hidden = activated.astype(bf16)
            expert_out = jnp.dot(hidden, w_second, preferred_element_type=f32).astype(bf16)
            grad_out = jnp.dot(hidden.T, upstream, preferred_element_type=f32)
            back_in = jnp.dot(upstream, w_second.T, preferred_element_type=f32)
            hidden_grad = gelu_back(back_in)[0].astype(bf16)
            grad_in = jnp.dot(dispatched.T, hidden_grad, preferred_element_type=f32)
            return (expert_out, grad_in, grad_out)
        outs_all, grads_in, grads_out = lax.map(replica, jnp.arange(N_DP, dtype=jnp.int32))
        total = adasum(grads_in, grads_out)
        new_w_first, new_m_first, new_v_first = adam_update(total[0].reshape(D, FF), w_first.astype(f32), moment_in[expert], second_in[expert])
        new_w_second, new_m_second, new_v_second = adam_update(total[1].reshape(FF, D), w_second.astype(f32), moment_out[expert], second_out[expert])
        return (outs_all, new_w_first, new_w_second, new_m_first, new_m_second, new_v_first, new_v_second)
    results = lax.map(expert_step, jnp.arange(EXPERTS, dtype=jnp.int32))
    outs_all = results[0]
    ids_three = expert_ids.reshape(N_DP, N_EXPERT, TOK_DEV)
    slots_three = slot_index.reshape(N_DP, N_EXPERT, TOK_DEV)
    replica_pos = jnp.arange(N_DP, dtype=jnp.int32)[:, None, None]
    source_pos = jnp.arange(N_EXPERT, dtype=jnp.int32)[None, :, None]
    picked = outs_all[ids_three, replica_pos, source_pos * CAP + slots_three]
    combined = (gate_prob.reshape(N_DP, N_EXPERT, TOK_DEV, 1) * picked.astype(f32)).astype(bf16).reshape(TOKENS, D)
    return (combined, results[1], results[2], results[3], results[4], results[5], results[6])
```

```python
import jax
import jax.numpy as jnp
from jax import lax
from jax.sharding import PartitionSpec as P

eps_adasum = 1e-06
SIDE = 4


def shift_z(x, step):
    side = SIDE
    return lax.ppermute(
        x,
        "dp",
        [(i, (i // side + step) % side * side + i % side) for i in range(side * side)],
    )


def gelu_tanh(values):
    return jax.nn.gelu(values, approximate=True)


def adam_update(grad, weight, moment, second):
    new_moment = 0.9 * moment + 0.1 * grad
    new_second = 0.999 * second + 0.001 * grad * grad
    corr_one = 1.0 - 0.9**10.0
    corr_two = 1.0 - 0.999**10.0
    update = new_moment / corr_one / (jnp.sqrt(new_second / corr_two) + 1e-08)
    return (weight - 0.001 * update, new_moment, new_second)


def contract_rows(left, right):
    return lax.dot_general(
        left, right, (((0,), (0,)), ((), ())), preferred_element_type=jnp.float32
    )


def pair_coefs(ab, aa, bb):
    return 1.0 - ab / (2.0 * (aa + eps_adasum)), 1.0 - ab / (2.0 * (bb + eps_adasum))


def tree_weights(gram):
    w0, w2 = pair_coefs(gram[0, 2], gram[0, 0], gram[2, 2])
    w1, w3 = pair_coefs(gram[1, 3], gram[1, 1], gram[3, 3])
    aa = w0 * w0 * gram[0, 0] + 2.0 * w0 * w2 * gram[0, 2] + w2 * w2 * gram[2, 2]
    bb = w1 * w1 * gram[1, 1] + 2.0 * w1 * w3 * gram[1, 3] + w3 * w3 * gram[3, 3]
    ab = w0 * (w1 * gram[0, 1] + w3 * gram[0, 3]) + w2 * (w1 * gram[2, 1] + w3 * gram[2, 3])
    u, v = pair_coefs(ab, aa, bb)
    return jnp.stack([u * w0, v * w1, u * w2, v * w3])


def local_gram(vectors):
    rows = []
    for i in range(4):
        rows.append([None] * 4)
    for i in range(4):
        for j in range(i, 4):
            s = sum(jnp.sum(a * b) for a, b in zip(vectors[i], vectors[j]))
            rows[i][j] = s
            rows[j][i] = s
    return jnp.stack([jnp.stack(r) for r in rows])


def expert_grads(rows, upstream, w_first, w_second):
    pre_act = jnp.dot(rows, w_first, preferred_element_type=jnp.float32)
    activated, gelu_back = jax.vjp(gelu_tanh, pre_act)
    hidden = activated.astype(jnp.bfloat16)
    back_in = lax.dot_general(
        upstream, w_second, (((1,), (1,)), ((), ())), preferred_element_type=jnp.float32
    )
    hidden_grad = gelu_back(back_in)[0].astype(jnp.bfloat16)
    return contract_rows(rows, hidden_grad), contract_rows(hidden, upstream)


def body(
    tokens,
    assigned,
    gate_prob,
    cotangent,
    weight_in,
    weight_out,
    moment_in,
    moment_out,
    second_in,
    second_out,
):
    f32 = jnp.float32
    bf16 = jnp.bfloat16
    side = SIDE
    experts = lax.axis_size("expert")
    replicas = lax.axis_size("dp")
    self_index = lax.axis_index("dp")
    z_index = self_index // side
    tok_rows = tokens.shape[0]
    width = tokens.shape[1]
    hidden_width = weight_in.shape[2]
    part = hidden_width // side
    capacity = 2 * tok_rows // experts
    buffer_rows = experts * capacity
    expert_ids = assigned[:, 0]
    one_hot = (expert_ids[:, None] == jnp.arange(experts, dtype=jnp.int32)[None, :]).astype(
        jnp.int32
    )
    slot_index = jnp.sum((jnp.cumsum(one_hot, axis=0) - one_hot) * one_hot, axis=1)
    slot_code = expert_ids * capacity + slot_index
    table = (jnp.arange(buffer_rows, dtype=jnp.int32)[:, None] == slot_code[None, :]).astype(bf16)
    scaled = (gate_prob * cotangent.astype(f32)).astype(bf16)

    def to_experts(x):
        sent = jnp.dot(table, x, preferred_element_type=f32).astype(bf16)
        got = lax.all_to_all(
            sent.reshape(experts, capacity, width), "expert", split_axis=0, concat_axis=0, tiled=True
        )
        return got.reshape(buffer_rows, width)

    rows_own = to_experts(tokens)
    up_own = to_experts(scaled)
    rows_lo = shift_z(rows_own, 1)
    rows_hi = shift_z(rows_own, -1)
    up_lo = shift_z(up_own, 1)
    up_hi = shift_z(up_own, -1)
    rows_far = shift_z(rows_lo, 1)
    up_far = shift_z(up_hi, -1)

    w_first = weight_in[0]
    w_second = weight_out[0]
    w_first_part = lax.dynamic_slice_in_dim(w_first, z_index * part, part, 1)
    w_second_part = lax.dynamic_slice_in_dim(w_second, z_index * part, part, 0)

    pre_act = jnp.dot(rows_own, w_first, preferred_element_type=f32)
    hidden = gelu_tanh(pre_act).astype(bf16)
    expert_out = (
        jnp.dot(hidden, w_second, preferred_element_type=f32)
        .astype(bf16)
        .reshape(experts, capacity, width)
    )
    returned = lax.all_to_all(expert_out, "expert", split_axis=0, concat_axis=0, tiled=True)
    picked = contract_rows(table, returned.reshape(buffer_rows, width))
    combined = (gate_prob * picked).astype(bf16)

    vectors = [
        expert_grads(rows, up, w_first_part, w_second_part)
        for rows, up in (
            (rows_own, up_own),
            (rows_hi, up_hi),
            (rows_far, up_far),
            (rows_lo, up_lo),
        )
    ]
    place = (jnp.arange(side)[:, None] == (jnp.arange(side)[None, :] + z_index) % side).astype(f32)
    near = local_gram(vectors)
    gram = jnp.sum(
        place[:, None, :, None] * place[None, :, None, :] * near[None, None], axis=(2, 3)
    )
    gram = gram + shift_z(gram, 2)
    gram = gram + shift_z(gram, 1)
    weights = tree_weights(gram)
    weights = jnp.sum(place * weights[:, None], axis=0)
    comb_in = sum(weights[k] * vectors[k][0] for k in range(side))
    comb_out = sum(weights[k] * vectors[k][1] for k in range(side))

    rows_first = width // replicas
    rows_second = hidden_width // replicas
    got_in = lax.all_to_all(
        comb_in.reshape(replicas, rows_first, part), "dp", split_axis=0, concat_axis=0, tiled=True
    ).reshape(side, side, rows_first, part)
    groups = [[z * side + y for y in range(side)] for z in range(side)]
    got_out = lax.all_to_all(
        comb_out.reshape(side, rows_second, width),
        "dp",
        split_axis=0,
        concat_axis=0,
        tiled=True,
        axis_index_groups=groups,
    )
    ys = [
        (jnp.concatenate([got_in[z, y] for z in range(side)], axis=1), got_out[y])
        for y in range(side)
    ]
    gram_y = local_gram(ys)
    for bit in range(4):
        gram_y = gram_y + lax.ppermute(gram_y, "dp", [(i, i ^ 1 << bit) for i in range(replicas)])
    weights_y = tree_weights(gram_y)
    seg_first = sum(weights_y[k] * ys[k][0] for k in range(side))
    seg_second = sum(weights_y[k] * ys[k][1] for k in range(side))

    own_first = lax.dynamic_slice_in_dim(w_first, self_index * rows_first, rows_first, 0).astype(
        f32
    )
    own_second = lax.dynamic_slice_in_dim(
        w_second, self_index * rows_second, rows_second, 0
    ).astype(f32)
    new_w_first, new_m_first, new_v_first = adam_update(
        seg_first, own_first, moment_in[0], second_in[0]
    )
    new_w_second, new_m_second, new_v_second = adam_update(
        seg_second, own_second, moment_out[0], second_out[0]
    )
    return (
        combined,
        new_w_first[None],
        new_w_second[None],
        new_m_first[None],
        new_m_second[None],
        new_v_first[None],
        new_v_second[None],
    )


def solution(mesh):
    return jax.shard_map(
        body,
        mesh=mesh,
        in_specs=(
            P(("dp", "expert"), None),
            P(("dp", "expert"), None),
            P(("dp", "expert"), None),
            P(("dp", "expert"), None),
            P("expert", None, None),
            P("expert", None, None),
            P("expert", "dp", None),
            P("expert", "dp", None),
            P("expert", "dp", None),
            P("expert", "dp", None),
        ),
        out_specs=(
            P(("dp", "expert"), None),
            P("expert", "dp", None),
            P("expert", "dp", None),
            P("expert", "dp", None),
            P("expert", "dp", None),
            P("expert", "dp", None),
            P("expert", "dp", None),
        ),
        check_vma=False,
    )
```

```python
import jax
import jax.numpy as jnp
from jax import lax
from jax.experimental import pallas as pl
from jax.experimental.pallas import tpu as pltpu
from jax.sharding import PartitionSpec as P

eps_adasum = 1e-06
SIDE = 4
LANES = 128
MESH = pl.DeviceIdType.MESH
PAIRS = [(a, b) for a in range(SIDE) for b in range(a, SIDE)]
SLOT = {pair: k for k, pair in enumerate(PAIRS)}


def adam_update(grad, weight, moment, second):
    new_moment = 0.9 * moment + 0.1 * grad
    new_second = 0.999 * second + 0.001 * grad * grad
    corr_one = 1.0 - 0.9**10.0
    corr_two = 1.0 - 0.999**10.0
    update = new_moment / corr_one / (jnp.sqrt(new_second / corr_two) + 1e-08)
    return (weight - 0.001 * update, new_moment, new_second)


def contract_rows(left, right):
    return lax.dot_general(
        left, right, (((0,), (0,)), ((), ())), preferred_element_type=jnp.float32
    )


def dot_nt(left, right):
    return lax.dot_general(
        left, right, (((1,), (1,)), ((), ())), preferred_element_type=jnp.float32
    )


def pair_coefs(ab, aa, bb):
    return 1.0 - ab / (2.0 * (aa + eps_adasum)), 1.0 - ab / (2.0 * (bb + eps_adasum))


def tree_weights(g):
    w0, w2 = pair_coefs(g(0, 2), g(0, 0), g(2, 2))
    w1, w3 = pair_coefs(g(1, 3), g(1, 1), g(3, 3))
    aa = w0 * w0 * g(0, 0) + 2.0 * w0 * w2 * g(0, 2) + w2 * w2 * g(2, 2)
    bb = w1 * w1 * g(1, 1) + 2.0 * w1 * w3 * g(1, 3) + w3 * w3 * g(3, 3)
    ab = w0 * (w1 * g(0, 1) + w3 * g(0, 3)) + w2 * (w1 * g(1, 2) + w3 * g(2, 3))
    u, v = pair_coefs(ab, aa, bb)
    return [u * w0, v * w1, u * w2, v * w3]


def gelu_parts(v):
    root = 0.7978845608028654
    square = v * v
    t = jnp.tanh(root * (v + 0.044715 * (square * v)))
    cdf = 0.5 * (1.0 + t)
    slope = cdf + v * (0.5 * (1.0 - t * t)) * (root * (1.0 + 0.134145 * square))
    return v * cdf, slope


def gelu_only(v):
    root = 0.7978845608028654
    return v * (0.5 * (1.0 + jnp.tanh(root * (v + 0.044715 * (v * v * v)))))


def gram_sums(refs, rows):
    width = refs[0].shape[2]

    def step(i, sums):
        sums = list(sums)
        at = pl.ds(pl.multiple_of(i * 8, 8), 8)
        for ref in refs:
            for c in range(width // LANES):
                cols = slice(c * LANES, (c + 1) * LANES)
                v = [ref[k, at, cols] for k in range(SIDE)]
                for p, (a, b) in enumerate(PAIRS):
                    sums[p] = sums[p] + v[a] * v[b]
        return tuple(sums)

    zero = jnp.zeros((8, LANES), jnp.float32)
    return lax.fori_loop(0, rows // 8, step, (zero,) * len(PAIRS))


def kernel(
    sent_t,
    sent_u,
    w1t,
    win_hbm,
    wout_hbm,
    ret,
    seg_in,
    seg_out,
    tok,
    ups,
    win,
    wout,
    g_in,
    g_out,
    ht,
    hgt,
    eout,
    acc,
    s_in,
    s_out,
    r_in,
    r_out,
    gz_out,
    gz_got,
    gy_out,
    gy_got,
    w_sem,
    loc_sem,
    d_send,
    d_recv,
    zf_send,
    zf_recv,
    far_send,
    far_recv,
    e_send,
    e_recv,
    gz_send,
    gz_recv,
    yo_send,
    yo_recv,
    yi_send,
    yi_recv,
    gy_send,
    gy_recv,
):
    f32 = jnp.float32
    bf16 = jnp.bfloat16
    dp = lax.axis_index("dp")
    me = lax.axis_index("expert")
    z, y = lax.div(dp, SIDE), lax.rem(dp, SIDE)
    x, core = lax.div(me, 2), lax.rem(me, 2)
    cap = sent_t.shape[1]
    chunk = 2 * cap
    part = w1t.shape[0]
    own_rows = pl.ds(pl.multiple_of(me * cap, cap), cap)

    def at_zy(i, j):
        return lax.rem(z + i, SIDE) * SIDE + lax.rem(y + j, SIDE)

    def to(dp_index, expert_index):
        return {"device_id": (dp_index, expert_index), "device_id_type": MESH}

    load_win = pltpu.make_async_copy(win_hbm, win, w_sem.at[0])
    load_wout = pltpu.make_async_copy(wout_hbm, wout, w_sem.at[1])
    load_wout.start()
    load_win.start()
    own_t = pltpu.make_async_copy(sent_t.at[me], tok.at[0, own_rows], loc_sem.at[0])
    own_u = pltpu.make_async_copy(sent_u.at[me], ups.at[0, own_rows], loc_sem.at[1])
    own_t.start()
    own_u.start()

    barrier = pltpu.get_barrier_semaphore()
    for k in range(1, 8):
        pl.semaphore_signal(barrier, inc=1, **to(dp, lax.rem(me + k, 8)))
    for i in range(SIDE):
        for j in range(SIDE):
            if i or j:
                pl.semaphore_signal(barrier, inc=1, **to(at_zy(i, j), me))
    pl.semaphore_wait(barrier, 7 + SIDE * SIDE - 1)

    dispatch = []
    for q in range(SIDE):
        for c in range(2):
            if q == 0 and c == 0:
                continue
            there = lax.rem(x + (q ^ (q >> 1)), SIDE) * 2 + lax.rem(core + c, 2)
            n = 2 * q + c
            for h, (src, dst) in enumerate(((sent_t, tok), (sent_u, ups))):
                copy = pltpu.make_async_remote_copy(
                    src_ref=src.at[there],
                    dst_ref=dst.at[0, own_rows],
                    send_sem=d_send.at[h, n],
                    recv_sem=d_recv.at[h, n],
                    **to(dp, there),
                )
                copy.start()
                dispatch.append(copy)

    def clear(i, carry):
        at = pl.ds(pl.multiple_of(i * 16, 16), 16)
        for k in range(SIDE):
            g_in[k, at, :] = jnp.zeros((16, g_in.shape[2]), f32)
            g_out[k, at, :] = jnp.zeros((16, g_out.shape[2]), f32)
        return carry

    lax.fori_loop(0, part // 16, clear, 0)
    load_wout.wait()
    w2_rows = pl.ds(pl.multiple_of(z * part, part), part)

    def chip_rows(q):
        return pl.ds(pl.multiple_of(lax.rem(x + SIDE - (q ^ (q >> 1)), SIDE) * chunk, chunk), chunk)

    def grads(slot, rows):
        t = tok[slot, rows, :]
        u = ups[slot, rows, :]
        act, slope = gelu_parts(dot_nt(w1t[...], t))
        ht[...] = act.astype(bf16)
        hgt[...] = (slope * dot_nt(wout[w2_rows, :], u)).astype(bf16)
        g_out[slot] = g_out[slot] + jnp.dot(ht[...], u, preferred_element_type=f32)
        g_in[slot] = g_in[slot] + jnp.dot(hgt[...], t, preferred_element_type=f32)

    def along_z(buf, slot, to_slot, rows, step, send, recv):
        return pltpu.make_async_remote_copy(
            src_ref=buf.at[slot, rows],
            dst_ref=buf.at[to_slot, rows],
            send_sem=send,
            recv_sem=recv,
            **to(at_zy(step, 0), me),
        )

    def first_hop(q):
        rows = chip_rows(q)
        copies = []
        for h, buf in enumerate((tok, ups)):
            copies.append(along_z(buf, 0, 3, rows, 1, zf_send.at[0, h, q], zf_recv.at[0, h, q]))
            copies.append(along_z(buf, 0, 1, rows, 3, zf_send.at[1, h, q], zf_recv.at[1, h, q]))
        return copies

    def second_hop(q):
        rows = chip_rows(q)
        return [
            along_z(tok, 3, 2, rows, 1, far_send.at[0, q], far_recv.at[0, q]),
            along_z(ups, 1, 2, rows, 3, far_send.at[1, q], far_recv.at[1, q]),
        ]

    own_t.wait()
    own_u.wait()
    for h in range(2):
        dispatch[h].wait_recv()
    for copy in first_hop(0):
        copy.start()
    grads(0, chip_rows(0))

    def own_step(q, carry):
        for c in range(2):
            for h, (src, dst) in enumerate(((sent_t, tok), (sent_u, ups))):
                pltpu.make_async_remote_copy(
                    src_ref=src.at[0],
                    dst_ref=dst.at[0, own_rows],
                    send_sem=d_send.at[h, 2 * q + c],
                    recv_sem=d_recv.at[h, 2 * q + c],
                    **to(dp, lax.rem(me + 1, 8)),
                ).wait_recv()
        for copy in first_hop(q):
            copy.start()
        grads(0, chip_rows(q))
        return carry

    lax.fori_loop(1, SIDE, own_step, 0)

    load_win.wait()
    tile = 512
    rows_all = tok.shape[1]
    half = rows_all // 2

    def forward(n, carry):
        cols = pl.ds(pl.multiple_of(n * tile, tile), tile)
        for r in range(2):
            rows = slice(r * half, (r + 1) * half)
            pre = jnp.dot(tok[0, rows, :], win[:, cols], preferred_element_type=f32)
            hid = gelu_only(pre).astype(bf16)
            more = jnp.dot(hid, wout[cols, :], preferred_element_type=f32)
            acc[rows, :] = acc[rows, :] + more
        return carry

    acc[...] = jnp.zeros_like(acc)
    lax.fori_loop(0, win.shape[1] // tile, forward, 0)

    def round_out(i, carry):
        at = pl.ds(pl.multiple_of(i * cap, cap), cap)
        eout[at, :] = acc[at, :].astype(bf16)
        return carry

    lax.fori_loop(0, rows_all // cap, round_out, 0)
    back = []
    for k in range(1, 8):
        there = lax.rem(me + k, 8)
        copy = pltpu.make_async_remote_copy(
            src_ref=eout.at[pl.ds(pl.multiple_of(there * cap, cap), cap)],
            dst_ref=ret.at[me],
            send_sem=e_send.at[k],
            recv_sem=e_recv.at[k],
            **to(dp, there),
        )
        copy.start()
        back.append(copy)
    back_own = pltpu.make_async_copy(eout.at[own_rows], ret.at[me], loc_sem.at[2])
    back_own.start()

    def near_step(q, carry):
        for copy in first_hop(q):
            copy.wait_recv()
        for copy in second_hop(q):
            copy.start()
        grads(1, chip_rows(q))
        grads(3, chip_rows(q))
        return carry

    lax.fori_loop(0, SIDE, near_step, 0)

    def far_step(q, carry):
        for copy in second_hop(q):
            copy.wait_recv()
        grads(2, chip_rows(q))
        return carry

    lax.fori_loop(0, SIDE, far_step, 0)

    for p, s in enumerate(gram_sums((g_in, g_out), part)):
        gz_out[p : p + 1, :] = jnp.sum(s, axis=0, keepdims=True)
    sums_z = []
    for i in range(1, SIDE):
        copy = pltpu.make_async_remote_copy(
            src_ref=gz_out,
            dst_ref=gz_got.at[SIDE - i],
            send_sem=gz_send.at[SIDE - i],
            recv_sem=gz_recv.at[SIDE - i],
            **to(at_zy(i, 0), me),
        )
        copy.start()
        sums_z.append(copy)
    total = [gz_out[p : p + 1, :] for p in range(len(PAIRS))]
    for copy in sums_z:
        copy.wait_recv()
    for i in range(1, SIDE):
        for p, (a, b) in enumerate(PAIRS):
            q = SLOT[tuple(sorted(((a + i) % SIDE, (b + i) % SIDE)))]
            total[q] = total[q] + gz_got[i, p : p + 1, :]
    total = [jnp.sum(t, axis=1, keepdims=True) for t in total]
    w = tree_weights(lambda a, b: total[SLOT[(a, b)]])

    rows_out = seg_out.shape[0]
    rows_in = seg_in.shape[0]
    sends = []
    for j in (1, 3, 2, 0):
        there = lax.rem(y + j, SIDE)
        base = there * rows_out

        def mix_out(n, carry, j=j, base=base):
            at = pl.ds(pl.multiple_of(base + n * 16, 16), 16)
            v = w[0] * g_out[0, at, :] + w[1] * g_out[1, at, :]
            v = v + w[2] * g_out[2, at, :] + w[3] * g_out[3, at, :]
            if j:
                s_out[at, :] = v
            else:
                r_out[0, pl.ds(pl.multiple_of(n * 16, 16), 16), :] = v
            return carry

        lax.fori_loop(0, rows_out // 16, mix_out, 0)
        if j:
            copy = pltpu.make_async_remote_copy(
                src_ref=s_out.at[pl.ds(pl.multiple_of(base, 8), rows_out)],
                dst_ref=r_out.at[SIDE - j],
                send_sem=yo_send.at[SIDE - j],
                recv_sem=yo_recv.at[SIDE - j],
                **to(at_zy(0, j), me),
            )
            copy.start()
            sends.append(copy)

    def mix_in(n, carry):
        cols = pl.ds(pl.multiple_of(n * LANES, LANES), LANES)
        for m in range(part // LANES):
            at = slice(m * LANES, (m + 1) * LANES)
            v = w[0] * g_in[0, at, cols] + w[1] * g_in[1, at, cols]
            v = v + w[2] * g_in[2, at, cols] + w[3] * g_in[3, at, cols]
            s_in[cols, at] = v.T
        return carry

    lax.fori_loop(0, s_in.shape[0] // LANES, mix_in, 0)
    own_block = pl.ds(pl.multiple_of(z * rows_in, 8), rows_in)
    for j in (1, 3, 2, 0):
        for i in range(SIDE):
            block = at_zy(i, j)
            src = s_in.at[pl.ds(pl.multiple_of(block * rows_in, 8), rows_in)]
            if i or j:
                k = (SIDE - i) % SIDE * SIDE + (SIDE - j) % SIDE
                copy = pltpu.make_async_remote_copy(
                    src_ref=src,
                    dst_ref=r_in.at[(SIDE - j) % SIDE, own_block],
                    send_sem=yi_send.at[k],
                    recv_sem=yi_recv.at[k],
                    **to(block, me),
                )
                copy.start()
                sends.append(copy)
            else:
                keep = pltpu.make_async_copy(src, r_in.at[0, own_block], loc_sem.at[3])
                keep.start()
    for copy in sends:
        copy.wait_recv()
    keep.wait()

    for p, s in enumerate(gram_sums((r_in, r_out), rows_out)):
        gy_out[p : p + 1, :] = jnp.sum(s, axis=0, keepdims=True)
    sums_y = []
    for i in range(SIDE):
        for j in range(SIDE):
            if i or j:
                k = (SIDE - i) % SIDE * SIDE + (SIDE - j) % SIDE
                copy = pltpu.make_async_remote_copy(
                    src_ref=gy_out,
                    dst_ref=gy_got.at[k],
                    send_sem=gy_send.at[k],
                    recv_sem=gy_recv.at[k],
                    **to(at_zy(i, j), me),
                )
                copy.start()
                sums_y.append(copy)
    total = [gy_out[p : p + 1, :] for p in range(len(PAIRS))]
    for copy in sums_y:
        copy.wait_recv()
    for j in range(SIDE):
        for i in range(SIDE):
            if i or j:
                for p, (a, b) in enumerate(PAIRS):
                    q = SLOT[tuple(sorted(((a + j) % SIDE, (b + j) % SIDE)))]
                    total[q] = total[q] + gy_got[i * SIDE + j, p : p + 1, :]
    total = [jnp.sum(t, axis=1, keepdims=True) for t in total]
    v = tree_weights(lambda a, b: total[SLOT[(a, b)]])
    for i in range(SIDE):
        at = slice(i * rows_in, (i + 1) * rows_in)
        seg_in[:, i * part : (i + 1) * part] = (
            v[0] * r_in[0, at, :] + v[1] * r_in[1, at, :]
        ) + (v[2] * r_in[2, at, :] + v[3] * r_in[3, at, :])
        at = slice(i * rows_in, (i + 1) * rows_in)
        seg_out[at, :] = (v[0] * r_out[0, at, :] + v[1] * r_out[1, at, :]) + (
            v[2] * r_out[2, at, :] + v[3] * r_out[3, at, :]
        )

    for copy in dispatch:
        copy.wait_send()

    def drain(q, carry):
        for copy in first_hop(q) + second_hop(q):
            copy.wait_send()
        return carry

    lax.fori_loop(0, SIDE, drain, 0)
    for copy in back:
        copy.wait()
    back_own.wait()
    for copy in sums_z + sends + sums_y:
        copy.wait_send()


def expert_step(sent_t, sent_u, w1t, w_in, w_out):
    f32 = jnp.float32
    bf16 = jnp.bfloat16
    experts, cap, width = sent_t.shape
    rows = experts * cap
    part = w1t.shape[0]
    side = SIDE
    any_space = pl.BlockSpec(memory_space=pl.ANY)
    vmem = pl.BlockSpec(memory_space=pltpu.VMEM)
    rows_in = width // (side * side)
    rows_out = part // side
    dma = pltpu.SemaphoreType.DMA
    return pl.pallas_call(
        kernel,
        out_shape=(
            jax.ShapeDtypeStruct((experts, cap, width), bf16),
            jax.ShapeDtypeStruct((rows_in, side * part), f32),
            jax.ShapeDtypeStruct((rows_out, width), f32),
        ),
        in_specs=[any_space, any_space, vmem, any_space, any_space],
        out_specs=(any_space, vmem, vmem),
        scratch_shapes=[
            pltpu.VMEM((side, rows, width), bf16),
            pltpu.VMEM((side, rows, width), bf16),
            pltpu.VMEM(w_in.shape, bf16),
            pltpu.VMEM(w_out.shape, bf16),
            pltpu.VMEM((side, part, width), f32),
            pltpu.VMEM((side, part, width), f32),
            pltpu.VMEM((part, 2 * cap), bf16),
            pltpu.VMEM((part, 2 * cap), bf16),
            pltpu.VMEM((rows, width), bf16),
            pltpu.VMEM((rows, width), f32),
            pltpu.VMEM((width, part), f32),
            pltpu.VMEM((part, width), f32),
            pltpu.VMEM((side, side * rows_in, part), f32),
            pltpu.VMEM((side, rows_out, width), f32),
            pltpu.VMEM((16, LANES), f32),
            pltpu.VMEM((side, 16, LANES), f32),
            pltpu.VMEM((16, LANES), f32),
            pltpu.VMEM((side * side, 16, LANES), f32),
            dma((2,)),
            dma((4,)),
            dma((2, 8)),
            dma((2, 8)),
            dma((2, 2, side)),
            dma((2, 2, side)),
            dma((2, side)),
            dma((2, side)),
            dma((8,)),
            dma((8,)),
            dma((side,)),
            dma((side,)),
            dma((side,)),
            dma((side,)),
            dma((side * side,)),
            dma((side * side,)),
            dma((side * side,)),
            dma((side * side,)),
        ],
        compiler_params=pltpu.CompilerParams(
            collective_id=0, has_side_effects=True, vmem_limit_bytes=66_000_000
        ),
        name="expert_step",
    )(sent_t, sent_u, w1t, w_in, w_out)


def body(
    tokens,
    assigned,
    gate_prob,
    cotangent,
    weight_in,
    weight_out,
    moment_in,
    moment_out,
    second_in,
    second_out,
):
    f32 = jnp.float32
    bf16 = jnp.bfloat16
    experts = lax.axis_size("expert")
    replicas = lax.axis_size("dp")
    self_index = lax.axis_index("dp")
    z_index = self_index // SIDE
    tok_rows, width = tokens.shape
    hidden_width = weight_in.shape[2]
    part = hidden_width // SIDE
    capacity = 2 * tok_rows // experts
    buffer_rows = experts * capacity
    expert_ids = assigned[:, 0]
    one_hot = (expert_ids[:, None] == jnp.arange(experts, dtype=jnp.int32)[None, :]).astype(
        jnp.int32
    )
    slot_index = jnp.sum((jnp.cumsum(one_hot, axis=0) - one_hot) * one_hot, axis=1)
    slot_code = expert_ids * capacity + slot_index
    table = (jnp.arange(buffer_rows, dtype=jnp.int32)[:, None] == slot_code[None, :]).astype(bf16)
    scaled = (gate_prob * cotangent.astype(f32)).astype(bf16)

    def placed(rows):
        out = jnp.dot(table, rows, preferred_element_type=f32).astype(bf16)
        return out.reshape(experts, capacity, width)

    w_first = weight_in[0]
    w_second = weight_out[0]
    w1t = lax.dynamic_slice_in_dim(w_first, z_index * part, part, 1).T
    returned, seg_first, seg_second = expert_step(
        placed(tokens), placed(scaled), w1t, w_first, w_second
    )
    picked = contract_rows(table, returned.reshape(buffer_rows, width))
    combined = (gate_prob * picked).astype(bf16)

    rows_first = width // replicas
    rows_second = hidden_width // replicas
    own_first = lax.dynamic_slice_in_dim(w_first, self_index * rows_first, rows_first, 0).astype(
        f32
    )
    own_second = lax.dynamic_slice_in_dim(
        w_second, self_index * rows_second, rows_second, 0
    ).astype(f32)
    new_w_first, new_m_first, new_v_first = adam_update(
        seg_first, own_first, moment_in[0], second_in[0]
    )
    new_w_second, new_m_second, new_v_second = adam_update(
        seg_second, own_second, moment_out[0], second_out[0]
    )
    return (
        combined,
        new_w_first[None],
        new_w_second[None],
        new_m_first[None],
        new_m_second[None],
        new_v_first[None],
        new_v_second[None],
    )


def solution(mesh):
    return jax.shard_map(
        body,
        mesh=mesh,
        in_specs=(
            P(("dp", "expert"), None),
            P(("dp", "expert"), None),
            P(("dp", "expert"), None),
            P(("dp", "expert"), None),
            P("expert", None, None),
            P("expert", None, None),
            P("expert", "dp", None),
            P("expert", "dp", None),
            P("expert", "dp", None),
            P("expert", "dp", None),
        ),
        out_specs=(
            P(("dp", "expert"), None),
            P("expert", "dp", None),
            P("expert", "dp", None),
            P("expert", "dp", None),
            P("expert", "dp", None),
            P("expert", "dp", None),
            P("expert", "dp", None),
        ),
        check_vma=False,
    )
```

```python
import jax
import jax.numpy as jnp
from jax import lax
from jax.experimental import pallas as pl
from jax.experimental.pallas import tpu as pltpu
from jax.sharding import PartitionSpec as P

eps_adasum = 1e-06
SIDE = 4
LANES = 128
MESH = pl.DeviceIdType.MESH
PAIRS = [(a, b) for a in range(SIDE) for b in range(a, SIDE)]
SLOT = {pair: k for k, pair in enumerate(PAIRS)}


def adam_update(grad, weight, moment, second):
    new_moment = 0.9 * moment + 0.1 * grad
    new_second = 0.999 * second + 0.001 * grad * grad
    corr_one = 1.0 - 0.9**10.0
    corr_two = 1.0 - 0.999**10.0
    update = new_moment / corr_one / (jnp.sqrt(new_second / corr_two) + 1e-08)
    return (weight - 0.001 * update, new_moment, new_second)


def dot_nt(left, right):
    return lax.dot_general(
        left, right, (((1,), (1,)), ((), ())), preferred_element_type=jnp.float32
    )


def pair_coefs(ab, aa, bb):
    return 1.0 - ab / (2.0 * (aa + eps_adasum)), 1.0 - ab / (2.0 * (bb + eps_adasum))


def tree_weights(g):
    w0, w2 = pair_coefs(g(0, 2), g(0, 0), g(2, 2))
    w1, w3 = pair_coefs(g(1, 3), g(1, 1), g(3, 3))
    aa = w0 * w0 * g(0, 0) + 2.0 * w0 * w2 * g(0, 2) + w2 * w2 * g(2, 2)
    bb = w1 * w1 * g(1, 1) + 2.0 * w1 * w3 * g(1, 3) + w3 * w3 * g(3, 3)
    ab = w0 * (w1 * g(0, 1) + w3 * g(0, 3)) + w2 * (w1 * g(1, 2) + w3 * g(2, 3))
    u, v = pair_coefs(ab, aa, bb)
    return [u * w0, v * w1, u * w2, v * w3]


def gelu_parts(v):
    root = 0.7978845608028654
    square = v * v
    t = jnp.tanh(root * (v + 0.044715 * (square * v)))
    cdf = 0.5 * (1.0 + t)
    slope = cdf + v * (0.5 * (1.0 - t * t)) * (root * (1.0 + 0.134145 * square))
    return v * cdf, slope


def gelu_only(v):
    root = 0.7978845608028654
    return v * (0.5 * (1.0 + jnp.tanh(root * (v + 0.044715 * (v * v * v)))))


def columns_of(row):
    return jnp.broadcast_to(row, (LANES, LANES)).T


def encode(v):
    most = jnp.maximum(jnp.max(jnp.abs(v), axis=0, keepdims=True), 1e-30)
    codes = jnp.round(v * (32767.0 / most)).astype(jnp.int32).astype(jnp.int16)
    return codes, most * (1.0 / 32767.0)


def gram_sums(refs, rows):
    width = refs[0].shape[2]

    def step(i, sums):
        sums = list(sums)
        at = pl.ds(pl.multiple_of(i * 8, 8), 8)
        for ref in refs:
            for c in range(width // LANES):
                cols = slice(c * LANES, (c + 1) * LANES)
                v = [ref[k, at, cols] for k in range(SIDE)]
                for p, (a, b) in enumerate(PAIRS):
                    sums[p] = sums[p] + v[a] * v[b]
        return tuple(sums)

    zero = jnp.zeros((8, LANES), jnp.float32)
    return lax.fori_loop(0, rows // 8, step, (zero,) * len(PAIRS))


def kernel(
    assigned,
    gate,
    tokens,
    cotangent,
    win_hbm,
    wout_hbm,
    combined,
    seg_in,
    seg_out,
    tok,
    ups,
    win,
    wout,
    w1t,
    g_in,
    g_out,
    ht,
    hgt,
    sent_t,
    sent_u,
    scaled,
    code_cols,
    gate_cols,
    eout,
    ret,
    pick,
    acc,
    q_in,
    q_out,
    rq_in,
    rq_out,
    f_in,
    f_out,
    rf_in,
    rf_out,
    gz_out,
    gz_got,
    gy_out,
    gy_got,
    w_sem,
    loc_sem,
    d_send,
    d_recv,
    zf_send,
    zf_recv,
    far_send,
    far_recv,
    e_send,
    e_recv,
    gz_send,
    gz_recv,
    yo_send,
    yo_recv,
    yi_send,
    yi_recv,
    gy_send,
    gy_recv,
):
    f32 = jnp.float32
    bf16 = jnp.bfloat16
    dp = lax.axis_index("dp")
    me = lax.axis_index("expert")
    z, y = lax.div(dp, SIDE), lax.rem(dp, SIDE)
    x, core = lax.div(me, 2), lax.rem(me, 2)
    cap = ret.shape[1]
    chunk = 2 * cap
    part = w1t.shape[0]
    toks, width = tokens.shape
    lane_blocks = width // LANES
    own_rows = pl.ds(pl.multiple_of(me * cap, cap), cap)

    def at_zy(i, j):
        return lax.rem(z + i, SIDE) * SIDE + lax.rem(y + j, SIDE)

    def to(dp_index, expert_index):
        return {"device_id": (dp_index, expert_index), "device_id_type": MESH}

    load_win = pltpu.make_async_copy(win_hbm, win, w_sem.at[0])
    load_wout = pltpu.make_async_copy(wout_hbm, wout, w_sem.at[1])
    load_win.start()
    load_wout.start()

    barrier = pltpu.get_barrier_semaphore()
    for k in range(1, 8):
        pl.semaphore_signal(barrier, inc=1, **to(dp, lax.rem(me + k, 8)))
    for i in range(SIDE):
        for j in range(SIDE):
            if i or j:
                pl.semaphore_signal(barrier, inc=1, **to(at_zy(i, j), me))

    named = assigned[...]
    hot = (lax.broadcasted_iota(jnp.int32, (16, toks), 0) == named).astype(f32)
    earlier = (
        lax.broadcasted_iota(jnp.int32, (toks, toks), 0)
        < lax.broadcasted_iota(jnp.int32, (toks, toks), 1)
    ).astype(f32)
    rank = jnp.dot(hot.astype(bf16), earlier.astype(bf16), preferred_element_type=f32)
    place = (named * cap).astype(f32) + jnp.sum(rank * hot, axis=0, keepdims=True)
    for b in range(toks // LANES):
        at = slice(b * LANES, (b + 1) * LANES)
        code_cols[at, :] = columns_of(place[:, at])
        column = columns_of(gate[:, at])
        gate_cols[at, :] = column
        for c in range(lane_blocks):
            cols = slice(c * LANES, (c + 1) * LANES)
            scaled[at, cols] = (column * cotangent[at, cols].astype(f32)).astype(bf16)

    def chip_at(q):
        return lax.rem(x + (q ^ (q >> 1)), SIDE)

    def chip_rows(q):
        return pl.ds(pl.multiple_of(lax.rem(x + SIDE - (q ^ (q >> 1)), SIDE) * chunk, chunk), chunk)

    def place_rows(q):
        base = (chip_at(q) * chunk).astype(f32)
        slots = lax.broadcasted_iota(jnp.int32, (chunk, toks), 0).astype(f32) + base
        table = (slots == place).astype(f32).astype(bf16)
        sent_t[q] = jnp.dot(table, tokens[...], preferred_element_type=f32).astype(bf16)
        sent_u[q] = jnp.dot(table, scaled[...], preferred_element_type=f32).astype(bf16)

    def dispatch(q, c):
        there = lax.rem(core + c, 2)
        return [
            pltpu.make_async_remote_copy(
                src_ref=src.at[q, pl.ds(pl.multiple_of(there * cap, cap), cap)],
                dst_ref=dst.at[0, own_rows],
                send_sem=d_send.at[h, 2 * q + c],
                recv_sem=d_recv.at[h, 2 * q + c],
                **to(dp, chip_at(q) * 2 + there),
            )
            for h, (src, dst) in enumerate(((sent_t, tok), (sent_u, ups)))
        ]

    def along_z(buf, slot, to_slot, rows, step, send, recv):
        return pltpu.make_async_remote_copy(
            src_ref=buf.at[slot, rows],
            dst_ref=buf.at[to_slot, rows],
            send_sem=send,
            recv_sem=recv,
            **to(at_zy(step, 0), me),
        )

    def first_hop(q, c):
        source = lax.rem(x + SIDE - (q ^ (q >> 1)), SIDE) * 2 + lax.rem(core + c, 2)
        rows = pl.ds(pl.multiple_of(source * cap, cap), cap)
        n = 2 * q + c
        copies = []
        for h, buf in enumerate((tok, ups)):
            copies.append(along_z(buf, 0, 3, rows, 1, zf_send.at[0, h, n], zf_recv.at[0, h, n]))
            copies.append(along_z(buf, 0, 1, rows, 3, zf_send.at[1, h, n], zf_recv.at[1, h, n]))
        return copies

    def second_hop(q):
        rows = chip_rows(q)
        return [
            along_z(tok, 3, 2, rows, 1, far_send.at[0, q], far_recv.at[0, q]),
            along_z(ups, 1, 2, rows, 3, far_send.at[1, q], far_recv.at[1, q]),
        ]

    place_rows(0)
    half_rows = pl.ds(pl.multiple_of(core * cap, cap), cap)
    tok[0, own_rows, :] = sent_t[0, half_rows, :]
    ups[0, own_rows, :] = sent_u[0, half_rows, :]
    pl.semaphore_wait(barrier, 7 + SIDE * SIDE - 1)
    for copy in dispatch(0, 1) + first_hop(0, 0):
        copy.start()

    def place_step(q, carry):
        place_rows(q)
        for copy in dispatch(q, 0) + dispatch(q, 1):
            copy.start()
        return carry

    lax.fori_loop(1, SIDE, place_step, 0)
    for copy in dispatch(0, 1):
        copy.wait_recv()
    for copy in first_hop(0, 1):
        copy.start()

    load_win.wait()

    def turn(n, carry):
        at = pl.ds(pl.multiple_of(n * LANES, LANES), LANES)
        cols = pl.ds(pl.multiple_of(z * part + n * LANES, LANES), LANES)
        for c in range(lane_blocks):
            rows = slice(c * LANES, (c + 1) * LANES)
            w1t[at, rows] = win[rows, cols].astype(f32).T.astype(bf16)
        return carry

    lax.fori_loop(0, part // LANES, turn, 0)

    def clear(i, carry):
        at = pl.ds(pl.multiple_of(i * 16, 16), 16)
        for k in range(SIDE):
            g_in[k, at, :] = jnp.zeros((16, width), f32)
            g_out[k, at, :] = jnp.zeros((16, width), f32)
        return carry

    lax.fori_loop(0, part // 16, clear, 0)
    load_wout.wait()
    w2_rows = pl.ds(pl.multiple_of(z * part, part), part)

    def grads(slot, rows):
        t = tok[slot, rows, :]
        u = ups[slot, rows, :]
        act, slope = gelu_parts(dot_nt(w1t[...], t))
        ht[...] = act.astype(bf16)
        hgt[...] = (slope * dot_nt(wout[w2_rows, :], u)).astype(bf16)
        g_out[slot] = g_out[slot] + jnp.dot(ht[...], u, preferred_element_type=f32)
        g_in[slot] = g_in[slot] + jnp.dot(hgt[...], t, preferred_element_type=f32)

    def own_step(q, carry):
        for c in range(2):
            for copy in dispatch(q, c):
                copy.wait_recv()
            for copy in first_hop(q, c):
                copy.start()
        grads(0, chip_rows(q - 1))
        return carry

    lax.fori_loop(1, SIDE, own_step, 0)
    grads(0, chip_rows(SIDE - 1))

    tile = 512
    rows_all = tok.shape[1]
    half = rows_all // 2

    def forward(n, carry):
        cols = pl.ds(pl.multiple_of(n * tile, tile), tile)
        for r in range(2):
            rows = slice(r * half, (r + 1) * half)
            pre = jnp.dot(tok[0, rows, :], win[:, cols], preferred_element_type=f32)
            hid = gelu_only(pre).astype(bf16)
            more = jnp.dot(hid, wout[cols, :], preferred_element_type=f32)
            acc[rows, :] = acc[rows, :] + more
        return carry

    acc[...] = jnp.zeros_like(acc)
    lax.fori_loop(0, win.shape[1] // tile, forward, 0)

    def round_out(i, carry):
        at = pl.ds(pl.multiple_of(i * cap, cap), cap)
        eout[at, :] = acc[at, :].astype(bf16)
        return carry

    lax.fori_loop(0, rows_all // cap, round_out, 0)

    def back(k):
        there = lax.rem(me + k, 8)
        return pltpu.make_async_remote_copy(
            src_ref=eout.at[pl.ds(pl.multiple_of(there * cap, cap), cap)],
            dst_ref=ret.at[me],
            send_sem=e_send.at[k],
            recv_sem=e_recv.at[k],
            **to(dp, there),
        )

    for k in range(1, 8):
        back(k).start()
    back_own = pltpu.make_async_copy(eout.at[own_rows], ret.at[me], loc_sem.at[0])
    back_own.start()

    def near_step(q, carry):
        for c in range(2):
            for copy in first_hop(q, c):
                copy.wait_recv()
        for copy in second_hop(q):
            copy.start()
        grads(1, chip_rows(q))
        grads(3, chip_rows(q))
        return carry

    lax.fori_loop(0, SIDE, near_step, 0)

    for k in range(1, 8):
        back(k).wait_recv()
    back_own.wait()
    for p in range(8):
        cols = slice(p * cap, (p + 1) * cap)
        for b in range(toks // LANES):
            at = slice(b * LANES, (b + 1) * LANES)
            slots = lax.broadcasted_iota(jnp.int32, (LANES, cap), 1).astype(f32) + float(p * cap)
            pick[at, cols] = (slots == code_cols[at, :]).astype(f32).astype(bf16)
    picked = jnp.dot(pick[...], ret[...].reshape(8 * cap, width), preferred_element_type=f32)
    for c in range(lane_blocks):
        cols = slice(c * LANES, (c + 1) * LANES)
        combined[:, cols] = (gate_cols[...] * picked[:, cols]).astype(bf16)

    def far_step(q, carry):
        for copy in second_hop(q):
            copy.wait_recv()
        grads(2, chip_rows(q))
        return carry

    lax.fori_loop(0, SIDE, far_step, 0)

    for p, s in enumerate(gram_sums((g_in, g_out), part)):
        gz_out[p : p + 1, :] = jnp.sum(s, axis=0, keepdims=True)
    sums_z = []
    for i in range(1, SIDE):
        copy = pltpu.make_async_remote_copy(
            src_ref=gz_out,
            dst_ref=gz_got.at[SIDE - i],
            send_sem=gz_send.at[SIDE - i],
            recv_sem=gz_recv.at[SIDE - i],
            **to(at_zy(i, 0), me),
        )
        copy.start()
        sums_z.append(copy)
    total = [gz_out[p : p + 1, :] for p in range(len(PAIRS))]
    for copy in sums_z:
        copy.wait_recv()
    for i in range(1, SIDE):
        for p, (a, b) in enumerate(PAIRS):
            q = SLOT[tuple(sorted(((a + i) % SIDE, (b + i) % SIDE)))]
            total[q] = total[q] + gz_got[i, p : p + 1, :]
    total = [jnp.sum(t, axis=1, keepdims=True) for t in total]
    w = tree_weights(lambda a, b: total[SLOT[(a, b)]])

    rows_out = seg_out.shape[0]
    rows_in = seg_in.shape[0]

    def send_out(j):
        k = (SIDE - j) % SIDE
        return [
            pltpu.make_async_remote_copy(
                src_ref=src.at[j],
                dst_ref=dst.at[k],
                send_sem=yo_send.at[h, k],
                recv_sem=yo_recv.at[h, k],
                **to(at_zy(0, j), me),
            )
            for h, (src, dst) in enumerate(((q_out, rq_out), (f_out, rf_out)))
        ]

    def send_in(i, j):
        n = i * SIDE + j
        k = (SIDE - j) % SIDE
        m = lax.rem(SIDE - i, SIDE) * SIDE + k
        return [
            pltpu.make_async_remote_copy(
                src_ref=src.at[n],
                dst_ref=dst.at[k, z],
                send_sem=yi_send.at[h, m],
                recv_sem=yi_recv.at[h, m],
                **to(at_zy(i, j), me),
            )
            for h, (src, dst) in enumerate(((q_in, rq_in), (f_in, rf_in)))
        ]

    for j in (1, 3, 2):
        rows = pl.ds(pl.multiple_of(lax.rem(y + j, SIDE) * rows_out, 8), rows_out)
        for c in range(lane_blocks):
            cols = slice(c * LANES, (c + 1) * LANES)
            v = w[0] * g_out[0, rows, cols] + w[1] * g_out[1, rows, cols]
            v = v + w[2] * g_out[2, rows, cols] + w[3] * g_out[3, rows, cols]
            q_out[j, :, cols], f_out[j, c : c + 1, :] = encode(v)
        for copy in send_out(j):
            copy.start()

    def mix_in(n, carry):
        cols = pl.ds(pl.multiple_of(n * LANES, LANES), LANES)
        for m in range(part // LANES):
            at = slice(m * LANES, (m + 1) * LANES)
            v = w[0] * g_in[0, at, cols] + w[1] * g_in[1, at, cols]
            v = v + w[2] * g_in[2, at, cols] + w[3] * g_in[3, at, cols]
            acc[cols, at] = v.T
        return carry

    lax.fori_loop(0, width // LANES, mix_in, 0)

    def block_rows(i, j):
        return pl.ds(pl.multiple_of(at_zy(i, j) * rows_in, 8), rows_in)

    for j in (1, 3, 2, 0):

        def code_in(i, carry, j=j):
            rows = block_rows(i, j)
            for c in range(lane_blocks):
                cols = slice(c * LANES, (c + 1) * LANES)
                codes, factor = encode(acc[rows, cols])
                q_in[i * SIDE + j, :, cols] = codes
                f_in[i * SIDE + j, c : c + 1, :] = factor
            for copy in send_in(i, j):
                copy.start()
            return carry

        lax.fori_loop(0 if j else 1, SIDE, code_in, 0)

    g_in[0, pl.ds(pl.multiple_of(z * rows_in, 8), rows_in), :] = acc[block_rows(0, 0), :]
    base = y * rows_out

    def mix_own(n, carry):
        rows = pl.ds(pl.multiple_of(base + n * 16, 16), 16)
        v = w[0] * g_out[0, rows, :] + w[1] * g_out[1, rows, :]
        v = v + w[2] * g_out[2, rows, :] + w[3] * g_out[3, rows, :]
        g_out[0, pl.ds(pl.multiple_of(n * 16, 16), 16), :] = v
        return carry

    lax.fori_loop(0, rows_out // 16, mix_own, 0)

    for k in (0, 3, 1, 2):
        j = (SIDE - k) % SIDE

        def decode_in(i, carry, j=j, k=k):
            for copy in send_in(i, j):
                copy.wait_recv()
            there = lax.rem(z + SIDE - i, SIDE)
            rows = pl.ds(pl.multiple_of(there * rows_in, 8), rows_in)
            for c in range(lane_blocks):
                cols = slice(c * LANES, (c + 1) * LANES)
                codes = rq_in[k, there, :, cols].astype(jnp.int32).astype(f32)
                g_in[k, rows, cols] = codes * rf_in[k, there, c : c + 1, :]
            return carry

        if k:
            for copy in send_out(j):
                copy.wait_recv()
            for c in range(lane_blocks):
                cols = slice(c * LANES, (c + 1) * LANES)
                codes = rq_out[k, :, cols].astype(jnp.int32).astype(f32)
                g_out[k, :rows_out, cols] = codes * rf_out[k, c : c + 1, :]
        lax.fori_loop(0 if k else 1, SIDE, decode_in, 0)

    for p, s in enumerate(gram_sums((g_in, g_out), rows_out)):
        gy_out[p : p + 1, :] = jnp.sum(s, axis=0, keepdims=True)
    sums_y = []
    for i in range(SIDE):
        for j in range(SIDE):
            if i or j:
                k = (SIDE - i) % SIDE * SIDE + (SIDE - j) % SIDE
                copy = pltpu.make_async_remote_copy(
                    src_ref=gy_out,
                    dst_ref=gy_got.at[k],
                    send_sem=gy_send.at[k],
                    recv_sem=gy_recv.at[k],
                    **to(at_zy(i, j), me),
                )
                copy.start()
                sums_y.append(copy)
    total = [gy_out[p : p + 1, :] for p in range(len(PAIRS))]
    for copy in sums_y:
        copy.wait_recv()
    for j in range(SIDE):
        for i in range(SIDE):
            if i or j:
                for p, (a, b) in enumerate(PAIRS):
                    q = SLOT[tuple(sorted(((a + j) % SIDE, (b + j) % SIDE)))]
                    total[q] = total[q] + gy_got[i * SIDE + j, p : p + 1, :]
    total = [jnp.sum(t, axis=1, keepdims=True) for t in total]
    v = tree_weights(lambda a, b: total[SLOT[(a, b)]])
    for i in range(SIDE):
        at = slice(i * rows_in, (i + 1) * rows_in)
        seg_in[:, i * part : (i + 1) * part] = (v[0] * g_in[0, at, :] + v[1] * g_in[1, at, :]) + (
            v[2] * g_in[2, at, :] + v[3] * g_in[3, at, :]
        )
        seg_out[at, :] = (v[0] * g_out[0, at, :] + v[1] * g_out[1, at, :]) + (
            v[2] * g_out[2, at, :] + v[3] * g_out[3, at, :]
        )

    def drain(q, carry):
        for copy in first_hop(q, 0) + first_hop(q, 1) + second_hop(q):
            copy.wait_send()
        return carry

    lax.fori_loop(0, SIDE, drain, 0)

    def drain_dispatch(q, carry):
        for copy in dispatch(q, 0) + dispatch(q, 1):
            copy.wait_send()
        return carry

    lax.fori_loop(1, SIDE, drain_dispatch, 0)
    for copy in dispatch(0, 1):
        copy.wait_send()
    for k in range(1, 8):
        back(k).wait_send()
    for j in range(SIDE):

        def drain_in(i, carry, j=j):
            for copy in send_in(i, j):
                copy.wait_send()
            return carry

        lax.fori_loop(0 if j else 1, SIDE, drain_in, 0)
        if j:
            for copy in send_out(j):
                copy.wait_send()
    for copy in sums_z + sums_y:
        copy.wait_send()


def expert_step(assigned, gate, tokens, cotangent, w_in, w_out):
    f32 = jnp.float32
    bf16 = jnp.bfloat16
    i16 = jnp.int16
    experts = 8
    toks, width = tokens.shape
    cap = 2 * toks // experts
    rows = experts * cap
    side = SIDE
    part = w_in.shape[1] // side
    any_space = pl.BlockSpec(memory_space=pl.ANY)
    vmem = pl.BlockSpec(memory_space=pltpu.VMEM)
    rows_in = width // (side * side)
    rows_out = part // side
    dma = pltpu.SemaphoreType.DMA
    return pl.pallas_call(
        kernel,
        out_shape=(
            jax.ShapeDtypeStruct((toks, width), bf16),
            jax.ShapeDtypeStruct((rows_in, side * part), f32),
            jax.ShapeDtypeStruct((rows_out, width), f32),
        ),
        in_specs=[vmem, vmem, vmem, vmem, any_space, any_space],
        out_specs=(vmem, vmem, vmem),
        scratch_shapes=[
            pltpu.VMEM((side, rows, width), bf16),
            pltpu.VMEM((side, rows, width), bf16),
            pltpu.VMEM(w_in.shape, bf16),
            pltpu.VMEM(w_out.shape, bf16),
            pltpu.VMEM((part, width), bf16),
            pltpu.VMEM((side, part, width), f32),
            pltpu.VMEM((side, part, width), f32),
            pltpu.VMEM((part, 2 * cap), bf16),
            pltpu.VMEM((part, 2 * cap), bf16),
            pltpu.VMEM((side, 2 * cap, width), bf16),
            pltpu.VMEM((side, 2 * cap, width), bf16),
            pltpu.VMEM((toks, width), bf16),
            pltpu.VMEM((toks, LANES), f32),
            pltpu.VMEM((toks, LANES), f32),
            pltpu.VMEM((rows, width), bf16),
            pltpu.VMEM((experts, cap, width), bf16),
            pltpu.VMEM((toks, rows), bf16),
            pltpu.VMEM((rows, width), f32),
            pltpu.VMEM((side * side, rows_in, part), i16),
            pltpu.VMEM((side, rows_out, width), i16),
            pltpu.VMEM((side, side, rows_in, part), i16),
            pltpu.VMEM((side, rows_out, width), i16),
            pltpu.VMEM((side * side, 8, LANES), f32),
            pltpu.VMEM((side, 8, LANES), f32),
            pltpu.VMEM((side, side, 8, LANES), f32),
            pltpu.VMEM((side, 8, LANES), f32),
            pltpu.VMEM((16, LANES), f32),
            pltpu.VMEM((side, 16, LANES), f32),
            pltpu.VMEM((16, LANES), f32),
            pltpu.VMEM((side * side, 16, LANES), f32),
            dma((2,)),
            dma((1,)),
            dma((2, 8)),
            dma((2, 8)),
            dma((2, 2, 8)),
            dma((2, 2, 8)),
            dma((2, side)),
            dma((2, side)),
            dma((8,)),
            dma((8,)),
            dma((side,)),
            dma((side,)),
            dma((2, side)),
            dma((2, side)),
            dma((2, side * side)),
            dma((2, side * side)),
            dma((side * side,)),
            dma((side * side,)),
        ],
        compiler_params=pltpu.CompilerParams(
            collective_id=0, has_side_effects=True, vmem_limit_bytes=67_000_000
        ),
        name="expert_step",
    )(assigned, gate, tokens, cotangent, w_in, w_out)


def body(
    tokens,
    assigned,
    gate_prob,
    cotangent,
    weight_in,
    weight_out,
    moment_in,
    moment_out,
    second_in,
    second_out,
):
    f32 = jnp.float32
    replicas = lax.axis_size("dp")
    self_index = lax.axis_index("dp")
    toks, width = tokens.shape
    hidden_width = weight_in.shape[2]
    w_first = weight_in[0]
    w_second = weight_out[0]
    combined, seg_first, seg_second = expert_step(
        assigned.reshape(1, toks), gate_prob.reshape(1, toks), tokens, cotangent, w_first, w_second
    )
    rows_first = width // replicas
    rows_second = hidden_width // replicas
    own_first = lax.dynamic_slice_in_dim(w_first, self_index * rows_first, rows_first, 0).astype(
        f32
    )
    own_second = lax.dynamic_slice_in_dim(
        w_second, self_index * rows_second, rows_second, 0
    ).astype(f32)
    new_w_first, new_m_first, new_v_first = adam_update(
        seg_first, own_first, moment_in[0], second_in[0]
    )
    new_w_second, new_m_second, new_v_second = adam_update(
        seg_second, own_second, moment_out[0], second_out[0]
    )
    return (
        combined,
        new_w_first[None],
        new_w_second[None],
        new_m_first[None],
        new_m_second[None],
        new_v_first[None],
        new_v_second[None],
    )


def solution(mesh):
    return jax.shard_map(
        body,
        mesh=mesh,
        in_specs=(
            P(("dp", "expert"), None),
            P(("dp", "expert"), None),
            P(("dp", "expert"), None),
            P(("dp", "expert"), None),
            P("expert", None, None),
            P("expert", None, None),
            P("expert", "dp", None),
            P("expert", "dp", None),
            P("expert", "dp", None),
            P("expert", "dp", None),
        ),
        out_specs=(
            P(("dp", "expert"), None),
            P("expert", "dp", None),
            P("expert", "dp", None),
            P("expert", "dp", None),
            P("expert", "dp", None),
            P("expert", "dp", None),
            P("expert", "dp", None),
        ),
        check_vma=False,
    )
```

```python
import jax
import jax.numpy as jnp
from jax import lax
from jax.experimental import pallas as pl
from jax.experimental.pallas import tpu as pltpu
from jax.sharding import PartitionSpec as P

eps_adasum = 1e-06
SIDE = 4
LANES = 128
SPLIT = 512
MESH = pl.DeviceIdType.MESH
PAIRS = [(a, b) for a in range(SIDE) for b in range(a, SIDE)]
SLOT = {pair: k for k, pair in enumerate(PAIRS)}


def adam_update(grad, weight, moment, second):
    new_moment = 0.9 * moment + 0.1 * grad
    new_second = 0.999 * second + 0.001 * grad * grad
    corr_one = 1.0 - 0.9**10.0
    corr_two = 1.0 - 0.999**10.0
    update = new_moment / corr_one / (jnp.sqrt(new_second / corr_two) + 1e-08)
    return (weight - 0.001 * update, new_moment, new_second)


def dot_nt(left, right):
    return lax.dot_general(
        left, right, (((1,), (1,)), ((), ())), preferred_element_type=jnp.float32
    )


def pair_coefs(ab, aa, bb):
    return 1.0 - ab / (2.0 * (aa + eps_adasum)), 1.0 - ab / (2.0 * (bb + eps_adasum))


def tree_weights(g):
    w0, w2 = pair_coefs(g(0, 2), g(0, 0), g(2, 2))
    w1, w3 = pair_coefs(g(1, 3), g(1, 1), g(3, 3))
    aa = w0 * w0 * g(0, 0) + 2.0 * w0 * w2 * g(0, 2) + w2 * w2 * g(2, 2)
    bb = w1 * w1 * g(1, 1) + 2.0 * w1 * w3 * g(1, 3) + w3 * w3 * g(3, 3)
    ab = w0 * (w1 * g(0, 1) + w3 * g(0, 3)) + w2 * (w1 * g(1, 2) + w3 * g(2, 3))
    u, v = pair_coefs(ab, aa, bb)
    return [u * w0, v * w1, u * w2, v * w3]


def gelu_parts(v):
    root = 0.7978845608028654
    square = v * v
    t = jnp.tanh(root * (v + 0.044715 * (square * v)))
    cdf = 0.5 * (1.0 + t)
    slope = cdf + v * (0.5 * (1.0 - t * t)) * (root * (1.0 + 0.134145 * square))
    return v * cdf, slope


def gelu_only(v):
    root = 0.7978845608028654
    return v * (0.5 * (1.0 + jnp.tanh(root * (v + 0.044715 * (v * v * v)))))


def columns_of(row):
    return jnp.broadcast_to(row, (LANES, LANES)).T


def encode(v):
    most = jnp.maximum(jnp.max(jnp.abs(v), axis=0, keepdims=True), 1e-30)
    codes = jnp.round(v * (32767.0 / most)).astype(jnp.int32).astype(jnp.int16)
    return codes, most * (1.0 / 32767.0)


def gram_sums(refs, rows):
    width = refs[0].shape[2]

    def step(i, sums):
        sums = list(sums)
        at = pl.ds(pl.multiple_of(i * 8, 8), 8)
        for ref in refs:
            for c in range(width // LANES):
                cols = slice(c * LANES, (c + 1) * LANES)
                v = [ref[k, at, cols] for k in range(SIDE)]
                for p, (a, b) in enumerate(PAIRS):
                    sums[p] = sums[p] + v[a] * v[b]
        return tuple(sums)

    zero = jnp.zeros((8, LANES), jnp.float32)
    return lax.fori_loop(0, rows // 8, step, (zero,) * len(PAIRS))


def kernel(
    assigned,
    gate,
    tokens,
    cotangent,
    win_hbm,
    wout_hbm,
    combined,
    seg_in,
    seg_out,
    tok,
    ups,
    win,
    wout,
    w1t,
    g_in,
    g_out,
    ht,
    hgt,
    sent_t,
    sent_u,
    scaled,
    raw,
    place_own,
    places,
    code_cols,
    gate_cols,
    eout,
    ret,
    acc,
    q_in,
    q_out,
    rq_in,
    rq_out,
    f_in,
    f_out,
    rf_in,
    rf_out,
    gz_out,
    gz_got,
    gy_out,
    gy_got,
    w_sem,
    loc_sem,
    d_send,
    d_recv,
    rz_send,
    rz_recv,
    rfar_send,
    rfar_recv,
    b_send,
    b_recv,
    zf_send,
    zf_recv,
    far_send,
    far_recv,
    e_send,
    e_recv,
    gz_send,
    gz_recv,
    yo_send,
    yo_recv,
    yi_send,
    yi_recv,
    gy_send,
    gy_recv,
):
    f32 = jnp.float32
    bf16 = jnp.bfloat16
    dp = lax.axis_index("dp")
    me = lax.axis_index("expert")
    z, y = lax.div(dp, SIDE), lax.rem(dp, SIDE)
    x, core = lax.div(me, 2), lax.rem(me, 2)
    cap = ret.shape[1]
    chunk = 2 * cap
    part = w1t.shape[0]
    toks, width = tokens.shape
    lane_blocks = width // LANES
    own_rows = pl.ds(pl.multiple_of(me * cap, cap), cap)

    def at_zy(i, j):
        return lax.rem(z + i, SIDE) * SIDE + lax.rem(y + j, SIDE)

    def to(dp_index, expert_index):
        return {"device_id": (dp_index, expert_index), "device_id_type": MESH}

    load_win = pltpu.make_async_copy(win_hbm, win, w_sem.at[0])
    load_wout = pltpu.make_async_copy(wout_hbm, wout, w_sem.at[1])
    load_win.start()
    load_wout.start()

    barrier = pltpu.get_barrier_semaphore()
    for k in range(1, 8):
        pl.semaphore_signal(barrier, inc=1, **to(dp, lax.rem(me + k, 8)))
    for i in range(SIDE):
        for j in range(SIDE):
            if i or j:
                pl.semaphore_signal(barrier, inc=1, **to(at_zy(i, j), me))

    named = assigned[...]
    hot = (lax.broadcasted_iota(jnp.int32, (16, toks), 0) == named).astype(f32)
    earlier = (
        lax.broadcasted_iota(jnp.int32, (toks, toks), 0)
        < lax.broadcasted_iota(jnp.int32, (toks, toks), 1)
    ).astype(f32)
    rank = jnp.dot(hot.astype(bf16), earlier.astype(bf16), preferred_element_type=f32)
    place = (named * cap).astype(f32) + jnp.sum(rank * hot, axis=0, keepdims=True)
    place_own[...] = jnp.broadcast_to(place, place_own.shape)
    for b in range(toks // LANES):
        at = slice(b * LANES, (b + 1) * LANES)
        code_cols[at, :] = columns_of(place[:, at])
        column = columns_of(gate[:, at])
        gate_cols[at, :] = column
        for c in range(lane_blocks):
            cols = slice(c * LANES, (c + 1) * LANES)
            scaled[at, cols] = (column * cotangent[at, cols].astype(f32)).astype(bf16)

    def chip_at(q):
        return lax.rem(x + (q ^ (q >> 1)), SIDE)

    def chip_rows(q):
        return pl.ds(pl.multiple_of(lax.rem(x + SIDE - (q ^ (q >> 1)), SIDE) * chunk, chunk), chunk)

    def table_of(q, places_row):
        base = (chip_at(q) * chunk).astype(f32)
        slots = lax.broadcasted_iota(jnp.int32, (chunk, toks), 0).astype(f32) + base
        return (slots == places_row).astype(f32).astype(bf16)

    def place_rows(q):
        table = table_of(q, place)
        sent_t[q] = jnp.dot(table, tokens[...], preferred_element_type=f32).astype(bf16)
        sent_u[q] = jnp.dot(table, scaled[...], preferred_element_type=f32).astype(bf16)

    def dispatch(q, c):
        there = lax.rem(core + c, 2)
        return [
            pltpu.make_async_remote_copy(
                src_ref=src.at[q, pl.ds(pl.multiple_of(there * cap, cap), cap)],
                dst_ref=dst.at[0, own_rows],
                send_sem=d_send.at[h, 2 * q + c],
                recv_sem=d_recv.at[h, 2 * q + c],
                **to(dp, chip_at(q) * 2 + there),
            )
            for h, (src, dst) in enumerate(((sent_t, tok), (sent_u, ups)))
        ]

    def along_z(buf, slot, to_slot, rows, step, send, recv):
        return pltpu.make_async_remote_copy(
            src_ref=buf.at[slot, rows, :SPLIT],
            dst_ref=buf.at[to_slot, rows, :SPLIT],
            send_sem=send,
            recv_sem=recv,
            **to(at_zy(step, 0), me),
        )

    def first_hop(q, c):
        source = lax.rem(x + SIDE - (q ^ (q >> 1)), SIDE) * 2 + lax.rem(core + c, 2)
        rows = pl.ds(pl.multiple_of(source * cap, cap), cap)
        n = 2 * q + c
        copies = []
        for h, buf in enumerate((tok, ups)):
            copies.append(along_z(buf, 0, 3, rows, 1, zf_send.at[0, h, n], zf_recv.at[0, h, n]))
            copies.append(along_z(buf, 0, 1, rows, 3, zf_send.at[1, h, n], zf_recv.at[1, h, n]))
        return copies

    def second_hop(q):
        rows = chip_rows(q)
        return [
            along_z(tok, 3, 2, rows, 1, far_send.at[0, q], far_recv.at[0, q]),
            along_z(ups, 1, 2, rows, 3, far_send.at[1, q], far_recv.at[1, q]),
        ]

    def raw_hop(what, way):
        src, dst, base = (
            (tokens.at[:, SPLIT:], raw, 0),
            (scaled.at[:, SPLIT:], raw, 3),
            (place_own, places, 0),
        )[what]
        return pltpu.make_async_remote_copy(
            src_ref=src,
            dst_ref=dst.at[base + (0 if way else 2)],
            send_sem=rz_send.at[way, what],
            recv_sem=rz_recv.at[way, what],
            **to(at_zy(3 if way else 1, 0), me),
        )

    def raw_far(what):
        buf, source, there = ((raw, 2, 1), (raw, 3, 4), (places, 2, 1))[what]
        return pltpu.make_async_remote_copy(
            src_ref=buf.at[source],
            dst_ref=buf.at[there],
            send_sem=rfar_send.at[what],
            recv_sem=rfar_recv.at[what],
            **to(at_zy(3 if what == 1 else 1, 0), me),
        )

    def raw_dispatch(slot, q, c):
        there = lax.rem(core + c, 2)
        cols = slice((slot - 1) * (width - SPLIT), slot * (width - SPLIT))
        return [
            pltpu.make_async_remote_copy(
                src_ref=src.at[q, pl.ds(pl.multiple_of(there * cap, cap), cap), cols],
                dst_ref=dst.at[slot, own_rows, SPLIT:],
                send_sem=b_send.at[slot - 1, h, 2 * q + c],
                recv_sem=b_recv.at[slot - 1, h, 2 * q + c],
                **to(dp, chip_at(q) * 2 + there),
            )
            for h, (src, dst) in enumerate(((sent_t, tok), (sent_u, ups)))
        ]

    pl.semaphore_wait(barrier, 7 + SIDE * SIDE - 1)
    for what in (0, 1, 2):
        for way in range(2):
            raw_hop(what, way).start()
    place_rows(0)
    half_rows = pl.ds(pl.multiple_of(core * cap, cap), cap)
    tok[0, own_rows, :] = sent_t[0, half_rows, :]
    ups[0, own_rows, :] = sent_u[0, half_rows, :]
    for copy in dispatch(0, 1) + first_hop(0, 0):
        copy.start()

    def place_step(q, carry):
        place_rows(q)
        for copy in dispatch(q, 0) + dispatch(q, 1):
            copy.start()
        return carry

    lax.fori_loop(1, SIDE, place_step, 0)
    for copy in dispatch(0, 1):
        copy.wait_recv()
    for copy in first_hop(0, 1):
        copy.start()

    load_win.wait()

    def turn(n, carry):
        at = pl.ds(pl.multiple_of(n * LANES, LANES), LANES)
        cols = pl.ds(pl.multiple_of(z * part + n * LANES, LANES), LANES)
        for c in range(lane_blocks):
            rows = slice(c * LANES, (c + 1) * LANES)
            w1t[at, rows] = win[rows, cols].astype(f32).T.astype(bf16)
        return carry

    lax.fori_loop(0, part // LANES, turn, 0)

    def clear(i, carry):
        at = pl.ds(pl.multiple_of(i * 16, 16), 16)
        for k in range(SIDE):
            g_in[k, at, :] = jnp.zeros((16, width), f32)
            g_out[k, at, :] = jnp.zeros((16, width), f32)
        return carry

    lax.fori_loop(0, part // 16, clear, 0)
    load_wout.wait()
    w2_rows = pl.ds(pl.multiple_of(z * part, part), part)

    def grads(slot, rows):
        t = tok[slot, rows, :]
        u = ups[slot, rows, :]
        act, slope = gelu_parts(dot_nt(w1t[...], t))
        ht[...] = act.astype(bf16)
        hgt[...] = (slope * dot_nt(wout[w2_rows, :], u)).astype(bf16)
        g_out[slot] = g_out[slot] + jnp.dot(ht[...], u, preferred_element_type=f32)
        g_in[slot] = g_in[slot] + jnp.dot(hgt[...], t, preferred_element_type=f32)

    for what in range(3):
        for way in range(2):
            raw_hop(what, way).wait_recv()
    for what in range(3):
        raw_far(what).start()

    def own_step(q, carry):
        for c in range(2):
            for copy in dispatch(q, c):
                copy.wait_recv()
            for copy in first_hop(q, c):
                copy.start()
        grads(0, chip_rows(q - 1))
        return carry

    lax.fori_loop(1, SIDE, own_step, 0)
    grads(0, chip_rows(SIDE - 1))

    def place_raw(slot, q):
        cols = slice((slot - 1) * (width - SPLIT), slot * (width - SPLIT))
        table = table_of(q, places[slot - 1, 0:1, :])
        for sent, base in ((sent_t, 0), (sent_u, 3)):
            rows = jnp.dot(table, raw[base + slot - 1], preferred_element_type=f32)
            sent[q, :, cols] = rows.astype(bf16)

    for slot in (1, 3, 2):
        if slot == 2:
            for what in range(3):
                raw_far(what).wait_recv()
        cols = slice((slot - 1) * (width - SPLIT), slot * (width - SPLIT))
        if slot == 1:
            for copy in dispatch(0, 1):
                copy.wait_send()
        place_raw(slot, 0)
        tok[slot, own_rows, SPLIT:] = sent_t[0, half_rows, cols]
        ups[slot, own_rows, SPLIT:] = sent_u[0, half_rows, cols]
        for copy in raw_dispatch(slot, 0, 1):
            copy.start()

        def raw_step(q, carry, slot=slot):
            if slot == 1:
                for copy in dispatch(q, 0) + dispatch(q, 1):
                    copy.wait_send()
            place_raw(slot, q)
            for copy in raw_dispatch(slot, q, 0) + raw_dispatch(slot, q, 1):
                copy.start()
            return carry

        lax.fori_loop(1, SIDE, raw_step, 0)

    def raw_arrived(slot, q):
        @pl.when(q > 0)
        def _():
            for copy in raw_dispatch(slot, q, 0):
                copy.wait_recv()

        for copy in raw_dispatch(slot, q, 1):
            copy.wait_recv()

    tile = 512
    rows_all = tok.shape[1]
    half = rows_all // 2

    def forward(n, carry):
        cols = pl.ds(pl.multiple_of(n * tile, tile), tile)
        for r in range(2):
            rows = slice(r * half, (r + 1) * half)
            pre = jnp.dot(tok[0, rows, :], win[:, cols], preferred_element_type=f32)
            hid = gelu_only(pre).astype(bf16)
            more = jnp.dot(hid, wout[cols, :], preferred_element_type=f32)
            acc[rows, :] = acc[rows, :] + more
        return carry

    acc[...] = jnp.zeros_like(acc)
    lax.fori_loop(0, win.shape[1] // tile, forward, 0)

    def round_out(i, carry):
        at = pl.ds(pl.multiple_of(i * cap, cap), cap)
        eout[at, :] = acc[at, :].astype(bf16)
        return carry

    lax.fori_loop(0, rows_all // cap, round_out, 0)

    def back(k):
        there = lax.rem(me + k, 8)
        return pltpu.make_async_remote_copy(
            src_ref=eout.at[pl.ds(pl.multiple_of(there * cap, cap), cap)],
            dst_ref=ret.at[me],
            send_sem=e_send.at[k],
            recv_sem=e_recv.at[k],
            **to(dp, there),
        )

    for k in range(1, 8):
        back(k).start()
    back_own = pltpu.make_async_copy(eout.at[own_rows], ret.at[me], loc_sem.at[0])
    back_own.start()

    def near_step(q, carry):
        for c in range(2):
            for copy in first_hop(q, c):
                copy.wait_recv()
        for copy in second_hop(q):
            copy.start()
        raw_arrived(1, q)
        raw_arrived(3, q)
        grads(1, chip_rows(q))
        grads(3, chip_rows(q))
        return carry

    lax.fori_loop(0, SIDE, near_step, 0)

    for k in range(1, 8):
        back(k).wait_recv()
    back_own.wait()
    for what in range(3):
        raw_far(what).wait_send()
    picked = jnp.zeros((toks, width), f32)
    for p in range(SIDE):
        for b in range(toks // LANES):
            at = slice(b * LANES, (b + 1) * LANES)
            for h in range(2):
                first = float((2 * p + h) * cap)
                slots = lax.broadcasted_iota(jnp.int32, (LANES, cap), 1).astype(f32) + first
                hit = (slots == code_cols[at, :]).astype(f32).astype(bf16)
                raw[p, at, h * cap : (h + 1) * cap] = hit
        rows = ret[2 * p : 2 * p + 2].reshape(chunk, width)
        picked = picked + jnp.dot(raw[p], rows, preferred_element_type=f32)
    for c in range(lane_blocks):
        cols = slice(c * LANES, (c + 1) * LANES)
        combined[:, cols] = (gate_cols[...] * picked[:, cols]).astype(bf16)

    def far_step(q, carry):
        for copy in second_hop(q):
            copy.wait_recv()
        raw_arrived(2, q)
        grads(2, chip_rows(q))
        return carry

    lax.fori_loop(0, SIDE, far_step, 0)

    for p, s in enumerate(gram_sums((g_in, g_out), part)):
        gz_out[p : p + 1, :] = jnp.sum(s, axis=0, keepdims=True)
    sums_z = []
    for i in range(1, SIDE):
        copy = pltpu.make_async_remote_copy(
            src_ref=gz_out,
            dst_ref=gz_got.at[SIDE - i],
            send_sem=gz_send.at[SIDE - i],
            recv_sem=gz_recv.at[SIDE - i],
            **to(at_zy(i, 0), me),
        )
        copy.start()
        sums_z.append(copy)
    total = [gz_out[p : p + 1, :] for p in range(len(PAIRS))]
    for copy in sums_z:
        copy.wait_recv()
    for i in range(1, SIDE):
        for p, (a, b) in enumerate(PAIRS):
            q = SLOT[tuple(sorted(((a + i) % SIDE, (b + i) % SIDE)))]
            total[q] = total[q] + gz_got[i, p : p + 1, :]
    total = [jnp.sum(t, axis=1, keepdims=True) for t in total]
    w = tree_weights(lambda a, b: total[SLOT[(a, b)]])

    rows_out = seg_out.shape[0]
    rows_in = seg_in.shape[0]

    def send_out(j):
        k = (SIDE - j) % SIDE
        return [
            pltpu.make_async_remote_copy(
                src_ref=src.at[j],
                dst_ref=dst.at[k],
                send_sem=yo_send.at[h, k],
                recv_sem=yo_recv.at[h, k],
                **to(at_zy(0, j), me),
            )
            for h, (src, dst) in enumerate(((q_out, rq_out), (f_out, rf_out)))
        ]

    def send_in(i, j):
        n = i * SIDE + j
        k = (SIDE - j) % SIDE
        m = lax.rem(SIDE - i, SIDE) * SIDE + k
        return [
            pltpu.make_async_remote_copy(
                src_ref=src.at[n],
                dst_ref=dst.at[k, z],
                send_sem=yi_send.at[h, m],
                recv_sem=yi_recv.at[h, m],
                **to(at_zy(i, j), me),
            )
            for h, (src, dst) in enumerate(((q_in, rq_in), (f_in, rf_in)))
        ]

    for j in (1, 3, 2):
        rows = pl.ds(pl.multiple_of(lax.rem(y + j, SIDE) * rows_out, 8), rows_out)
        for c in range(lane_blocks):
            cols = slice(c * LANES, (c + 1) * LANES)
            v = w[0] * g_out[0, rows, cols] + w[1] * g_out[1, rows, cols]
            v = v + w[2] * g_out[2, rows, cols] + w[3] * g_out[3, rows, cols]
            q_out[j, :, cols], f_out[j, c : c + 1, :] = encode(v)
        for copy in send_out(j):
            copy.start()

    def mix_in(n, carry):
        cols = pl.ds(pl.multiple_of(n * LANES, LANES), LANES)
        for m in range(part // LANES):
            at = slice(m * LANES, (m + 1) * LANES)
            v = w[0] * g_in[0, at, cols] + w[1] * g_in[1, at, cols]
            v = v + w[2] * g_in[2, at, cols] + w[3] * g_in[3, at, cols]
            acc[cols, at] = v.T
        return carry

    lax.fori_loop(0, width // LANES, mix_in, 0)

    def block_rows(i, j):
        return pl.ds(pl.multiple_of(at_zy(i, j) * rows_in, 8), rows_in)

    for j in (1, 3, 2, 0):

        def code_in(i, carry, j=j):
            rows = block_rows(i, j)
            for c in range(lane_blocks):
                cols = slice(c * LANES, (c + 1) * LANES)
                codes, factor = encode(acc[rows, cols])
                q_in[i * SIDE + j, :, cols] = codes
                f_in[i * SIDE + j, c : c + 1, :] = factor
            for copy in send_in(i, j):
                copy.start()
            return carry

        lax.fori_loop(0 if j else 1, SIDE, code_in, 0)

    g_in[0, pl.ds(pl.multiple_of(z * rows_in, 8), rows_in), :] = acc[block_rows(0, 0), :]
    base = y * rows_out

    def mix_own(n, carry):
        rows = pl.ds(pl.multiple_of(base + n * 16, 16), 16)
        v = w[0] * g_out[0, rows, :] + w[1] * g_out[1, rows, :]
        v = v + w[2] * g_out[2, rows, :] + w[3] * g_out[3, rows, :]
        g_out[0, pl.ds(pl.multiple_of(n * 16, 16), 16), :] = v
        return carry

    lax.fori_loop(0, rows_out // 16, mix_own, 0)

    for k in (0, 3, 1, 2):
        j = (SIDE - k) % SIDE

        def decode_in(i, carry, j=j, k=k):
            for copy in send_in(i, j):
                copy.wait_recv()
            there = lax.rem(z + SIDE - i, SIDE)
            rows = pl.ds(pl.multiple_of(there * rows_in, 8), rows_in)
            for c in range(lane_blocks):
                cols = slice(c * LANES, (c + 1) * LANES)
                codes = rq_in[k, there, :, cols].astype(jnp.int32).astype(f32)
                g_in[k, rows, cols] = codes * rf_in[k, there, c : c + 1, :]
            return carry

        if k:
            for copy in send_out(j):
                copy.wait_recv()
            for c in range(lane_blocks):
                cols = slice(c * LANES, (c + 1) * LANES)
                codes = rq_out[k, :, cols].astype(jnp.int32).astype(f32)
                g_out[k, :rows_out, cols] = codes * rf_out[k, c : c + 1, :]
        lax.fori_loop(0 if k else 1, SIDE, decode_in, 0)

    for p, s in enumerate(gram_sums((g_in, g_out), rows_out)):
        gy_out[p : p + 1, :] = jnp.sum(s, axis=0, keepdims=True)
    sums_y = []
    for i in range(SIDE):
        for j in range(SIDE):
            if i or j:
                k = (SIDE - i) % SIDE * SIDE + (SIDE - j) % SIDE
                copy = pltpu.make_async_remote_copy(
                    src_ref=gy_out,
                    dst_ref=gy_got.at[k],
                    send_sem=gy_send.at[k],
                    recv_sem=gy_recv.at[k],
                    **to(at_zy(i, j), me),
                )
                copy.start()
                sums_y.append(copy)
    total = [gy_out[p : p + 1, :] for p in range(len(PAIRS))]
    for copy in sums_y:
        copy.wait_recv()
    for j in range(SIDE):
        for i in range(SIDE):
            if i or j:
                for p, (a, b) in enumerate(PAIRS):
                    q = SLOT[tuple(sorted(((a + j) % SIDE, (b + j) % SIDE)))]
                    total[q] = total[q] + gy_got[i * SIDE + j, p : p + 1, :]
    total = [jnp.sum(t, axis=1, keepdims=True) for t in total]
    v = tree_weights(lambda a, b: total[SLOT[(a, b)]])
    for i in range(SIDE):
        at = slice(i * rows_in, (i + 1) * rows_in)
        seg_in[:, i * part : (i + 1) * part] = (v[0] * g_in[0, at, :] + v[1] * g_in[1, at, :]) + (
            v[2] * g_in[2, at, :] + v[3] * g_in[3, at, :]
        )
        seg_out[at, :] = (v[0] * g_out[0, at, :] + v[1] * g_out[1, at, :]) + (
            v[2] * g_out[2, at, :] + v[3] * g_out[3, at, :]
        )

    def drain(q, carry):
        for copy in first_hop(q, 0) + first_hop(q, 1) + second_hop(q):
            copy.wait_send()
        return carry

    lax.fori_loop(0, SIDE, drain, 0)

    for slot in range(1, SIDE):
        for copy in raw_dispatch(slot, 0, 1):
            copy.wait_send()

        def drain_raw(q, carry, slot=slot):
            for copy in raw_dispatch(slot, q, 0) + raw_dispatch(slot, q, 1):
                copy.wait_send()
            return carry

        lax.fori_loop(1, SIDE, drain_raw, 0)
    for what in range(3):
        for way in range(2):
            raw_hop(what, way).wait_send()
    for k in range(1, 8):
        back(k).wait_send()
    for j in range(SIDE):

        def drain_in(i, carry, j=j):
            for copy in send_in(i, j):
                copy.wait_send()
            return carry

        lax.fori_loop(0 if j else 1, SIDE, drain_in, 0)
        if j:
            for copy in send_out(j):
                copy.wait_send()
    for copy in sums_z + sums_y:
        copy.wait_send()


def expert_step(assigned, gate, tokens, cotangent, w_in, w_out):
    f32 = jnp.float32
    bf16 = jnp.bfloat16
    i16 = jnp.int16
    experts = 8
    toks, width = tokens.shape
    cap = 2 * toks // experts
    rows = experts * cap
    side = SIDE
    part = w_in.shape[1] // side
    any_space = pl.BlockSpec(memory_space=pl.ANY)
    vmem = pl.BlockSpec(memory_space=pltpu.VMEM)
    rows_in = width // (side * side)
    rows_out = part // side
    dma = pltpu.SemaphoreType.DMA
    return pl.pallas_call(
        kernel,
        out_shape=(
            jax.ShapeDtypeStruct((toks, width), bf16),
            jax.ShapeDtypeStruct((rows_in, side * part), f32),
            jax.ShapeDtypeStruct((rows_out, width), f32),
        ),
        in_specs=[vmem, vmem, vmem, vmem, any_space, any_space],
        out_specs=(vmem, vmem, vmem),
        scratch_shapes=[
            pltpu.VMEM((side, rows, width), bf16),
            pltpu.VMEM((side, rows, width), bf16),
            pltpu.VMEM(w_in.shape, bf16),
            pltpu.VMEM(w_out.shape, bf16),
            pltpu.VMEM((part, width), bf16),
            pltpu.VMEM((side, part, width), f32),
            pltpu.VMEM((side, part, width), f32),
            pltpu.VMEM((part, 2 * cap), bf16),
            pltpu.VMEM((part, 2 * cap), bf16),
            pltpu.VMEM((side, 2 * cap, width), bf16),
            pltpu.VMEM((side, 2 * cap, width), bf16),
            pltpu.VMEM((toks, width), bf16),
            pltpu.VMEM((2 * (side - 1), toks, width - SPLIT), bf16),
            pltpu.VMEM((8, toks), f32),
            pltpu.VMEM((side - 1, 8, toks), f32),
            pltpu.VMEM((toks, LANES), f32),
            pltpu.VMEM((toks, LANES), f32),
            pltpu.VMEM((rows, width), bf16),
            pltpu.VMEM((experts, cap, width), bf16),
            pltpu.VMEM((rows, width), f32),
            pltpu.VMEM((side * side, rows_in, part), i16),
            pltpu.VMEM((side, rows_out, width), i16),
            pltpu.VMEM((side, side, rows_in, part), i16),
            pltpu.VMEM((side, rows_out, width), i16),
            pltpu.VMEM((side * side, 8, LANES), f32),
            pltpu.VMEM((side, 8, LANES), f32),
            pltpu.VMEM((side, side, 8, LANES), f32),
            pltpu.VMEM((side, 8, LANES), f32),
            pltpu.VMEM((16, LANES), f32),
            pltpu.VMEM((side, 16, LANES), f32),
            pltpu.VMEM((16, LANES), f32),
            pltpu.VMEM((side * side, 16, LANES), f32),
            dma((2,)),
            dma((1,)),
            dma((2, 8)),
            dma((2, 8)),
            dma((2, 3)),
            dma((2, 3)),
            dma((3,)),
            dma((3,)),
            dma((side - 1, 2, 8)),
            dma((side - 1, 2, 8)),
            dma((2, 2, 8)),
            dma((2, 2, 8)),
            dma((2, side)),
            dma((2, side)),
            dma((8,)),
            dma((8,)),
            dma((side,)),
            dma((side,)),
            dma((2, side)),
            dma((2, side)),
            dma((2, side * side)),
            dma((2, side * side)),
            dma((side * side,)),
            dma((side * side,)),
        ],
        compiler_params=pltpu.CompilerParams(
            collective_id=0, has_side_effects=True, vmem_limit_bytes=67_000_000
        ),
        name="expert_step",
    )(assigned, gate, tokens, cotangent, w_in, w_out)


def body(
    tokens,
    assigned,
    gate_prob,
    cotangent,
    weight_in,
    weight_out,
    moment_in,
    moment_out,
    second_in,
    second_out,
):
    f32 = jnp.float32
    replicas = lax.axis_size("dp")
    self_index = lax.axis_index("dp")
    toks, width = tokens.shape
    hidden_width = weight_in.shape[2]
    w_first = weight_in[0]
    w_second = weight_out[0]
    combined, seg_first, seg_second = expert_step(
        assigned.reshape(1, toks), gate_prob.reshape(1, toks), tokens, cotangent, w_first, w_second
    )
    rows_first = width // replicas
    rows_second = hidden_width // replicas
    own_first = lax.dynamic_slice_in_dim(w_first, self_index * rows_first, rows_first, 0).astype(
        f32
    )
    own_second = lax.dynamic_slice_in_dim(
        w_second, self_index * rows_second, rows_second, 0
    ).astype(f32)
    new_w_first, new_m_first, new_v_first = adam_update(
        seg_first, own_first, moment_in[0], second_in[0]
    )
    new_w_second, new_m_second, new_v_second = adam_update(
        seg_second, own_second, moment_out[0], second_out[0]
    )
    return (
        combined,
        new_w_first[None],
        new_w_second[None],
        new_m_first[None],
        new_m_second[None],
        new_v_first[None],
        new_v_second[None],
    )


def solution(mesh):
    return jax.shard_map(
        body,
        mesh=mesh,
        in_specs=(
            P(("dp", "expert"), None),
            P(("dp", "expert"), None),
            P(("dp", "expert"), None),
            P(("dp", "expert"), None),
            P("expert", None, None),
            P("expert", None, None),
            P("expert", "dp", None),
            P("expert", "dp", None),
            P("expert", "dp", None),
            P("expert", "dp", None),
        ),
        out_specs=(
            P(("dp", "expert"), None),
            P("expert", "dp", None),
            P("expert", "dp", None),
            P("expert", "dp", None),
            P("expert", "dp", None),
            P("expert", "dp", None),
            P("expert", "dp", None),
        ),
        check_vma=False,
    )
```

```python
import jax
import jax.numpy as jnp
from jax import lax
from jax.experimental import pallas as pl
from jax.experimental.pallas import tpu as pltpu
from jax.sharding import PartitionSpec as P

eps_adasum = 1e-06
SIDE = 4
LANES = 128
SPLIT = 512
MESH = pl.DeviceIdType.MESH
PAIRS = [(a, b) for a in range(SIDE) for b in range(a, SIDE)]
SLOT = {pair: k for k, pair in enumerate(PAIRS)}


def adam_update(grad, weight, moment, second):
    new_moment = 0.9 * moment + 0.1 * grad
    new_second = 0.999 * second + 0.001 * grad * grad
    corr_one = 1.0 - 0.9**10.0
    corr_two = 1.0 - 0.999**10.0
    update = new_moment / corr_one / (jnp.sqrt(new_second / corr_two) + 1e-08)
    return (weight - 0.001 * update, new_moment, new_second)


def dot_nt(left, right):
    return lax.dot_general(
        left, right, (((1,), (1,)), ((), ())), preferred_element_type=jnp.float32
    )


def pair_coefs(ab, aa, bb):
    return 1.0 - ab / (2.0 * (aa + eps_adasum)), 1.0 - ab / (2.0 * (bb + eps_adasum))


def tree_weights(g):
    w0, w2 = pair_coefs(g(0, 2), g(0, 0), g(2, 2))
    w1, w3 = pair_coefs(g(1, 3), g(1, 1), g(3, 3))
    aa = w0 * w0 * g(0, 0) + 2.0 * w0 * w2 * g(0, 2) + w2 * w2 * g(2, 2)
    bb = w1 * w1 * g(1, 1) + 2.0 * w1 * w3 * g(1, 3) + w3 * w3 * g(3, 3)
    ab = w0 * (w1 * g(0, 1) + w3 * g(0, 3)) + w2 * (w1 * g(1, 2) + w3 * g(2, 3))
    u, v = pair_coefs(ab, aa, bb)
    return [u * w0, v * w1, u * w2, v * w3]


def gelu_parts(v):
    root = 0.7978845608028654
    square = v * v
    t = jnp.tanh(root * (v + 0.044715 * (square * v)))
    cdf = 0.5 * (1.0 + t)
    slope = cdf + v * (0.5 * (1.0 - t * t)) * (root * (1.0 + 0.134145 * square))
    return v * cdf, slope


def gelu_only(v):
    root = 0.7978845608028654
    return v * (0.5 * (1.0 + jnp.tanh(root * (v + 0.044715 * (v * v * v)))))


def columns_of(row):
    return jnp.broadcast_to(row, (LANES, LANES)).T


def encode(v):
    most = jnp.maximum(jnp.max(jnp.abs(v), axis=0, keepdims=True), 1e-30)
    codes = jnp.round(v * (32767.0 / most)).astype(jnp.int32).astype(jnp.int16)
    return codes, most * (1.0 / 32767.0)


def gram_sums(refs, rows):
    width = refs[0].shape[2]

    def step(i, sums):
        sums = list(sums)
        at = pl.ds(pl.multiple_of(i * 8, 8), 8)
        for ref in refs:
            for c in range(width // LANES):
                cols = slice(c * LANES, (c + 1) * LANES)
                v = [ref[k, at, cols] for k in range(SIDE)]
                for p, (a, b) in enumerate(PAIRS):
                    sums[p] = sums[p] + v[a] * v[b]
        return tuple(sums)

    zero = jnp.zeros((8, LANES), jnp.float32)
    return lax.fori_loop(0, rows // 8, step, (zero,) * len(PAIRS))


def kernel(
    assigned,
    gate,
    tokens,
    cotangent,
    win_hbm,
    wout_hbm,
    combined,
    seg_in,
    seg_out,
    tok,
    ups,
    win,
    wout,
    w1t,
    g_in,
    g_out,
    ht,
    hgt,
    sent_t,
    sent_u,
    scaled,
    raw,
    place_own,
    places,
    code_cols,
    gate_cols,
    eout,
    ret,
    acc,
    q_in,
    q_out,
    rq_in,
    rq_out,
    f_in,
    f_out,
    rf_in,
    rf_out,
    gz_out,
    gz_got,
    gy_out,
    gy_got,
    w_sem,
    loc_sem,
    d_send,
    d_recv,
    rz_send,
    rz_recv,
    rfar_send,
    rfar_recv,
    b_send,
    b_recv,
    zf_send,
    zf_recv,
    far_send,
    far_recv,
    e_send,
    e_recv,
    gz_send,
    gz_recv,
    yo_send,
    yo_recv,
    yi_send,
    yi_recv,
    gy_send,
    gy_recv,
):
    f32 = jnp.float32
    bf16 = jnp.bfloat16
    dp = lax.axis_index("dp")
    me = lax.axis_index("expert")
    z, y = lax.div(dp, SIDE), lax.rem(dp, SIDE)
    x, core = lax.div(me, 2), lax.rem(me, 2)
    cap = ret.shape[1]
    chunk = 2 * cap
    part = w1t.shape[0]
    toks, width = tokens.shape
    lane_blocks = width // LANES
    own_rows = pl.ds(pl.multiple_of(me * cap, cap), cap)

    def at_zy(i, j):
        return lax.rem(z + i, SIDE) * SIDE + lax.rem(y + j, SIDE)

    def to(dp_index, expert_index):
        return {"device_id": (dp_index, expert_index), "device_id_type": MESH}

    load_win = pltpu.make_async_copy(win_hbm, win, w_sem.at[0])
    load_wout = pltpu.make_async_copy(wout_hbm, wout, w_sem.at[1])
    load_win.start()
    load_wout.start()

    barrier = pltpu.get_barrier_semaphore()
    for k in range(1, 8):
        pl.semaphore_signal(barrier, inc=1, **to(dp, lax.rem(me + k, 8)))
    for i in range(SIDE):
        for j in range(SIDE):
            if i or j:
                pl.semaphore_signal(barrier, inc=1, **to(at_zy(i, j), me))

    named = assigned[...]
    hot = (lax.broadcasted_iota(jnp.int32, (16, toks), 0) == named).astype(f32)
    earlier = (
        lax.broadcasted_iota(jnp.int32, (toks, toks), 0)
        < lax.broadcasted_iota(jnp.int32, (toks, toks), 1)
    ).astype(f32)
    rank = jnp.dot(hot.astype(bf16), earlier.astype(bf16), preferred_element_type=f32)
    place = (named * cap).astype(f32) + jnp.sum(rank * hot, axis=0, keepdims=True)
    place_own[...] = jnp.broadcast_to(place, place_own.shape)
    for b in range(toks // LANES):
        at = slice(b * LANES, (b + 1) * LANES)
        code_cols[at, :] = columns_of(place[:, at])
        column = columns_of(gate[:, at])
        gate_cols[at, :] = column
        for c in range(lane_blocks):
            cols = slice(c * LANES, (c + 1) * LANES)
            scaled[at, cols] = (column * cotangent[at, cols].astype(f32)).astype(bf16)

    def chip_at(q):
        return lax.rem(x + (q ^ (q >> 1)), SIDE)

    def chip_rows(q):
        return pl.ds(pl.multiple_of(lax.rem(x + SIDE - (q ^ (q >> 1)), SIDE) * chunk, chunk), chunk)

    def table_of(q, places_row):
        base = (chip_at(q) * chunk).astype(f32)
        slots = lax.broadcasted_iota(jnp.int32, (chunk, toks), 0).astype(f32) + base
        return (slots == places_row).astype(f32).astype(bf16)

    def place_rows(q):
        table = table_of(q, place)
        sent_t[q] = jnp.dot(table, tokens[...], preferred_element_type=f32).astype(bf16)
        sent_u[q] = jnp.dot(table, scaled[...], preferred_element_type=f32).astype(bf16)

    def dispatch(q, c):
        there = lax.rem(core + c, 2)
        return [
            pltpu.make_async_remote_copy(
                src_ref=src.at[q, pl.ds(pl.multiple_of(there * cap, cap), cap)],
                dst_ref=dst.at[0, own_rows],
                send_sem=d_send.at[h, 2 * q + c],
                recv_sem=d_recv.at[h, 2 * q + c],
                **to(dp, chip_at(q) * 2 + there),
            )
            for h, (src, dst) in enumerate(((sent_t, tok), (sent_u, ups)))
        ]

    def along_z(buf, slot, to_slot, rows, step, send, recv):
        return pltpu.make_async_remote_copy(
            src_ref=buf.at[slot, rows, :SPLIT],
            dst_ref=buf.at[to_slot, rows, :SPLIT],
            send_sem=send,
            recv_sem=recv,
            **to(at_zy(step, 0), me),
        )

    def first_hop(q, c):
        source = lax.rem(x + SIDE - (q ^ (q >> 1)), SIDE) * 2 + lax.rem(core + c, 2)
        rows = pl.ds(pl.multiple_of(source * cap, cap), cap)
        n = 2 * q + c
        copies = []
        for h, buf in enumerate((tok, ups)):
            copies.append(along_z(buf, 0, 3, rows, 1, zf_send.at[0, h, n], zf_recv.at[0, h, n]))
            copies.append(along_z(buf, 0, 1, rows, 3, zf_send.at[1, h, n], zf_recv.at[1, h, n]))
        return copies

    def second_hop(q):
        rows = chip_rows(q)
        return [
            along_z(tok, 3, 2, rows, 1, far_send.at[0, q], far_recv.at[0, q]),
            along_z(ups, 1, 2, rows, 3, far_send.at[1, q], far_recv.at[1, q]),
        ]

    def raw_hop(what, way):
        src, dst, base = (
            (tokens.at[:, SPLIT:], raw, 0),
            (scaled.at[:, SPLIT:], raw, 3),
            (place_own, places, 0),
        )[what]
        return pltpu.make_async_remote_copy(
            src_ref=src,
            dst_ref=dst.at[base + (0 if way else 2)],
            send_sem=rz_send.at[way, what],
            recv_sem=rz_recv.at[way, what],
            **to(at_zy(3 if way else 1, 0), me),
        )

    def raw_far(what):
        buf, source, there = ((raw, 2, 1), (raw, 3, 4), (places, 2, 1))[what]
        return pltpu.make_async_remote_copy(
            src_ref=buf.at[source],
            dst_ref=buf.at[there],
            send_sem=rfar_send.at[what],
            recv_sem=rfar_recv.at[what],
            **to(at_zy(3 if what == 1 else 1, 0), me),
        )

    def raw_dispatch(slot, q, c):
        there = lax.rem(core + c, 2)
        cols = slice((slot - 1) * (width - SPLIT), slot * (width - SPLIT))
        return [
            pltpu.make_async_remote_copy(
                src_ref=src.at[q, pl.ds(pl.multiple_of(there * cap, cap), cap), cols],
                dst_ref=dst.at[slot, own_rows, SPLIT:],
                send_sem=b_send.at[slot - 1, h, 2 * q + c],
                recv_sem=b_recv.at[slot - 1, h, 2 * q + c],
                **to(dp, chip_at(q) * 2 + there),
            )
            for h, (src, dst) in enumerate(((sent_t, tok), (sent_u, ups)))
        ]

    pl.semaphore_wait(barrier, 7 + SIDE * SIDE - 1)
    for what in (0, 1, 2):
        for way in range(2):
            raw_hop(what, way).start()
    place_rows(0)
    half_rows = pl.ds(pl.multiple_of(core * cap, cap), cap)
    tok[0, own_rows, :] = sent_t[0, half_rows, :]
    ups[0, own_rows, :] = sent_u[0, half_rows, :]
    for copy in dispatch(0, 1) + first_hop(0, 0):
        copy.start()

    def place_step(q, carry):
        place_rows(q)
        for copy in dispatch(q, 0) + dispatch(q, 1):
            copy.start()
        return carry

    lax.fori_loop(1, SIDE, place_step, 0)
    for copy in dispatch(0, 1):
        copy.wait_recv()
    for copy in first_hop(0, 1):
        copy.start()

    load_win.wait()

    def turn(n, carry):
        at = pl.ds(pl.multiple_of(n * LANES, LANES), LANES)
        cols = pl.ds(pl.multiple_of(z * part + n * LANES, LANES), LANES)
        for c in range(lane_blocks):
            rows = slice(c * LANES, (c + 1) * LANES)
            w1t[at, rows] = win[rows, cols].astype(f32).T.astype(bf16)
        return carry

    lax.fori_loop(0, part // LANES, turn, 0)

    def clear(i, carry):
        at = pl.ds(pl.multiple_of(i * 16, 16), 16)
        for k in range(SIDE):
            g_in[k, at, :] = jnp.zeros((16, width), f32)
            g_out[k, at, :] = jnp.zeros((16, width), f32)
        return carry

    lax.fori_loop(0, part // 16, clear, 0)
    load_wout.wait()
    w2_rows = pl.ds(pl.multiple_of(z * part, part), part)

    def grads(slot, rows):
        t = tok[slot, rows, :]
        u = ups[slot, rows, :]
        act, slope = gelu_parts(dot_nt(w1t[...], t))
        ht[...] = act.astype(bf16)
        hgt[...] = (slope * dot_nt(wout[w2_rows, :], u)).astype(bf16)
        g_out[slot] = g_out[slot] + jnp.dot(ht[...], u, preferred_element_type=f32)
        g_in[slot] = g_in[slot] + jnp.dot(hgt[...], t, preferred_element_type=f32)

    tile = part

    def forward(rows):
        acc[rows, :] = jnp.zeros((chunk, width), f32)

        def step(n, carry):
            cols = pl.ds(pl.multiple_of(n * tile, tile), tile)
            pre = jnp.dot(tok[0, rows, :], win[:, cols], preferred_element_type=f32)
            hid = gelu_only(pre).astype(bf16)
            acc[rows, :] = acc[rows, :] + jnp.dot(hid, wout[cols, :], preferred_element_type=f32)
            return carry

        lax.fori_loop(0, win.shape[1] // tile, step, 0)
        eout[rows, :] = acc[rows, :].astype(bf16)

    def back(q, c):
        there = lax.rem(x + SIDE - (q ^ (q >> 1)), SIDE) * 2 + lax.rem(core + c, 2)
        return pltpu.make_async_remote_copy(
            src_ref=eout.at[pl.ds(pl.multiple_of(there * cap, cap), cap)],
            dst_ref=ret.at[me],
            send_sem=e_send.at[2 * q + c],
            recv_sem=e_recv.at[2 * q + c],
            **to(dp, there),
        )

    for what in range(3):
        for way in range(2):
            raw_hop(what, way).wait_recv()
    for what in range(3):
        raw_far(what).start()

    def own_step(q, carry):
        for c in range(2):
            for copy in dispatch(q, c):
                copy.wait_recv()
            for copy in first_hop(q, c):
                copy.start()
        grads(0, chip_rows(q - 1))
        forward(chip_rows(q - 1))
        return carry

    lax.fori_loop(1, SIDE, own_step, 0)

    def place_raw(slot, q):
        cols = slice((slot - 1) * (width - SPLIT), slot * (width - SPLIT))
        table = table_of(q, places[slot - 1, 0:1, :])
        for sent, base in ((sent_t, 0), (sent_u, 3)):
            rows = jnp.dot(table, raw[base + slot - 1], preferred_element_type=f32)
            sent[q, :, cols] = rows.astype(bf16)

    for slot in (1, 3, 2):
        if slot == 2:
            for what in range(3):
                raw_far(what).wait_recv()
        cols = slice((slot - 1) * (width - SPLIT), slot * (width - SPLIT))
        if slot == 1:
            for copy in dispatch(0, 1):
                copy.wait_send()
        place_raw(slot, 0)
        tok[slot, own_rows, SPLIT:] = sent_t[0, half_rows, cols]
        ups[slot, own_rows, SPLIT:] = sent_u[0, half_rows, cols]
        for copy in raw_dispatch(slot, 0, 1):
            copy.start()

        def raw_step(q, carry, slot=slot):
            if slot == 1:
                for copy in dispatch(q, 0) + dispatch(q, 1):
                    copy.wait_send()
            place_raw(slot, q)
            for copy in raw_dispatch(slot, q, 0) + raw_dispatch(slot, q, 1):
                copy.start()
            return carry

        lax.fori_loop(1, SIDE, raw_step, 0)

    grads(0, chip_rows(SIDE - 1))
    forward(chip_rows(SIDE - 1))

    def raw_arrived(slot, q):
        @pl.when(q > 0)
        def _():
            for copy in raw_dispatch(slot, q, 0):
                copy.wait_recv()

        for copy in raw_dispatch(slot, q, 1):
            copy.wait_recv()

    for q in range(SIDE):
        for c in range(2):
            if q or c:
                back(q, c).start()
    back_own = pltpu.make_async_copy(eout.at[own_rows], ret.at[me], loc_sem.at[0])
    back_own.start()

    def near_step(q, carry):
        for c in range(2):
            for copy in first_hop(q, c):
                copy.wait_recv()
        for copy in second_hop(q):
            copy.start()
        raw_arrived(1, q)
        raw_arrived(3, q)
        grads(1, chip_rows(q))
        grads(3, chip_rows(q))
        return carry

    lax.fori_loop(0, SIDE, near_step, 0)

    def far_step(q, carry):
        for copy in second_hop(q):
            copy.wait_recv()
        raw_arrived(2, q)
        grads(2, chip_rows(q))
        return carry

    lax.fori_loop(0, SIDE, far_step, 0)

    for p, s in enumerate(gram_sums((g_in, g_out), part)):
        gz_out[p : p + 1, :] = jnp.sum(s, axis=0, keepdims=True)
    sums_z = []
    for i in range(1, SIDE):
        copy = pltpu.make_async_remote_copy(
            src_ref=gz_out,
            dst_ref=gz_got.at[SIDE - i],
            send_sem=gz_send.at[SIDE - i],
            recv_sem=gz_recv.at[SIDE - i],
            **to(at_zy(i, 0), me),
        )
        copy.start()
        sums_z.append(copy)
    total = [gz_out[p : p + 1, :] for p in range(len(PAIRS))]
    for copy in sums_z:
        copy.wait_recv()
    for i in range(1, SIDE):
        for p, (a, b) in enumerate(PAIRS):
            q = SLOT[tuple(sorted(((a + i) % SIDE, (b + i) % SIDE)))]
            total[q] = total[q] + gz_got[i, p : p + 1, :]
    total = [jnp.sum(t, axis=1, keepdims=True) for t in total]
    w = tree_weights(lambda a, b: total[SLOT[(a, b)]])

    rows_out = seg_out.shape[0]
    rows_in = seg_in.shape[0]

    def send_out(j):
        k = (SIDE - j) % SIDE
        return [
            pltpu.make_async_remote_copy(
                src_ref=src.at[j],
                dst_ref=dst.at[k],
                send_sem=yo_send.at[h, k],
                recv_sem=yo_recv.at[h, k],
                **to(at_zy(0, j), me),
            )
            for h, (src, dst) in enumerate(((q_out, rq_out), (f_out, rf_out)))
        ]

    def send_in(i, j):
        n = i * SIDE + j
        k = (SIDE - j) % SIDE
        m = lax.rem(SIDE - i, SIDE) * SIDE + k
        return [
            pltpu.make_async_remote_copy(
                src_ref=src.at[n],
                dst_ref=dst.at[k, z],
                send_sem=yi_send.at[h, m],
                recv_sem=yi_recv.at[h, m],
                **to(at_zy(i, j), me),
            )
            for h, (src, dst) in enumerate(((q_in, rq_in), (f_in, rf_in)))
        ]

    for j in (1, 3, 2):
        rows = pl.ds(pl.multiple_of(lax.rem(y + j, SIDE) * rows_out, 8), rows_out)
        for c in range(lane_blocks):
            cols = slice(c * LANES, (c + 1) * LANES)
            v = w[0] * g_out[0, rows, cols] + w[1] * g_out[1, rows, cols]
            v = v + w[2] * g_out[2, rows, cols] + w[3] * g_out[3, rows, cols]
            q_out[j, :, cols], f_out[j, c : c + 1, :] = encode(v)
        for copy in send_out(j):
            copy.start()

    def mix_in(n, carry):
        cols = pl.ds(pl.multiple_of(n * LANES, LANES), LANES)
        for m in range(part // LANES):
            at = slice(m * LANES, (m + 1) * LANES)
            v = w[0] * g_in[0, at, cols] + w[1] * g_in[1, at, cols]
            v = v + w[2] * g_in[2, at, cols] + w[3] * g_in[3, at, cols]
            acc[cols, at] = v.T
        return carry

    lax.fori_loop(0, width // LANES, mix_in, 0)

    def block_rows(i, j):
        return pl.ds(pl.multiple_of(at_zy(i, j) * rows_in, 8), rows_in)

    for j in (1, 3, 2, 0):

        def code_in(i, carry, j=j):
            rows = block_rows(i, j)
            for c in range(lane_blocks):
                cols = slice(c * LANES, (c + 1) * LANES)
                codes, factor = encode(acc[rows, cols])
                q_in[i * SIDE + j, :, cols] = codes
                f_in[i * SIDE + j, c : c + 1, :] = factor
            for copy in send_in(i, j):
                copy.start()
            return carry

        lax.fori_loop(0 if j else 1, SIDE, code_in, 0)

    g_in[0, pl.ds(pl.multiple_of(z * rows_in, 8), rows_in), :] = acc[block_rows(0, 0), :]
    base = y * rows_out

    def mix_own(n, carry):
        rows = pl.ds(pl.multiple_of(base + n * 16, 16), 16)
        v = w[0] * g_out[0, rows, :] + w[1] * g_out[1, rows, :]
        v = v + w[2] * g_out[2, rows, :] + w[3] * g_out[3, rows, :]
        g_out[0, pl.ds(pl.multiple_of(n * 16, 16), 16), :] = v
        return carry

    lax.fori_loop(0, rows_out // 16, mix_own, 0)

    for q in range(SIDE):
        for c in range(2):
            if q or c:
                back(q, c).wait_recv()
    back_own.wait()
    for what in range(3):
        raw_far(what).wait_send()
    picked = jnp.zeros((toks, width), f32)
    for p in range(SIDE):
        for b in range(toks // LANES):
            at = slice(b * LANES, (b + 1) * LANES)
            for h in range(2):
                first = float((2 * p + h) * cap)
                slots = lax.broadcasted_iota(jnp.int32, (LANES, cap), 1).astype(f32) + first
                hit = (slots == code_cols[at, :]).astype(f32).astype(bf16)
                raw[p, at, h * cap : (h + 1) * cap] = hit
        rows = ret[2 * p : 2 * p + 2].reshape(chunk, width)
        picked = picked + jnp.dot(raw[p], rows, preferred_element_type=f32)
    for c in range(lane_blocks):
        cols = slice(c * LANES, (c + 1) * LANES)
        combined[:, cols] = (gate_cols[...] * picked[:, cols]).astype(bf16)

    for k in (0, 3, 1, 2):
        j = (SIDE - k) % SIDE

        def decode_in(i, carry, j=j, k=k):
            for copy in send_in(i, j):
                copy.wait_recv()
            there = lax.rem(z + SIDE - i, SIDE)
            rows = pl.ds(pl.multiple_of(there * rows_in, 8), rows_in)
            for c in range(lane_blocks):
                cols = slice(c * LANES, (c + 1) * LANES)
                codes = rq_in[k, there, :, cols].astype(jnp.int32).astype(f32)
                g_in[k, rows, cols] = codes * rf_in[k, there, c : c + 1, :]
            return carry

        if k:
            for copy in send_out(j):
                copy.wait_recv()
            for c in range(lane_blocks):
                cols = slice(c * LANES, (c + 1) * LANES)
                codes = rq_out[k, :, cols].astype(jnp.int32).astype(f32)
                g_out[k, :rows_out, cols] = codes * rf_out[k, c : c + 1, :]
        lax.fori_loop(0 if k else 1, SIDE, decode_in, 0)

    for p, s in enumerate(gram_sums((g_in, g_out), rows_out)):
        gy_out[p : p + 1, :] = jnp.sum(s, axis=0, keepdims=True)
    sums_y = []
    for i in range(SIDE):
        for j in range(SIDE):
            if i or j:
                k = (SIDE - i) % SIDE * SIDE + (SIDE - j) % SIDE
                copy = pltpu.make_async_remote_copy(
                    src_ref=gy_out,
                    dst_ref=gy_got.at[k],
                    send_sem=gy_send.at[k],
                    recv_sem=gy_recv.at[k],
                    **to(at_zy(i, j), me),
                )
                copy.start()
                sums_y.append(copy)
    total = [gy_out[p : p + 1, :] for p in range(len(PAIRS))]
    for copy in sums_y:
        copy.wait_recv()
    for j in range(SIDE):
        for i in range(SIDE):
            if i or j:
                for p, (a, b) in enumerate(PAIRS):
                    q = SLOT[tuple(sorted(((a + j) % SIDE, (b + j) % SIDE)))]
                    total[q] = total[q] + gy_got[i * SIDE + j, p : p + 1, :]
    total = [jnp.sum(t, axis=1, keepdims=True) for t in total]
    v = tree_weights(lambda a, b: total[SLOT[(a, b)]])
    for i in range(SIDE):
        at = slice(i * rows_in, (i + 1) * rows_in)
        seg_in[:, i * part : (i + 1) * part] = (v[0] * g_in[0, at, :] + v[1] * g_in[1, at, :]) + (
            v[2] * g_in[2, at, :] + v[3] * g_in[3, at, :]
        )
        seg_out[at, :] = (v[0] * g_out[0, at, :] + v[1] * g_out[1, at, :]) + (
            v[2] * g_out[2, at, :] + v[3] * g_out[3, at, :]
        )

    def drain(q, carry):
        for copy in first_hop(q, 0) + first_hop(q, 1) + second_hop(q):
            copy.wait_send()
        return carry

    lax.fori_loop(0, SIDE, drain, 0)

    for slot in range(1, SIDE):
        for copy in raw_dispatch(slot, 0, 1):
            copy.wait_send()

        def drain_raw(q, carry, slot=slot):
            for copy in raw_dispatch(slot, q, 0) + raw_dispatch(slot, q, 1):
                copy.wait_send()
            return carry

        lax.fori_loop(1, SIDE, drain_raw, 0)
    for what in range(3):
        for way in range(2):
            raw_hop(what, way).wait_send()
    for q in range(SIDE):
        for c in range(2):
            if q or c:
                back(q, c).wait_send()
    for j in range(SIDE):

        def drain_in(i, carry, j=j):
            for copy in send_in(i, j):
                copy.wait_send()
            return carry

        lax.fori_loop(0 if j else 1, SIDE, drain_in, 0)
        if j:
            for copy in send_out(j):
                copy.wait_send()
    for copy in sums_z + sums_y:
        copy.wait_send()


def expert_step(assigned, gate, tokens, cotangent, w_in, w_out):
    f32 = jnp.float32
    bf16 = jnp.bfloat16
    i16 = jnp.int16
    experts = 8
    toks, width = tokens.shape
    cap = 2 * toks // experts
    rows = experts * cap
    side = SIDE
    part = w_in.shape[1] // side
    any_space = pl.BlockSpec(memory_space=pl.ANY)
    vmem = pl.BlockSpec(memory_space=pltpu.VMEM)
    rows_in = width // (side * side)
    rows_out = part // side
    dma = pltpu.SemaphoreType.DMA
    return pl.pallas_call(
        kernel,
        out_shape=(
            jax.ShapeDtypeStruct((toks, width), bf16),
            jax.ShapeDtypeStruct((rows_in, side * part), f32),
            jax.ShapeDtypeStruct((rows_out, width), f32),
        ),
        in_specs=[vmem, vmem, vmem, vmem, any_space, any_space],
        out_specs=(vmem, vmem, vmem),
        scratch_shapes=[
            pltpu.VMEM((side, rows, width), bf16),
            pltpu.VMEM((side, rows, width), bf16),
            pltpu.VMEM(w_in.shape, bf16),
            pltpu.VMEM(w_out.shape, bf16),
            pltpu.VMEM((part, width), bf16),
            pltpu.VMEM((side, part, width), f32),
            pltpu.VMEM((side, part, width), f32),
            pltpu.VMEM((part, 2 * cap), bf16),
            pltpu.VMEM((part, 2 * cap), bf16),
            pltpu.VMEM((side, 2 * cap, width), bf16),
            pltpu.VMEM((side, 2 * cap, width), bf16),
            pltpu.VMEM((toks, width), bf16),
            pltpu.VMEM((2 * (side - 1), toks, width - SPLIT), bf16),
            pltpu.VMEM((8, toks), f32),
            pltpu.VMEM((side - 1, 8, toks), f32),
            pltpu.VMEM((toks, LANES), f32),
            pltpu.VMEM((toks, LANES), f32),
            pltpu.VMEM((rows, width), bf16),
            pltpu.VMEM((experts, cap, width), bf16),
            pltpu.VMEM((rows, width), f32),
            pltpu.VMEM((side * side, rows_in, part), i16),
            pltpu.VMEM((side, rows_out, width), i16),
            pltpu.VMEM((side, side, rows_in, part), i16),
            pltpu.VMEM((side, rows_out, width), i16),
            pltpu.VMEM((side * side, 8, LANES), f32),
            pltpu.VMEM((side, 8, LANES), f32),
            pltpu.VMEM((side, side, 8, LANES), f32),
            pltpu.VMEM((side, 8, LANES), f32),
            pltpu.VMEM((16, LANES), f32),
            pltpu.VMEM((side, 16, LANES), f32),
            pltpu.VMEM((16, LANES), f32),
            pltpu.VMEM((side * side, 16, LANES), f32),
            dma((2,)),
            dma((1,)),
            dma((2, 8)),
            dma((2, 8)),
            dma((2, 3)),
            dma((2, 3)),
            dma((3,)),
            dma((3,)),
            dma((side - 1, 2, 8)),
            dma((side - 1, 2, 8)),
            dma((2, 2, 8)),
            dma((2, 2, 8)),
            dma((2, side)),
            dma((2, side)),
            dma((8,)),
            dma((8,)),
            dma((side,)),
            dma((side,)),
            dma((2, side)),
            dma((2, side)),
            dma((2, side * side)),
            dma((2, side * side)),
            dma((side * side,)),
            dma((side * side,)),
        ],
        compiler_params=pltpu.CompilerParams(
            collective_id=0, has_side_effects=True, vmem_limit_bytes=67_000_000
        ),
        name="expert_step",
    )(assigned, gate, tokens, cotangent, w_in, w_out)


def body(
    tokens,
    assigned,
    gate_prob,
    cotangent,
    weight_in,
    weight_out,
    moment_in,
    moment_out,
    second_in,
    second_out,
):
    f32 = jnp.float32
    replicas = lax.axis_size("dp")
    self_index = lax.axis_index("dp")
    toks, width = tokens.shape
    hidden_width = weight_in.shape[2]
    w_first = weight_in[0]
    w_second = weight_out[0]
    combined, seg_first, seg_second = expert_step(
        assigned.reshape(1, toks), gate_prob.reshape(1, toks), tokens, cotangent, w_first, w_second
    )
    rows_first = width // replicas
    rows_second = hidden_width // replicas
    own_first = lax.dynamic_slice_in_dim(w_first, self_index * rows_first, rows_first, 0).astype(
        f32
    )
    own_second = lax.dynamic_slice_in_dim(
        w_second, self_index * rows_second, rows_second, 0
    ).astype(f32)
    new_w_first, new_m_first, new_v_first = adam_update(
        seg_first, own_first, moment_in[0], second_in[0]
    )
    new_w_second, new_m_second, new_v_second = adam_update(
        seg_second, own_second, moment_out[0], second_out[0]
    )
    return (
        combined,
        new_w_first[None],
        new_w_second[None],
        new_m_first[None],
        new_m_second[None],
        new_v_first[None],
        new_v_second[None],
    )


def solution(mesh):
    return jax.shard_map(
        body,
        mesh=mesh,
        in_specs=(
            P(("dp", "expert"), None),
            P(("dp", "expert"), None),
            P(("dp", "expert"), None),
            P(("dp", "expert"), None),
            P("expert", None, None),
            P("expert", None, None),
            P("expert", "dp", None),
            P("expert", "dp", None),
            P("expert", "dp", None),
            P("expert", "dp", None),
        ),
        out_specs=(
            P(("dp", "expert"), None),
            P("expert", "dp", None),
            P("expert", "dp", None),
            P("expert", "dp", None),
            P("expert", "dp", None),
            P("expert", "dp", None),
            P("expert", "dp", None),
        ),
        check_vma=False,
    )
```

```python
import jax
import jax.numpy as jnp
from jax import lax
from jax.experimental import pallas as pl
from jax.experimental.pallas import tpu as pltpu
from jax.sharding import PartitionSpec as P

eps_adasum = 1e-06
SIDE = 4
LANES = 128
PANELS = 3
MESH = pl.DeviceIdType.MESH
PAIRS = [(a, b) for a in range(SIDE) for b in range(a, SIDE)]
SLOT = {pair: k for k, pair in enumerate(PAIRS)}
FAR = [pair for pair in PAIRS if 2 in pair]
NEAR = [pair for pair in PAIRS if 2 not in pair]


def adam_update(grad, weight, moment, second):
    new_moment = 0.9 * moment + 0.1 * grad
    new_second = 0.999 * second + 0.001 * grad * grad
    corr_one = 1.0 - 0.9**10.0
    corr_two = 1.0 - 0.999**10.0
    update = new_moment / corr_one / (jnp.sqrt(new_second / corr_two) + 1e-08)
    return (weight - 0.001 * update, new_moment, new_second)


def dot_nt(left, right):
    return lax.dot_general(
        left, right, (((1,), (1,)), ((), ())), preferred_element_type=jnp.float32
    )


def pair_coefs(ab, aa, bb):
    return 1.0 - ab / (2.0 * (aa + eps_adasum)), 1.0 - ab / (2.0 * (bb + eps_adasum))


def tree_weights(g):
    w0, w2 = pair_coefs(g(0, 2), g(0, 0), g(2, 2))
    w1, w3 = pair_coefs(g(1, 3), g(1, 1), g(3, 3))
    aa = w0 * w0 * g(0, 0) + 2.0 * w0 * w2 * g(0, 2) + w2 * w2 * g(2, 2)
    bb = w1 * w1 * g(1, 1) + 2.0 * w1 * w3 * g(1, 3) + w3 * w3 * g(3, 3)
    ab = w0 * (w1 * g(0, 1) + w3 * g(0, 3)) + w2 * (w1 * g(1, 2) + w3 * g(2, 3))
    u, v = pair_coefs(ab, aa, bb)
    return [u * w0, v * w1, u * w2, v * w3]


def gelu_parts(v):
    root = 0.7978845608028654
    square = v * v
    t = jnp.tanh(root * (v + 0.044715 * (square * v)))
    cdf = 0.5 * (1.0 + t)
    slope = cdf + v * (0.5 * (1.0 - t * t)) * (root * (1.0 + 0.134145 * square))
    return v * cdf, slope


def gelu_only(v):
    root = 0.7978845608028654
    return v * (0.5 * (1.0 + jnp.tanh(root * (v + 0.044715 * (v * v * v)))))


def columns_of(row):
    return jnp.broadcast_to(row, (LANES, LANES)).T


def encode(v):
    most = jnp.maximum(jnp.max(jnp.abs(v), axis=0, keepdims=True), 1e-30)
    codes = jnp.round(v * (32767.0 / most)).astype(jnp.int32).astype(jnp.int16)
    return codes, most * (1.0 / 32767.0)


def gram_sums(refs, rows, pairs):
    width = refs[0].shape[2]
    used = sorted({k for pair in pairs for k in pair})

    def step(i, sums):
        sums = list(sums)
        at = pl.ds(pl.multiple_of(i * 8, 8), 8)
        for ref in refs:
            for c in range(width // LANES):
                cols = slice(c * LANES, (c + 1) * LANES)
                v = {k: ref[k, at, cols] for k in used}
                for p, (a, b) in enumerate(pairs):
                    sums[p] = sums[p] + v[a] * v[b]
        return tuple(sums)

    zero = jnp.zeros((8, LANES), jnp.float32)
    return lax.fori_loop(0, rows // 8, step, (zero,) * len(pairs))


def kernel(
    assigned,
    gate,
    tokens,
    cotangent,
    win_hbm,
    wout_hbm,
    combined,
    seg_in,
    seg_out,
    tok,
    ups,
    win,
    wout,
    w1t,
    g_in,
    g_out,
    ht,
    hgt,
    sent_t,
    sent_u,
    scaled,
    last,
    raw,
    place_own,
    places,
    eout,
    ret,
    acc,
    q_in,
    q_out,
    rq_in,
    rq_out,
    f_in,
    f_out,
    rf_in,
    rf_out,
    gz_out,
    gz_got,
    gy_out,
    gy_got,
    w_sem,
    loc_sem,
    d_send,
    d_recv,
    rz_send,
    rz_recv,
    rfar_send,
    rfar_recv,
    b_send,
    b_recv,
    zf_send,
    zf_recv,
    far_send,
    far_recv,
    e_send,
    e_recv,
    gz_send,
    gz_recv,
    yo_send,
    yo_recv,
    yi_send,
    yi_recv,
    gy_send,
    gy_recv,
):
    f32 = jnp.float32
    bf16 = jnp.bfloat16
    dp = lax.axis_index("dp")
    me = lax.axis_index("expert")
    z, y = lax.div(dp, SIDE), lax.rem(dp, SIDE)
    x, core = lax.div(me, 2), lax.rem(me, 2)
    cap = ret.shape[1]
    chunk = 2 * cap
    part = w1t.shape[0]
    toks, width = tokens.shape
    lane_blocks = width // LANES
    panel = width // PANELS
    own_rows = pl.ds(pl.multiple_of(me * cap, cap), cap)

    def at_zy(i, j):
        return lax.rem(z + i, SIDE) * SIDE + lax.rem(y + j, SIDE)

    def to(dp_index, expert_index):
        return {"device_id": (dp_index, expert_index), "device_id_type": MESH}

    load_win = pltpu.make_async_copy(win_hbm, win, w_sem.at[0])
    load_wout = pltpu.make_async_copy(wout_hbm, wout, w_sem.at[1])
    load_win.start()
    load_wout.start()

    barrier = pltpu.get_barrier_semaphore()
    for k in range(1, 8):
        pl.semaphore_signal(barrier, inc=1, **to(dp, lax.rem(me + k, 8)))
    for i in range(SIDE):
        for j in range(SIDE):
            if i or j:
                pl.semaphore_signal(barrier, inc=1, **to(at_zy(i, j), me))

    def raw_hop(what, way):
        src, dst, base = (
            (last, raw, 0),
            (scaled.at[PANELS - 1], raw, 3),
            (place_own, places, 0),
        )[what]
        return pltpu.make_async_remote_copy(
            src_ref=src,
            dst_ref=dst.at[base + (0 if way else 2)],
            send_sem=rz_send.at[way, what],
            recv_sem=rz_recv.at[way, what],
            **to(at_zy(3 if way else 1, 0), me),
        )

    last[...] = tokens[:, width - panel :]
    pl.semaphore_wait(barrier, 7 + SIDE * SIDE - 1)
    for way in range(2):
        raw_hop(0, way).start()

    named = assigned[...]
    hot = (lax.broadcasted_iota(jnp.int32, (16, toks), 0) == named).astype(f32)
    earlier = (
        lax.broadcasted_iota(jnp.int32, (toks, toks), 0)
        < lax.broadcasted_iota(jnp.int32, (toks, toks), 1)
    ).astype(f32)
    rank = jnp.dot(hot.astype(bf16), earlier.astype(bf16), preferred_element_type=f32)
    place = (named * cap).astype(f32) + jnp.sum(rank * hot, axis=0, keepdims=True)
    place_own[...] = jnp.broadcast_to(place, place_own.shape)
    for b in range(toks // LANES):
        at = slice(b * LANES, (b + 1) * LANES)
        column = columns_of(gate[:, at])
        for c in range(lane_blocks):
            cols = slice(c * LANES, (c + 1) * LANES)
            value = (column * cotangent[at, cols].astype(f32)).astype(bf16)
            start = c * LANES % panel
            scaled[c * LANES // panel, at, start : start + LANES] = value

    def chip_at(q):
        return lax.rem(x + (q ^ (q >> 1)), SIDE)

    def chip_rows(q):
        return pl.ds(pl.multiple_of(lax.rem(x + SIDE - (q ^ (q >> 1)), SIDE) * chunk, chunk), chunk)

    def table_of(q, places_row):
        base = (chip_at(q) * chunk).astype(f32)
        slots = lax.broadcasted_iota(jnp.int32, (chunk, toks), 0).astype(f32) + base
        return (slots == places_row).astype(f32).astype(bf16)

    def panels_of(p):
        return slice(p * panel, (p + 1) * panel)

    def joined(buf, slot, rows):
        return jnp.concatenate([buf[slot, p, rows, :] for p in range(PANELS)], axis=1)

    def place_rows(q):
        table = table_of(q, place)
        for p in range(PANELS):
            rows = jnp.dot(table, tokens[:, panels_of(p)], preferred_element_type=f32)
            sent_t[p, q] = rows.astype(bf16)
            rows = jnp.dot(table, scaled[p], preferred_element_type=f32)
            sent_u[p, q] = rows.astype(bf16)

    def dispatch(q, c):
        there = lax.rem(core + c, 2)
        return [
            pltpu.make_async_remote_copy(
                src_ref=src.at[:, q, pl.ds(pl.multiple_of(there * cap, cap), cap)],
                dst_ref=dst.at[0, :, own_rows],
                send_sem=d_send.at[h, 2 * q + c],
                recv_sem=d_recv.at[h, 2 * q + c],
                **to(dp, chip_at(q) * 2 + there),
            )
            for h, (src, dst) in enumerate(((sent_t, tok), (sent_u, ups)))
        ]

    def along_z(buf, slot, to_slot, rows, step, send, recv):
        return pltpu.make_async_remote_copy(
            src_ref=buf.at[slot, : PANELS - 1, rows],
            dst_ref=buf.at[to_slot, : PANELS - 1, rows],
            send_sem=send,
            recv_sem=recv,
            **to(at_zy(step, 0), me),
        )

    def first_hop(q, c):
        source = lax.rem(x + SIDE - (q ^ (q >> 1)), SIDE) * 2 + lax.rem(core + c, 2)
        rows = pl.ds(pl.multiple_of(source * cap, cap), cap)
        n = 2 * q + c
        copies = []
        for h, buf in enumerate((tok, ups)):
            copies.append(along_z(buf, 0, 3, rows, 1, zf_send.at[0, h, n], zf_recv.at[0, h, n]))
            copies.append(along_z(buf, 0, 1, rows, 3, zf_send.at[1, h, n], zf_recv.at[1, h, n]))
        return copies

    def second_hop(q):
        rows = chip_rows(q)
        return [
            along_z(tok, 3, 2, rows, 1, far_send.at[0, q], far_recv.at[0, q]),
            along_z(ups, 1, 2, rows, 3, far_send.at[1, q], far_recv.at[1, q]),
        ]

    def raw_far(what):
        buf, source, there = ((raw, 2, 1), (raw, 3, 4), (places, 2, 1))[what]
        return pltpu.make_async_remote_copy(
            src_ref=buf.at[source],
            dst_ref=buf.at[there],
            send_sem=rfar_send.at[what],
            recv_sem=rfar_recv.at[what],
            **to(at_zy(3 if what == 1 else 1, 0), me),
        )

    def raw_dispatch(slot, q, c):
        there = lax.rem(core + c, 2)
        return [
            pltpu.make_async_remote_copy(
                src_ref=src.at[slot - 1, q, pl.ds(pl.multiple_of(there * cap, cap), cap)],
                dst_ref=dst.at[slot, PANELS - 1, own_rows],
                send_sem=b_send.at[slot - 1, h, 2 * q + c],
                recv_sem=b_recv.at[slot - 1, h, 2 * q + c],
                **to(dp, chip_at(q) * 2 + there),
            )
            for h, (src, dst) in enumerate(((sent_t, tok), (sent_u, ups)))
        ]

    for what in (1, 2):
        for way in range(2):
            raw_hop(what, way).start()
    place_rows(0)
    half_rows = pl.ds(pl.multiple_of(core * cap, cap), cap)
    for p in range(PANELS):
        tok[0, p, own_rows, :] = sent_t[p, 0, half_rows, :]
        ups[0, p, own_rows, :] = sent_u[p, 0, half_rows, :]
    for copy in dispatch(0, 1) + first_hop(0, 0):
        copy.start()

    def place_step(q, carry):
        place_rows(q)
        for copy in dispatch(q, 0) + dispatch(q, 1):
            copy.start()
        return carry

    lax.fori_loop(1, SIDE, place_step, 0)
    for copy in dispatch(0, 1):
        copy.wait_recv()
    for copy in first_hop(0, 1):
        copy.start()

    load_win.wait()

    def turn(n, carry):
        at = pl.ds(pl.multiple_of(n * LANES, LANES), LANES)
        cols = pl.ds(pl.multiple_of(z * part + n * LANES, LANES), LANES)
        for c in range(lane_blocks):
            rows = slice(c * LANES, (c + 1) * LANES)
            w1t[at, rows] = win[rows, cols].astype(f32).T.astype(bf16)
        return carry

    lax.fori_loop(0, part // LANES, turn, 0)

    def clear(i, carry):
        at = pl.ds(pl.multiple_of(i * 16, 16), 16)
        for k in range(SIDE):
            g_in[k, at, :] = jnp.zeros((16, width), f32)
            g_out[k, at, :] = jnp.zeros((16, width), f32)
        return carry

    lax.fori_loop(0, part // 16, clear, 0)
    load_wout.wait()
    w2_rows = pl.ds(pl.multiple_of(z * part, part), part)

    def grads(slot, rows):
        t = joined(tok, slot, rows)
        u = joined(ups, slot, rows)
        act, slope = gelu_parts(dot_nt(w1t[...], t))
        ht[...] = act.astype(bf16)
        hgt[...] = (slope * dot_nt(wout[w2_rows, :], u)).astype(bf16)
        g_out[slot] = g_out[slot] + jnp.dot(ht[...], u, preferred_element_type=f32)
        g_in[slot] = g_in[slot] + jnp.dot(hgt[...], t, preferred_element_type=f32)

    tile = part

    def forward(rows):
        acc[rows, :] = jnp.zeros((chunk, width), f32)

        def step(n, carry):
            cols = pl.ds(pl.multiple_of(n * tile, tile), tile)
            pre = jnp.dot(joined(tok, 0, rows), win[:, cols], preferred_element_type=f32)
            hid = gelu_only(pre).astype(bf16)
            acc[rows, :] = acc[rows, :] + jnp.dot(hid, wout[cols, :], preferred_element_type=f32)
            return carry

        lax.fori_loop(0, win.shape[1] // tile, step, 0)
        eout[rows, :] = acc[rows, :].astype(bf16)

    def back(q, c):
        there = lax.rem(x + SIDE - (q ^ (q >> 1)), SIDE) * 2 + lax.rem(core + c, 2)
        return pltpu.make_async_remote_copy(
            src_ref=eout.at[pl.ds(pl.multiple_of(there * cap, cap), cap)],
            dst_ref=ret.at[me],
            send_sem=e_send.at[2 * q + c],
            recv_sem=e_recv.at[2 * q + c],
            **to(dp, there),
        )

    for what in range(3):
        for way in range(2):
            raw_hop(what, way).wait_recv()
    for what in range(3):
        raw_far(what).start()

    def own_step(q, carry):
        for c in range(2):
            for copy in dispatch(q, c):
                copy.wait_recv()
            for copy in first_hop(q, c):
                copy.start()
        grads(0, chip_rows(q - 1))

        @pl.when(q < SIDE - 1)
        def _():
            forward(chip_rows(q - 1))

        return carry

    lax.fori_loop(1, SIDE, own_step, 0)

    def place_raw(slot, q):
        table = table_of(q, places[slot - 1, 0:1, :])
        for sent, base in ((sent_t, 0), (sent_u, 3)):
            rows = jnp.dot(table, raw[base + slot - 1], preferred_element_type=f32)
            sent[slot - 1, q] = rows.astype(bf16)

    for slot in (1, 3, 2):
        if slot == 2:
            for what in range(3):
                raw_far(what).wait_recv()
        if slot == 1:
            for copy in dispatch(0, 1):
                copy.wait_send()
        place_raw(slot, 0)
        tok[slot, PANELS - 1, own_rows, :] = sent_t[slot - 1, 0, half_rows, :]
        ups[slot, PANELS - 1, own_rows, :] = sent_u[slot - 1, 0, half_rows, :]
        for copy in raw_dispatch(slot, 0, 1):
            copy.start()

        def raw_step(q, carry, slot=slot):
            if slot == 1:
                for copy in dispatch(q, 0) + dispatch(q, 1):
                    copy.wait_send()
            place_raw(slot, q)
            for copy in raw_dispatch(slot, q, 0) + raw_dispatch(slot, q, 1):
                copy.start()
            return carry

        lax.fori_loop(1, SIDE, raw_step, 0)

    grads(0, chip_rows(SIDE - 1))

    def raw_arrived(slot, q):
        @pl.when(q > 0)
        def _():
            for copy in raw_dispatch(slot, q, 0):
                copy.wait_recv()

        for copy in raw_dispatch(slot, q, 1):
            copy.wait_recv()

    for q in range(2):
        for c in range(2):
            if q or c:
                back(q, c).start()
    back_own = pltpu.make_async_copy(eout.at[own_rows], ret.at[me], loc_sem.at[0])
    back_own.start()

    def near_step(q, carry):
        for c in range(2):
            for copy in first_hop(q, c):
                copy.wait_recv()
        for copy in second_hop(q):
            copy.start()
        raw_arrived(1, q)
        raw_arrived(3, q)
        grads(1, chip_rows(q))
        grads(3, chip_rows(q))
        return carry

    lax.fori_loop(0, SIDE, near_step, 0)

    def z_sums(pairs):
        for pair, s in zip(pairs, gram_sums((g_in, g_out), part, pairs)):
            p = SLOT[pair]
            gz_out[p : p + 1, :] = jnp.sum(s, axis=0, keepdims=True)

    z_sums(NEAR)

    def far_step(q, carry):
        for copy in second_hop(q):
            copy.wait_recv()
        raw_arrived(2, q)
        grads(2, chip_rows(q))
        return carry

    lax.fori_loop(0, SIDE, far_step, 0)

    z_sums(FAR)
    sums_z = []
    for i in range(1, SIDE):
        copy = pltpu.make_async_remote_copy(
            src_ref=gz_out,
            dst_ref=gz_got.at[SIDE - i],
            send_sem=gz_send.at[SIDE - i],
            recv_sem=gz_recv.at[SIDE - i],
            **to(at_zy(i, 0), me),
        )
        copy.start()
        sums_z.append(copy)
    total = [gz_out[p : p + 1, :] for p in range(len(PAIRS))]
    for copy in sums_z:
        copy.wait_recv()
    for i in range(1, SIDE):
        for p, (a, b) in enumerate(PAIRS):
            q = SLOT[tuple(sorted(((a + i) % SIDE, (b + i) % SIDE)))]
            total[q] = total[q] + gz_got[i, p : p + 1, :]
    total = [jnp.sum(t, axis=1, keepdims=True) for t in total]
    w = tree_weights(lambda a, b: total[SLOT[(a, b)]])

    rows_out = seg_out.shape[0]
    rows_in = seg_in.shape[0]

    def send_out(j):
        k = (SIDE - j) % SIDE
        return [
            pltpu.make_async_remote_copy(
                src_ref=src.at[j],
                dst_ref=dst.at[k],
                send_sem=yo_send.at[h, k],
                recv_sem=yo_recv.at[h, k],
                **to(at_zy(0, j), me),
            )
            for h, (src, dst) in enumerate(((q_out, rq_out), (f_out, rf_out)))
        ]

    def send_in(i, j):
        n = i * SIDE + j
        k = (SIDE - j) % SIDE
        m = lax.rem(SIDE - i, SIDE) * SIDE + k
        return [
            pltpu.make_async_remote_copy(
                src_ref=src.at[n],
                dst_ref=dst.at[k, z],
                send_sem=yi_send.at[h, m],
                recv_sem=yi_recv.at[h, m],
                **to(at_zy(i, j), me),
            )
            for h, (src, dst) in enumerate(((q_in, rq_in), (f_in, rf_in)))
        ]

    for j in (1, 3, 2):
        rows = pl.ds(pl.multiple_of(lax.rem(y + j, SIDE) * rows_out, 8), rows_out)
        for c in range(lane_blocks):
            cols = slice(c * LANES, (c + 1) * LANES)
            v = w[0] * g_out[0, rows, cols] + w[1] * g_out[1, rows, cols]
            v = v + w[2] * g_out[2, rows, cols] + w[3] * g_out[3, rows, cols]
            q_out[j, :, cols], f_out[j, c : c + 1, :] = encode(v)
        for copy in send_out(j):
            copy.start()

    def mix_in(n, carry):
        cols = pl.ds(pl.multiple_of(n * LANES, LANES), LANES)
        for m in range(part // LANES):
            at = slice(m * LANES, (m + 1) * LANES)
            v = w[0] * g_in[0, at, cols] + w[1] * g_in[1, at, cols]
            v = v + w[2] * g_in[2, at, cols] + w[3] * g_in[3, at, cols]
            acc[cols, at] = v.T
        return carry

    lax.fori_loop(0, width // LANES, mix_in, 0)

    def block_rows(i, j):
        return pl.ds(pl.multiple_of(at_zy(i, j) * rows_in, 8), rows_in)

    for j in (1, 3, 2, 0):

        def code_in(i, carry, j=j):
            rows = block_rows(i, j)
            for c in range(lane_blocks):
                cols = slice(c * LANES, (c + 1) * LANES)
                codes, factor = encode(acc[rows, cols])
                q_in[i * SIDE + j, :, cols] = codes
                f_in[i * SIDE + j, c : c + 1, :] = factor
            for copy in send_in(i, j):
                copy.start()
            return carry

        lax.fori_loop(0 if j else 1, SIDE, code_in, 0)

    g_in[0, pl.ds(pl.multiple_of(z * rows_in, 8), rows_in), :] = acc[block_rows(0, 0), :]
    base = y * rows_out

    def mix_own(n, carry):
        rows = pl.ds(pl.multiple_of(base + n * 16, 16), 16)
        v = w[0] * g_out[0, rows, :] + w[1] * g_out[1, rows, :]
        v = v + w[2] * g_out[2, rows, :] + w[3] * g_out[3, rows, :]
        g_out[0, pl.ds(pl.multiple_of(n * 16, 16), 16), :] = v
        return carry

    lax.fori_loop(0, rows_out // 16, mix_own, 0)

    def late_step(q, carry):
        forward(chip_rows(q))
        for copy in (back(q, 0), back(q, 1)):
            copy.start()
        return carry

    lax.fori_loop(2, SIDE, late_step, 0)

    for k in (0, 3, 1, 2):
        j = (SIDE - k) % SIDE

        def decode_in(i, carry, j=j, k=k):
            for copy in send_in(i, j):
                copy.wait_recv()
            there = lax.rem(z + SIDE - i, SIDE)
            rows = pl.ds(pl.multiple_of(there * rows_in, 8), rows_in)
            for c in range(lane_blocks):
                cols = slice(c * LANES, (c + 1) * LANES)
                codes = rq_in[k, there, :, cols].astype(jnp.int32).astype(f32)
                g_in[k, rows, cols] = codes * rf_in[k, there, c : c + 1, :]
            return carry

        if k:
            for copy in send_out(j):
                copy.wait_recv()
            for c in range(lane_blocks):
                cols = slice(c * LANES, (c + 1) * LANES)
                codes = rq_out[k, :, cols].astype(jnp.int32).astype(f32)
                g_out[k, :rows_out, cols] = codes * rf_out[k, c : c + 1, :]
        lax.fori_loop(0 if k else 1, SIDE, decode_in, 0)

    for p, s in enumerate(gram_sums((g_in, g_out), rows_out, PAIRS)):
        gy_out[p : p + 1, :] = jnp.sum(s, axis=0, keepdims=True)
    sums_y = []
    for i in range(SIDE):
        for j in range(SIDE):
            if i or j:
                k = (SIDE - i) % SIDE * SIDE + (SIDE - j) % SIDE
                copy = pltpu.make_async_remote_copy(
                    src_ref=gy_out,
                    dst_ref=gy_got.at[k],
                    send_sem=gy_send.at[k],
                    recv_sem=gy_recv.at[k],
                    **to(at_zy(i, j), me),
                )
                copy.start()
                sums_y.append(copy)
    for q in range(SIDE):
        for c in range(2):
            if q or c:
                back(q, c).wait_recv()
    back_own.wait()
    for what in range(3):
        raw_far(what).wait_send()
    for b in range(toks // LANES):
        at = slice(b * LANES, (b + 1) * LANES)
        code = columns_of(place_own[0:1, at])
        for n in range(2 * SIDE):
            slots = lax.broadcasted_iota(jnp.int32, (LANES, cap), 1).astype(f32) + float(n * cap)
            hit = (slots == code).astype(f32).astype(bf16)
            raw[n // 2, at, n % 2 * cap : (n % 2 + 1) * cap] = hit
    picked = jnp.zeros((toks, width), f32)
    for p in range(SIDE):
        rows = ret[2 * p : 2 * p + 2].reshape(chunk, width)
        picked = picked + jnp.dot(raw[p], rows, preferred_element_type=f32)
    for b in range(toks // LANES):
        at = slice(b * LANES, (b + 1) * LANES)
        column = columns_of(gate[:, at])
        for c in range(lane_blocks):
            cols = slice(c * LANES, (c + 1) * LANES)
            combined[at, cols] = (column * picked[at, cols]).astype(bf16)
    total = [gy_out[p : p + 1, :] for p in range(len(PAIRS))]
    for copy in sums_y:
        copy.wait_recv()
    for j in range(SIDE):
        for i in range(SIDE):
            if i or j:
                for p, (a, b) in enumerate(PAIRS):
                    q = SLOT[tuple(sorted(((a + j) % SIDE, (b + j) % SIDE)))]
                    total[q] = total[q] + gy_got[i * SIDE + j, p : p + 1, :]
    total = [jnp.sum(t, axis=1, keepdims=True) for t in total]
    v = tree_weights(lambda a, b: total[SLOT[(a, b)]])
    for i in range(SIDE):
        at = slice(i * rows_in, (i + 1) * rows_in)
        seg_in[:, i * part : (i + 1) * part] = (v[0] * g_in[0, at, :] + v[1] * g_in[1, at, :]) + (
            v[2] * g_in[2, at, :] + v[3] * g_in[3, at, :]
        )
        seg_out[at, :] = (v[0] * g_out[0, at, :] + v[1] * g_out[1, at, :]) + (
            v[2] * g_out[2, at, :] + v[3] * g_out[3, at, :]
        )

    def drain(q, carry):
        for copy in first_hop(q, 0) + first_hop(q, 1) + second_hop(q):
            copy.wait_send()
        return carry

    lax.fori_loop(0, SIDE, drain, 0)

    for slot in range(1, SIDE):
        for copy in raw_dispatch(slot, 0, 1):
            copy.wait_send()

        def drain_raw(q, carry, slot=slot):
            for copy in raw_dispatch(slot, q, 0) + raw_dispatch(slot, q, 1):
                copy.wait_send()
            return carry

        lax.fori_loop(1, SIDE, drain_raw, 0)
    for what in range(3):
        for way in range(2):
            raw_hop(what, way).wait_send()
    for q in range(SIDE):
        for c in range(2):
            if q or c:
                back(q, c).wait_send()
    for j in range(SIDE):

        def drain_in(i, carry, j=j):
            for copy in send_in(i, j):
                copy.wait_send()
            return carry

        lax.fori_loop(0 if j else 1, SIDE, drain_in, 0)
        if j:
            for copy in send_out(j):
                copy.wait_send()
    for copy in sums_z + sums_y:
        copy.wait_send()


def expert_step(assigned, gate, tokens, cotangent, w_in, w_out):
    f32 = jnp.float32
    bf16 = jnp.bfloat16
    i16 = jnp.int16
    experts = 8
    toks, width = tokens.shape
    cap = 2 * toks // experts
    rows = experts * cap
    side = SIDE
    part = w_in.shape[1] // side
    any_space = pl.BlockSpec(memory_space=pl.ANY)
    vmem = pl.BlockSpec(memory_space=pltpu.VMEM)
    rows_in = width // (side * side)
    rows_out = part // side
    dma = pltpu.SemaphoreType.DMA
    return pl.pallas_call(
        kernel,
        out_shape=(
            jax.ShapeDtypeStruct((toks, width), bf16),
            jax.ShapeDtypeStruct((rows_in, side * part), f32),
            jax.ShapeDtypeStruct((rows_out, width), f32),
        ),
        in_specs=[vmem, vmem, vmem, vmem, any_space, any_space],
        out_specs=(vmem, vmem, vmem),
        scratch_shapes=[
            pltpu.VMEM((side, PANELS, rows, width // PANELS), bf16),
            pltpu.VMEM((side, PANELS, rows, width // PANELS), bf16),
            pltpu.VMEM(w_in.shape, bf16),
            pltpu.VMEM(w_out.shape, bf16),
            pltpu.VMEM((part, width), bf16),
            pltpu.VMEM((side, part, width), f32),
            pltpu.VMEM((side, part, width), f32),
            pltpu.VMEM((part, 2 * cap), bf16),
            pltpu.VMEM((part, 2 * cap), bf16),
            pltpu.VMEM((PANELS, side, 2 * cap, width // PANELS), bf16),
            pltpu.VMEM((PANELS, side, 2 * cap, width // PANELS), bf16),
            pltpu.VMEM((PANELS, toks, width // PANELS), bf16),
            pltpu.VMEM((toks, width // PANELS), bf16),
            pltpu.VMEM((2 * (side - 1), toks, width // PANELS), bf16),
            pltpu.VMEM((8, toks), f32),
            pltpu.VMEM((side - 1, 8, toks), f32),
            pltpu.VMEM((rows, width), bf16),
            pltpu.VMEM((experts, cap, width), bf16),
            pltpu.VMEM((rows, width), f32),
            pltpu.VMEM((side * side, rows_in, part), i16),
            pltpu.VMEM((side, rows_out, width), i16),
            pltpu.VMEM((side, side, rows_in, part), i16),
            pltpu.VMEM((side, rows_out, width), i16),
            pltpu.VMEM((side * side, 8, LANES), f32),
            pltpu.VMEM((side, 8, LANES), f32),
            pltpu.VMEM((side, side, 8, LANES), f32),
            pltpu.VMEM((side, 8, LANES), f32),
            pltpu.VMEM((16, LANES), f32),
            pltpu.VMEM((side, 16, LANES), f32),
            pltpu.VMEM((16, LANES), f32),
            pltpu.VMEM((side * side, 16, LANES), f32),
            dma((2,)),
            dma((1,)),
            dma((2, 8)),
            dma((2, 8)),
            dma((2, 3)),
            dma((2, 3)),
            dma((3,)),
            dma((3,)),
            dma((side - 1, 2, 8)),
            dma((side - 1, 2, 8)),
            dma((2, 2, 8)),
            dma((2, 2, 8)),
            dma((2, side)),
            dma((2, side)),
            dma((8,)),
            dma((8,)),
            dma((side,)),
            dma((side,)),
            dma((2, side)),
            dma((2, side)),
            dma((2, side * side)),
            dma((2, side * side)),
            dma((side * side,)),
            dma((side * side,)),
        ],
        compiler_params=pltpu.CompilerParams(
            collective_id=0, has_side_effects=True, vmem_limit_bytes=67_000_000
        ),
        name="expert_step",
    )(assigned, gate, tokens, cotangent, w_in, w_out)


def adam_kernel(index, *refs):
    for grad, weight, moment, second, new_weight, new_moment, new_second in (
        refs[0:4] + refs[8:11],
        refs[4:8] + refs[11:14],
    ):
        out = adam_update(grad[...], weight[0].astype(jnp.float32), moment[0], second[0])
        new_weight[0], new_moment[0], new_second[0] = out


def adam_step(index, first, second):
    steps = 3
    in_specs, out_specs, out_shape = [], [], []
    for grad, weight, moment, _ in (first, second):
        rows, cols = grad.shape
        own = (1, rows // steps, cols)
        state = pl.BlockSpec(own, lambda i, index: (0, i, 0))
        in_specs.append(pl.BlockSpec(own[1:], lambda i, index: (i, 0)))
        in_specs.append(pl.BlockSpec(own, lambda i, index: (0, index[0] * steps + i, 0)))
        in_specs += [state, state]
        out_specs += [state] * 3
        out_shape += [jax.ShapeDtypeStruct(moment.shape, jnp.float32)] * 3
    return pl.pallas_call(
        adam_kernel,
        out_shape=out_shape,
        grid_spec=pltpu.PrefetchScalarGridSpec(
            num_scalar_prefetch=1, grid=(steps,), in_specs=in_specs, out_specs=out_specs
        ),
        name="adam_step",
    )(index, *first, *second)


def body(
    tokens,
    assigned,
    gate_prob,
    cotangent,
    weight_in,
    weight_out,
    moment_in,
    moment_out,
    second_in,
    second_out,
):
    self_index = lax.axis_index("dp")
    toks = tokens.shape[0]
    w_first = weight_in[0]
    w_second = weight_out[0]
    combined, seg_first, seg_second = expert_step(
        assigned.reshape(1, toks), gate_prob.reshape(1, toks), tokens, cotangent, w_first, w_second
    )
    new_w_first, new_m_first, new_v_first, new_w_second, new_m_second, new_v_second = adam_step(
        self_index.reshape(1),
        (seg_first, weight_in, moment_in, second_in),
        (seg_second, weight_out, moment_out, second_out),
    )
    return (
        combined,
        new_w_first,
        new_w_second,
        new_m_first,
        new_m_second,
        new_v_first,
        new_v_second,
    )


def solution(mesh):
    return jax.shard_map(
        body,
        mesh=mesh,
        in_specs=(
            P(("dp", "expert"), None),
            P(("dp", "expert"), None),
            P(("dp", "expert"), None),
            P(("dp", "expert"), None),
            P("expert", None, None),
            P("expert", None, None),
            P("expert", "dp", None),
            P("expert", "dp", None),
            P("expert", "dp", None),
            P("expert", "dp", None),
        ),
        out_specs=(
            P(("dp", "expert"), None),
            P("expert", "dp", None),
            P("expert", "dp", None),
            P("expert", "dp", None),
            P("expert", "dp", None),
            P("expert", "dp", None),
            P("expert", "dp", None),
        ),
        check_vma=False,
    )
```

```python
import jax
import jax.numpy as jnp
from jax import lax
from jax.experimental import pallas as pl
from jax.experimental.pallas import tpu as pltpu
from jax.sharding import PartitionSpec as P

eps_adasum = 1e-06
SIDE = 4
LANES = 128
PANELS = 3
MESH = pl.DeviceIdType.MESH
PAIRS = [(a, b) for a in range(SIDE) for b in range(a, SIDE)]
SLOT = {pair: k for k, pair in enumerate(PAIRS)}
FAR = [pair for pair in PAIRS if 2 in pair]
NEAR = [pair for pair in PAIRS if 2 not in pair]


def adam_update(grad, weight, moment, second):
    new_moment = 0.9 * moment + 0.1 * grad
    new_second = 0.999 * second + 0.001 * grad * grad
    corr_one = 1.0 - 0.9**10.0
    corr_two = 1.0 - 0.999**10.0
    update = new_moment / corr_one / (jnp.sqrt(new_second / corr_two) + 1e-08)
    return (weight - 0.001 * update, new_moment, new_second)


def dot_nt(left, right):
    return lax.dot_general(
        left, right, (((1,), (1,)), ((), ())), preferred_element_type=jnp.float32
    )


def pair_coefs(ab, aa, bb):
    return 1.0 - ab / (2.0 * (aa + eps_adasum)), 1.0 - ab / (2.0 * (bb + eps_adasum))


def tree_weights(g):
    w0, w2 = pair_coefs(g(0, 2), g(0, 0), g(2, 2))
    w1, w3 = pair_coefs(g(1, 3), g(1, 1), g(3, 3))
    aa = w0 * w0 * g(0, 0) + 2.0 * w0 * w2 * g(0, 2) + w2 * w2 * g(2, 2)
    bb = w1 * w1 * g(1, 1) + 2.0 * w1 * w3 * g(1, 3) + w3 * w3 * g(3, 3)
    ab = w0 * (w1 * g(0, 1) + w3 * g(0, 3)) + w2 * (w1 * g(1, 2) + w3 * g(2, 3))
    u, v = pair_coefs(ab, aa, bb)
    return [u * w0, v * w1, u * w2, v * w3]


def gelu_parts(v):
    root = 0.7978845608028654
    square = v * v
    t = jnp.tanh(root * (v + 0.044715 * (square * v)))
    cdf = 0.5 * (1.0 + t)
    slope = cdf + v * (0.5 * (1.0 - t * t)) * (root * (1.0 + 0.134145 * square))
    return v * cdf, slope


def gelu_only(v):
    root = 0.7978845608028654
    return v * (0.5 * (1.0 + jnp.tanh(root * (v + 0.044715 * (v * v * v)))))


def columns_of(row):
    return jnp.broadcast_to(row, (LANES, LANES)).T


def encode(v):
    most = jnp.maximum(jnp.max(jnp.abs(v), axis=0, keepdims=True), 1e-30)
    codes = jnp.round(v * (32767.0 / most)).astype(jnp.int32).astype(jnp.int16)
    return codes, most * (1.0 / 32767.0)


def gram_sums(refs, rows, pairs):
    width = refs[0].shape[2]
    used = sorted({k for pair in pairs for k in pair})

    def step(i, sums):
        sums = list(sums)
        at = pl.ds(pl.multiple_of(i * 8, 8), 8)
        for ref in refs:
            for c in range(width // LANES):
                cols = slice(c * LANES, (c + 1) * LANES)
                v = {k: ref[k, at, cols] for k in used}
                for p, (a, b) in enumerate(pairs):
                    sums[p] = sums[p] + v[a] * v[b]
        return tuple(sums)

    zero = jnp.zeros((8, LANES), jnp.float32)
    return lax.fori_loop(0, rows // 8, step, (zero,) * len(pairs))


def kernel(
    assigned,
    gate,
    tokens,
    cotangent,
    win_hbm,
    wout_hbm,
    combined,
    seg_in,
    seg_out,
    tok,
    ups,
    win,
    wout,
    w1t,
    g_in,
    g_out,
    ht,
    hgt,
    sent_t,
    sent_u,
    scaled,
    last,
    raw,
    place_own,
    places,
    eout,
    ret,
    acc,
    q_in,
    q_out,
    rq_in,
    rq_out,
    f_in,
    f_out,
    rf_in,
    rf_out,
    gz_out,
    gz_got,
    gy_out,
    gy_got,
    w_sem,
    loc_sem,
    d_send,
    d_recv,
    rz_send,
    rz_recv,
    rfar_send,
    rfar_recv,
    b_send,
    b_recv,
    zf_send,
    zf_recv,
    far_send,
    far_recv,
    e_send,
    e_recv,
    gz_send,
    gz_recv,
    yo_send,
    yo_recv,
    yi_send,
    yi_recv,
    gy_send,
    gy_recv,
):
    f32 = jnp.float32
    bf16 = jnp.bfloat16
    dp = lax.axis_index("dp")
    me = lax.axis_index("expert")
    z, y = lax.div(dp, SIDE), lax.rem(dp, SIDE)
    x, core = lax.div(me, 2), lax.rem(me, 2)
    cap = ret.shape[1]
    chunk = 2 * cap
    part = w1t.shape[0]
    toks, width = tokens.shape
    lane_blocks = width // LANES
    panel = width // PANELS
    own_rows = pl.ds(pl.multiple_of(me * cap, cap), cap)

    def at_zy(i, j):
        return lax.rem(z + i, SIDE) * SIDE + lax.rem(y + j, SIDE)

    def to(dp_index, expert_index):
        return {"device_id": (dp_index, expert_index), "device_id_type": MESH}

    load_win = pltpu.make_async_copy(win_hbm, win, w_sem.at[0])
    load_wout = pltpu.make_async_copy(wout_hbm, wout, w_sem.at[1])
    load_win.start()
    load_wout.start()

    barrier = pltpu.get_barrier_semaphore()
    for k in range(1, 8):
        pl.semaphore_signal(barrier, inc=1, **to(dp, lax.rem(me + k, 8)))
    for i in range(SIDE):
        for j in range(SIDE):
            if i or j:
                pl.semaphore_signal(barrier, inc=1, **to(at_zy(i, j), me))

    def raw_hop(what, way):
        src, dst, base = (
            (last, raw, 0),
            (scaled.at[PANELS - 1], raw, 3),
            (place_own, places, 0),
        )[what]
        return pltpu.make_async_remote_copy(
            src_ref=src,
            dst_ref=dst.at[base + (0 if way else 2)],
            send_sem=rz_send.at[way, what],
            recv_sem=rz_recv.at[way, what],
            **to(at_zy(3 if way else 1, 0), me),
        )

    last[...] = tokens[:, width - panel :]
    pl.semaphore_wait(barrier, 7 + SIDE * SIDE - 1)
    for way in range(2):
        raw_hop(0, way).start()

    named = assigned[...]
    hot = (lax.broadcasted_iota(jnp.int32, (16, toks), 0) == named).astype(f32)
    earlier = (
        lax.broadcasted_iota(jnp.int32, (toks, toks), 0)
        < lax.broadcasted_iota(jnp.int32, (toks, toks), 1)
    ).astype(f32)
    rank = jnp.dot(hot.astype(bf16), earlier.astype(bf16), preferred_element_type=f32)
    place = (named * cap).astype(f32) + jnp.sum(rank * hot, axis=0, keepdims=True)
    place_own[...] = jnp.broadcast_to(place, place_own.shape)
    for b in range(toks // LANES):
        at = slice(b * LANES, (b + 1) * LANES)
        column = columns_of(gate[:, at])
        for c in range(lane_blocks):
            cols = slice(c * LANES, (c + 1) * LANES)
            value = (column * cotangent[at, cols].astype(f32)).astype(bf16)
            start = c * LANES % panel
            scaled[c * LANES // panel, at, start : start + LANES] = value

    def chip_at(q):
        return lax.rem(x + (q ^ (q >> 1)), SIDE)

    def chip_rows(q):
        return pl.ds(pl.multiple_of(lax.rem(x + SIDE - (q ^ (q >> 1)), SIDE) * chunk, chunk), chunk)

    def table_of(q, places_row):
        base = (chip_at(q) * chunk).astype(f32)
        slots = lax.broadcasted_iota(jnp.int32, (chunk, toks), 0).astype(f32) + base
        return (slots == places_row).astype(f32).astype(bf16)

    def panels_of(p):
        return slice(p * panel, (p + 1) * panel)

    def joined(buf, slot, rows):
        return jnp.concatenate([buf[slot, p, rows, :] for p in range(PANELS)], axis=1)

    def place_rows(q):
        table = table_of(q, place)
        for p in range(PANELS):
            rows = jnp.dot(table, tokens[:, panels_of(p)], preferred_element_type=f32)
            sent_t[p, q] = rows.astype(bf16)
            rows = jnp.dot(table, scaled[p], preferred_element_type=f32)
            sent_u[p, q] = rows.astype(bf16)

    def dispatch(q, c):
        there = lax.rem(core + c, 2)
        return [
            pltpu.make_async_remote_copy(
                src_ref=src.at[:, q, pl.ds(pl.multiple_of(there * cap, cap), cap)],
                dst_ref=dst.at[0, :, own_rows],
                send_sem=d_send.at[h, 2 * q + c],
                recv_sem=d_recv.at[h, 2 * q + c],
                **to(dp, chip_at(q) * 2 + there),
            )
            for h, (src, dst) in enumerate(((sent_t, tok), (sent_u, ups)))
        ]

    def along_z(buf, slot, to_slot, rows, step, send, recv):
        return pltpu.make_async_remote_copy(
            src_ref=buf.at[slot, : PANELS - 1, rows],
            dst_ref=buf.at[to_slot, : PANELS - 1, rows],
            send_sem=send,
            recv_sem=recv,
            **to(at_zy(step, 0), me),
        )

    def first_hop(q, c):
        source = lax.rem(x + SIDE - (q ^ (q >> 1)), SIDE) * 2 + lax.rem(core + c, 2)
        rows = pl.ds(pl.multiple_of(source * cap, cap), cap)
        n = 2 * q + c
        copies = []
        for h, buf in enumerate((tok, ups)):
            copies.append(along_z(buf, 0, 3, rows, 1, zf_send.at[0, h, n], zf_recv.at[0, h, n]))
            copies.append(along_z(buf, 0, 1, rows, 3, zf_send.at[1, h, n], zf_recv.at[1, h, n]))
        return copies

    def second_hop(q):
        rows = chip_rows(q)
        return [
            along_z(tok, 3, 2, rows, 1, far_send.at[0, q], far_recv.at[0, q]),
            along_z(ups, 1, 2, rows, 3, far_send.at[1, q], far_recv.at[1, q]),
        ]

    def raw_far(what):
        buf, source, there = ((raw, 2, 1), (raw, 3, 4), (places, 2, 1))[what]
        return pltpu.make_async_remote_copy(
            src_ref=buf.at[source],
            dst_ref=buf.at[there],
            send_sem=rfar_send.at[what],
            recv_sem=rfar_recv.at[what],
            **to(at_zy(3 if what == 1 else 1, 0), me),
        )

    def raw_dispatch(slot, q, c):
        there = lax.rem(core + c, 2)
        return [
            pltpu.make_async_remote_copy(
                src_ref=src.at[slot - 1, q, pl.ds(pl.multiple_of(there * cap, cap), cap)],
                dst_ref=dst.at[slot, PANELS - 1, own_rows],
                send_sem=b_send.at[slot - 1, h, 2 * q + c],
                recv_sem=b_recv.at[slot - 1, h, 2 * q + c],
                **to(dp, chip_at(q) * 2 + there),
            )
            for h, (src, dst) in enumerate(((sent_t, tok), (sent_u, ups)))
        ]

    for what in (1, 2):
        for way in range(2):
            raw_hop(what, way).start()
    place_rows(0)
    half_rows = pl.ds(pl.multiple_of(core * cap, cap), cap)
    for p in range(PANELS):
        tok[0, p, own_rows, :] = sent_t[p, 0, half_rows, :]
        ups[0, p, own_rows, :] = sent_u[p, 0, half_rows, :]
    for copy in dispatch(0, 1) + first_hop(0, 0):
        copy.start()

    def place_step(q, carry):
        place_rows(q)
        for copy in dispatch(q, 0) + dispatch(q, 1):
            copy.start()
        return carry

    lax.fori_loop(1, SIDE, place_step, 0)
    for copy in dispatch(0, 1):
        copy.wait_recv()
    for copy in first_hop(0, 1):
        copy.start()

    load_win.wait()

    def turn(n, carry):
        at = pl.ds(pl.multiple_of(n * LANES, LANES), LANES)
        cols = pl.ds(pl.multiple_of(z * part + n * LANES, LANES), LANES)
        for c in range(lane_blocks):
            rows = slice(c * LANES, (c + 1) * LANES)
            w1t[at, rows] = win[rows, cols].astype(f32).T.astype(bf16)
        return carry

    lax.fori_loop(0, part // LANES, turn, 0)

    def clear(i, carry):
        at = pl.ds(pl.multiple_of(i * 16, 16), 16)
        for k in range(SIDE):
            g_in[k, at, :] = jnp.zeros((16, width), f32)
            g_out[k, at, :] = jnp.zeros((16, width), f32)
        return carry

    lax.fori_loop(0, part // 16, clear, 0)
    load_wout.wait()
    w2_rows = pl.ds(pl.multiple_of(z * part, part), part)

    def grads(slot, rows):
        t = joined(tok, slot, rows)
        u = joined(ups, slot, rows)
        act, slope = gelu_parts(dot_nt(w1t[...], t))
        ht[...] = act.astype(bf16)
        hgt[...] = (slope * dot_nt(wout[w2_rows, :], u)).astype(bf16)
        g_out[slot] = g_out[slot] + jnp.dot(ht[...], u, preferred_element_type=f32)
        g_in[slot] = g_in[slot] + jnp.dot(hgt[...], t, preferred_element_type=f32)

    tile = part

    def forward(rows):
        acc[rows, :] = jnp.zeros((chunk, width), f32)

        def step(n, carry):
            cols = pl.ds(pl.multiple_of(n * tile, tile), tile)
            pre = jnp.dot(joined(tok, 0, rows), win[:, cols], preferred_element_type=f32)
            hid = gelu_only(pre).astype(bf16)
            acc[rows, :] = acc[rows, :] + jnp.dot(hid, wout[cols, :], preferred_element_type=f32)
            return carry

        lax.fori_loop(0, win.shape[1] // tile, step, 0)
        eout[rows, :] = acc[rows, :].astype(bf16)

    def back(q, c):
        there = lax.rem(x + SIDE - (q ^ (q >> 1)), SIDE) * 2 + lax.rem(core + c, 2)
        return pltpu.make_async_remote_copy(
            src_ref=eout.at[pl.ds(pl.multiple_of(there * cap, cap), cap)],
            dst_ref=ret.at[me],
            send_sem=e_send.at[2 * q + c],
            recv_sem=e_recv.at[2 * q + c],
            **to(dp, there),
        )

    for what in range(3):
        for way in range(2):
            raw_hop(what, way).wait_recv()
    for what in range(3):
        raw_far(what).start()

    def own_step(q, carry):
        for c in range(2):
            for copy in dispatch(q, c):
                copy.wait_recv()
            for copy in first_hop(q, c):
                copy.start()
        grads(0, chip_rows(q - 1))

        @pl.when(q < SIDE - 1)
        def _():
            forward(chip_rows(q - 1))

        return carry

    lax.fori_loop(1, SIDE, own_step, 0)

    def place_raw(slot, q):
        table = table_of(q, places[slot - 1, 0:1, :])
        for sent, base in ((sent_t, 0), (sent_u, 3)):
            rows = jnp.dot(table, raw[base + slot - 1], preferred_element_type=f32)
            sent[slot - 1, q] = rows.astype(bf16)

    for slot in (1, 3, 2):
        if slot == 2:
            for what in range(3):
                raw_far(what).wait_recv()
        if slot == 1:
            for copy in dispatch(0, 1):
                copy.wait_send()
        place_raw(slot, 0)
        tok[slot, PANELS - 1, own_rows, :] = sent_t[slot - 1, 0, half_rows, :]
        ups[slot, PANELS - 1, own_rows, :] = sent_u[slot - 1, 0, half_rows, :]
        for copy in raw_dispatch(slot, 0, 1):
            copy.start()

        def raw_step(q, carry, slot=slot):
            if slot == 1:
                for copy in dispatch(q, 0) + dispatch(q, 1):
                    copy.wait_send()
            place_raw(slot, q)
            for copy in raw_dispatch(slot, q, 0) + raw_dispatch(slot, q, 1):
                copy.start()
            return carry

        lax.fori_loop(1, SIDE, raw_step, 0)

    grads(0, chip_rows(SIDE - 1))

    def raw_arrived(slot, q):
        @pl.when(q > 0)
        def _():
            for copy in raw_dispatch(slot, q, 0):
                copy.wait_recv()

        for copy in raw_dispatch(slot, q, 1):
            copy.wait_recv()

    for q in range(2):
        for c in range(2):
            if q or c:
                back(q, c).start()
    back_own = pltpu.make_async_copy(eout.at[own_rows], ret.at[me], loc_sem.at[0])
    back_own.start()

    def near_step(q, carry):
        for c in range(2):
            for copy in first_hop(q, c):
                copy.wait_recv()
        for copy in second_hop(q):
            copy.start()
        raw_arrived(1, q)
        raw_arrived(3, q)
        grads(1, chip_rows(q))
        grads(3, chip_rows(q))
        return carry

    lax.fori_loop(0, SIDE, near_step, 0)

    def z_sums(pairs):
        for pair, s in zip(pairs, gram_sums((g_in, g_out), part, pairs)):
            p = SLOT[pair]
            gz_out[p : p + 1, :] = jnp.sum(s, axis=0, keepdims=True)

    z_sums(NEAR)

    def far_step(q, carry):
        for copy in second_hop(q):
            copy.wait_recv()
        raw_arrived(2, q)
        grads(2, chip_rows(q))
        return carry

    lax.fori_loop(0, SIDE, far_step, 0)

    z_sums(FAR)
    sums_z = []
    for i in range(1, SIDE):
        copy = pltpu.make_async_remote_copy(
            src_ref=gz_out,
            dst_ref=gz_got.at[SIDE - i],
            send_sem=gz_send.at[SIDE - i],
            recv_sem=gz_recv.at[SIDE - i],
            **to(at_zy(i, 0), me),
        )
        copy.start()
        sums_z.append(copy)
    total = [gz_out[p : p + 1, :] for p in range(len(PAIRS))]
    for copy in sums_z:
        copy.wait_recv()
    for i in range(1, SIDE):
        for p, (a, b) in enumerate(PAIRS):
            q = SLOT[tuple(sorted(((a + i) % SIDE, (b + i) % SIDE)))]
            total[q] = total[q] + gz_got[i, p : p + 1, :]
    total = [jnp.sum(t, axis=1, keepdims=True) for t in total]
    w = tree_weights(lambda a, b: total[SLOT[(a, b)]])

    rows_out = seg_out.shape[0]
    rows_in = seg_in.shape[0]

    def send_out(j):
        k = (SIDE - j) % SIDE
        return [
            pltpu.make_async_remote_copy(
                src_ref=src.at[j],
                dst_ref=dst.at[k],
                send_sem=yo_send.at[h, k],
                recv_sem=yo_recv.at[h, k],
                **to(at_zy(0, j), me),
            )
            for h, (src, dst) in enumerate(((q_out, rq_out), (f_out, rf_out)))
        ]

    def send_in(i, j):
        n = i * SIDE + j
        k = (SIDE - j) % SIDE
        m = lax.rem(SIDE - i, SIDE) * SIDE + k
        return [
            pltpu.make_async_remote_copy(
                src_ref=src.at[n],
                dst_ref=dst.at[k, z],
                send_sem=yi_send.at[h, m],
                recv_sem=yi_recv.at[h, m],
                **to(at_zy(i, j), me),
            )
            for h, (src, dst) in enumerate(((q_in, rq_in), (f_in, rf_in)))
        ]

    for j in (1, 3, 2):
        rows = pl.ds(pl.multiple_of(lax.rem(y + j, SIDE) * rows_out, 8), rows_out)
        for c in range(lane_blocks):
            cols = slice(c * LANES, (c + 1) * LANES)
            v = w[0] * g_out[0, rows, cols] + w[1] * g_out[1, rows, cols]
            v = v + w[2] * g_out[2, rows, cols] + w[3] * g_out[3, rows, cols]
            q_out[j, :, cols], f_out[j, c : c + 1, :] = encode(v)
        for copy in send_out(j):
            copy.start()

    def mix_in(n, carry):
        cols = pl.ds(pl.multiple_of(n * LANES, LANES), LANES)
        for m in range(part // LANES):
            at = slice(m * LANES, (m + 1) * LANES)
            v = w[0] * g_in[0, at, cols] + w[1] * g_in[1, at, cols]
            v = v + w[2] * g_in[2, at, cols] + w[3] * g_in[3, at, cols]
            acc[cols, at] = v.T
        return carry

    lax.fori_loop(0, width // LANES, mix_in, 0)

    def block_rows(i, j):
        return pl.ds(pl.multiple_of(at_zy(i, j) * rows_in, 8), rows_in)

    for j in (1, 3, 2, 0):

        def code_in(i, carry, j=j):
            rows = block_rows(i, j)
            for c in range(lane_blocks):
                cols = slice(c * LANES, (c + 1) * LANES)
                codes, factor = encode(acc[rows, cols])
                q_in[i * SIDE + j, :, cols] = codes
                f_in[i * SIDE + j, c : c + 1, :] = factor
            for copy in send_in(i, j):
                copy.start()
            return carry

        lax.fori_loop(0 if j else 1, SIDE, code_in, 0)

    g_in[0, pl.ds(pl.multiple_of(z * rows_in, 8), rows_in), :] = acc[block_rows(0, 0), :]
    base = y * rows_out

    def mix_own(n, carry):
        rows = pl.ds(pl.multiple_of(base + n * 16, 16), 16)
        v = w[0] * g_out[0, rows, :] + w[1] * g_out[1, rows, :]
        v = v + w[2] * g_out[2, rows, :] + w[3] * g_out[3, rows, :]
        g_out[0, pl.ds(pl.multiple_of(n * 16, 16), 16), :] = v
        return carry

    lax.fori_loop(0, rows_out // 16, mix_own, 0)

    def late_step(q, carry):
        forward(chip_rows(q))
        for copy in (back(q, 0), back(q, 1)):
            copy.start()
        return carry

    lax.fori_loop(2, SIDE, late_step, 0)

    def y_sums(pairs):
        for pair, s in zip(pairs, gram_sums((g_in, g_out), rows_out, pairs)):
            p = SLOT[pair]
            gy_out[p : p + 1, :] = jnp.sum(s, axis=0, keepdims=True)

    for k in (0, 3, 1, 2):
        j = (SIDE - k) % SIDE
        if k == 2:
            y_sums(NEAR)

        def decode_in(i, carry, j=j, k=k):
            for copy in send_in(i, j):
                copy.wait_recv()
            there = lax.rem(z + SIDE - i, SIDE)
            rows = pl.ds(pl.multiple_of(there * rows_in, 8), rows_in)
            for c in range(lane_blocks):
                cols = slice(c * LANES, (c + 1) * LANES)
                codes = rq_in[k, there, :, cols].astype(jnp.int32).astype(f32)
                g_in[k, rows, cols] = codes * rf_in[k, there, c : c + 1, :]
            return carry

        if k:
            for copy in send_out(j):
                copy.wait_recv()
            for c in range(lane_blocks):
                cols = slice(c * LANES, (c + 1) * LANES)
                codes = rq_out[k, :, cols].astype(jnp.int32).astype(f32)
                g_out[k, :rows_out, cols] = codes * rf_out[k, c : c + 1, :]
        lax.fori_loop(0 if k else 1, SIDE, decode_in, 0)

    y_sums(FAR)
    sums_y = []
    for i in range(SIDE):
        for j in range(SIDE):
            if i or j:
                k = (SIDE - i) % SIDE * SIDE + (SIDE - j) % SIDE
                copy = pltpu.make_async_remote_copy(
                    src_ref=gy_out,
                    dst_ref=gy_got.at[k],
                    send_sem=gy_send.at[k],
                    recv_sem=gy_recv.at[k],
                    **to(at_zy(i, j), me),
                )
                copy.start()
                sums_y.append(copy)
    for q in range(SIDE):
        for c in range(2):
            if q or c:
                back(q, c).wait_recv()
    back_own.wait()
    for what in range(3):
        raw_far(what).wait_send()
    for b in range(toks // LANES):
        at = slice(b * LANES, (b + 1) * LANES)
        code = columns_of(place_own[0:1, at])
        for n in range(2 * SIDE):
            slots = lax.broadcasted_iota(jnp.int32, (LANES, cap), 1).astype(f32) + float(n * cap)
            hit = (slots == code).astype(f32).astype(bf16)
            raw[n // 2, at, n % 2 * cap : (n % 2 + 1) * cap] = hit
    picked = jnp.zeros((toks, width), f32)
    for p in range(SIDE):
        rows = ret[2 * p : 2 * p + 2].reshape(chunk, width)
        picked = picked + jnp.dot(raw[p], rows, preferred_element_type=f32)
    for b in range(toks // LANES):
        at = slice(b * LANES, (b + 1) * LANES)
        column = columns_of(gate[:, at])
        for c in range(lane_blocks):
            cols = slice(c * LANES, (c + 1) * LANES)
            combined[at, cols] = (column * picked[at, cols]).astype(bf16)
    total = [gy_out[p : p + 1, :] for p in range(len(PAIRS))]
    for copy in sums_y:
        copy.wait_recv()
    for j in range(SIDE):
        for i in range(SIDE):
            if i or j:
                for p, (a, b) in enumerate(PAIRS):
                    q = SLOT[tuple(sorted(((a + j) % SIDE, (b + j) % SIDE)))]
                    total[q] = total[q] + gy_got[i * SIDE + j, p : p + 1, :]
    total = [jnp.sum(t, axis=1, keepdims=True) for t in total]
    v = tree_weights(lambda a, b: total[SLOT[(a, b)]])
    for i in range(SIDE):
        at = slice(i * rows_in, (i + 1) * rows_in)
        seg_in[:, i * part : (i + 1) * part] = (v[0] * g_in[0, at, :] + v[1] * g_in[1, at, :]) + (
            v[2] * g_in[2, at, :] + v[3] * g_in[3, at, :]
        )
        seg_out[at, :] = (v[0] * g_out[0, at, :] + v[1] * g_out[1, at, :]) + (
            v[2] * g_out[2, at, :] + v[3] * g_out[3, at, :]
        )

    def drain(q, carry):
        for copy in first_hop(q, 0) + first_hop(q, 1) + second_hop(q):
            copy.wait_send()
        return carry

    lax.fori_loop(0, SIDE, drain, 0)

    for slot in range(1, SIDE):
        for copy in raw_dispatch(slot, 0, 1):
            copy.wait_send()

        def drain_raw(q, carry, slot=slot):
            for copy in raw_dispatch(slot, q, 0) + raw_dispatch(slot, q, 1):
                copy.wait_send()
            return carry

        lax.fori_loop(1, SIDE, drain_raw, 0)
    for what in range(3):
        for way in range(2):
            raw_hop(what, way).wait_send()
    for q in range(SIDE):
        for c in range(2):
            if q or c:
                back(q, c).wait_send()
    for j in range(SIDE):

        def drain_in(i, carry, j=j):
            for copy in send_in(i, j):
                copy.wait_send()
            return carry

        lax.fori_loop(0 if j else 1, SIDE, drain_in, 0)
        if j:
            for copy in send_out(j):
                copy.wait_send()
    for copy in sums_z + sums_y:
        copy.wait_send()


def expert_step(assigned, gate, tokens, cotangent, w_in, w_out):
    f32 = jnp.float32
    bf16 = jnp.bfloat16
    i16 = jnp.int16
    experts = 8
    toks, width = tokens.shape
    cap = 2 * toks // experts
    rows = experts * cap
    side = SIDE
    part = w_in.shape[1] // side
    any_space = pl.BlockSpec(memory_space=pl.ANY)
    vmem = pl.BlockSpec(memory_space=pltpu.VMEM)
    rows_in = width // (side * side)
    rows_out = part // side
    dma = pltpu.SemaphoreType.DMA
    return pl.pallas_call(
        kernel,
        out_shape=(
            jax.ShapeDtypeStruct((toks, width), bf16),
            jax.ShapeDtypeStruct((rows_in, side * part), f32),
            jax.ShapeDtypeStruct((rows_out, width), f32),
        ),
        in_specs=[vmem, vmem, vmem, vmem, any_space, any_space],
        out_specs=(vmem, vmem, vmem),
        scratch_shapes=[
            pltpu.VMEM((side, PANELS, rows, width // PANELS), bf16),
            pltpu.VMEM((side, PANELS, rows, width // PANELS), bf16),
            pltpu.VMEM(w_in.shape, bf16),
            pltpu.VMEM(w_out.shape, bf16),
            pltpu.VMEM((part, width), bf16),
            pltpu.VMEM((side, part, width), f32),
            pltpu.VMEM((side, part, width), f32),
            pltpu.VMEM((part, 2 * cap), bf16),
            pltpu.VMEM((part, 2 * cap), bf16),
            pltpu.VMEM((PANELS, side, 2 * cap, width // PANELS), bf16),
            pltpu.VMEM((PANELS, side, 2 * cap, width // PANELS), bf16),
            pltpu.VMEM((PANELS, toks, width // PANELS), bf16),
            pltpu.VMEM((toks, width // PANELS), bf16),
            pltpu.VMEM((2 * (side - 1), toks, width // PANELS), bf16),
            pltpu.VMEM((8, toks), f32),
            pltpu.VMEM((side - 1, 8, toks), f32),
            pltpu.VMEM((rows, width), bf16),
            pltpu.VMEM((experts, cap, width), bf16),
            pltpu.VMEM((rows, width), f32),
            pltpu.VMEM((side * side, rows_in, part), i16),
            pltpu.VMEM((side, rows_out, width), i16),
            pltpu.VMEM((side, side, rows_in, part), i16),
            pltpu.VMEM((side, rows_out, width), i16),
            pltpu.VMEM((side * side, 8, LANES), f32),
            pltpu.VMEM((side, 8, LANES), f32),
            pltpu.VMEM((side, side, 8, LANES), f32),
            pltpu.VMEM((side, 8, LANES), f32),
            pltpu.VMEM((16, LANES), f32),
            pltpu.VMEM((side, 16, LANES), f32),
            pltpu.VMEM((16, LANES), f32),
            pltpu.VMEM((side * side, 16, LANES), f32),
            dma((2,)),
            dma((1,)),
            dma((2, 8)),
            dma((2, 8)),
            dma((2, 3)),
            dma((2, 3)),
            dma((3,)),
            dma((3,)),
            dma((side - 1, 2, 8)),
            dma((side - 1, 2, 8)),
            dma((2, 2, 8)),
            dma((2, 2, 8)),
            dma((2, side)),
            dma((2, side)),
            dma((8,)),
            dma((8,)),
            dma((side,)),
            dma((side,)),
            dma((2, side)),
            dma((2, side)),
            dma((2, side * side)),
            dma((2, side * side)),
            dma((side * side,)),
            dma((side * side,)),
        ],
        compiler_params=pltpu.CompilerParams(
            collective_id=0, has_side_effects=True, vmem_limit_bytes=67_000_000
        ),
        name="expert_step",
    )(assigned, gate, tokens, cotangent, w_in, w_out)


def adam_kernel(index, *refs):
    for grad, weight, moment, second, new_weight, new_moment, new_second in (
        refs[0:4] + refs[8:11],
        refs[4:8] + refs[11:14],
    ):
        out = adam_update(grad[...], weight[0].astype(jnp.float32), moment[0], second[0])
        new_weight[0], new_moment[0], new_second[0] = out


def adam_step(index, first, second):
    steps = 1
    in_specs, out_specs, out_shape = [], [], []
    for grad, weight, moment, _ in (first, second):
        rows, cols = grad.shape
        own = (1, rows // steps, cols)
        state = pl.BlockSpec(own, lambda i, index: (0, i, 0))
        in_specs.append(pl.BlockSpec(own[1:], lambda i, index: (i, 0)))
        in_specs.append(pl.BlockSpec(own, lambda i, index: (0, index[0] * steps + i, 0)))
        in_specs += [state, state]
        out_specs += [state] * 3
        out_shape += [jax.ShapeDtypeStruct(moment.shape, jnp.float32)] * 3
    return pl.pallas_call(
        adam_kernel,
        out_shape=out_shape,
        grid_spec=pltpu.PrefetchScalarGridSpec(
            num_scalar_prefetch=1, grid=(steps,), in_specs=in_specs, out_specs=out_specs
        ),
        name="adam_step",
    )(index, *first, *second)


def body(
    tokens,
    assigned,
    gate_prob,
    cotangent,
    weight_in,
    weight_out,
    moment_in,
    moment_out,
    second_in,
    second_out,
):
    self_index = lax.axis_index("dp")
    toks = tokens.shape[0]
    w_first = weight_in[0]
    w_second = weight_out[0]
    combined, seg_first, seg_second = expert_step(
        assigned.reshape(1, toks), gate_prob.reshape(1, toks), tokens, cotangent, w_first, w_second
    )
    new_w_first, new_m_first, new_v_first, new_w_second, new_m_second, new_v_second = adam_step(
        self_index.reshape(1),
        (seg_first, weight_in, moment_in, second_in),
        (seg_second, weight_out, moment_out, second_out),
    )
    return (
        combined,
        new_w_first,
        new_w_second,
        new_m_first,
        new_m_second,
        new_v_first,
        new_v_second,
    )


def solution(mesh):
    return jax.shard_map(
        body,
        mesh=mesh,
        in_specs=(
            P(("dp", "expert"), None),
            P(("dp", "expert"), None),
            P(("dp", "expert"), None),
            P(("dp", "expert"), None),
            P("expert", None, None),
            P("expert", None, None),
            P("expert", "dp", None),
            P("expert", "dp", None),
            P("expert", "dp", None),
            P("expert", "dp", None),
        ),
        out_specs=(
            P(("dp", "expert"), None),
            P("expert", "dp", None),
            P("expert", "dp", None),
            P("expert", "dp", None),
            P("expert", "dp", None),
            P("expert", "dp", None),
            P("expert", "dp", None),
        ),
        check_vma=False,
    )
```
